128 devices in a mesh: seq: 16 (over x, z), exp: 8 (over y, core).
Axes of the slice: x: 4, y: 4, z: 4, core: 2. Of those that a mesh axis runs over, the one named last changes fastest.
Arguments:
- ssd_input: bfloat16 [8192, 2, 4096], P('seq', None, 'exp'), may hold values from -6 to 6
- ssd_gate: bfloat16 [8192, 2, 4096], P('seq', None, 'exp'), may hold values from -6 to 6
- state_write: bfloat16 [8192, 2, 1024], P('seq', None, 'exp'), may hold values from -2 to 2
- state_read: bfloat16 [8192, 2, 1024], P('seq', None, 'exp'), may hold values from -2 to 2
- step_size: float32 [64, 2, 8192], P('exp', None, 'seq'), may hold values from 0.02 to 0.1
- decay_log: float32 [64, 2, 8192], P('exp', None, 'seq'), may hold values from -0.78 to 0
- skip_gain: float32 [64], P('exp'), may hold values from 0.5 to 2
- norm_gain: float32 [4096], P('exp'), may hold values from 0.5 to 1.5
- w_out: bfloat16 [4096, 2048], P('exp'), may hold values from -0.09375 to 0.09375
- resid: bfloat16 [8192, 2, 2048], P(('seq', 'exp')), may hold values from -6 to 6
- moe_gain: float32 [2048], replicated, may hold values from 0.5 to 1.5
- w_gate: bfloat16 [16, 2048, 7168], P('seq', None, 'exp'), may hold values from -0.125 to 0.125
- w_up: bfloat16 [16, 2048, 7168], P('seq', None, 'exp'), may hold values from -0.125 to 0.125
- w_down: bfloat16 [16, 7168, 2048], P('seq', 'exp'), may hold values from -0.0625 to 0.0625
- routes: int32 [8192, 2, 2], P(('seq', 'exp')), may hold values from 0 to 15, all different within a row; in each aligned block of 128 rows (0 to 127, 128 to 255, ..., all dimensions but the last counted through in order) at most 17 rows name the same one
- gates: float32 [8192, 2, 2], P(('seq', 'exp')), may hold values from 0.2 to 1
- directions: float32 [4, 2048], replicated, may hold values from -6 to 6
Outputs:
- steered: bfloat16 [8192, 2, 2048], P(('seq', 'exp'))
The draws below stay inside these ranges and needn't reach their ends.
Inputs may be any that keep to these rules, and one draw needn't show every extreme that they name: `routes`: in every aligned block of 128 rows, rows taken in the order position then sequence (the rows of one device), each expert is named by at most 17 picks, a bound that some block reaches; the two ids of a row differ.
All inputs are finite; a program needn't handle non-finite values.
Results may differ from the reference program's by a relative error of at most 0.023.
Values may be sent and summed in bfloat16 or wider, within the bound.
No kernel may reach another device: no remote copies, remote signals or barrier semaphores. Data moves between devices by JAX's collectives and lax.ppermute only.
A program may use at most 128 MiB of HBM per device.

```python
import math
import jax
import jax.numpy as jnp
import numpy as np
from jax import lax

D = 2048
FF = 7168
HEADS = 64
HEAD_DIM = 64
STATE = 128
GROUPS = 8
BLOCK = 256
SEQUENCE_COUNT = 2
NDIR = 4
SEQUENCE_LENGTH = 8192
EXPERTS = 16
TOK_DEV = 128
CAP = 17
N_EXP = 8


def draw_decay_log(key, part):
    random_keys = jax.random.split(jax.random.fold_in(key, 17), 6)
    share = 0.5
    slow = jax.random.uniform(random_keys[0], (HEADS,)) < share
    slow_rate = jnp.exp(jax.random.uniform(random_keys[1], (HEADS,), minval=math.log(0.1 / SEQUENCE_LENGTH), maxval=math.log(0.8 / SEQUENCE_LENGTH)))
    fast_rate = jnp.exp(jax.random.uniform(random_keys[2], (HEADS,), minval=math.log(1.0 / 60.0), maxval=math.log(1.0 / 25.0)))
    decay_rate = jnp.where(slow, slow_rate, fast_rate)
    noisy_input = jnp.exp(jax.random.uniform(random_keys[3], (HEADS, SEQUENCE_COUNT, SEQUENCE_LENGTH), minval=math.log(0.5), maxval=math.log(2.0)))
    spike_positions = jax.random.randint(random_keys[4], (SEQUENCE_COUNT, 2), 0, SEQUENCE_LENGTH)
    token_positions = jnp.arange(SEQUENCE_LENGTH, dtype=jnp.int32)
    spike_draw = jnp.any(token_positions[None, :, None] == spike_positions[:, None, :], axis=2)
    objective_loss = jax.random.uniform(random_keys[5], (HEADS, SEQUENCE_COUNT, SEQUENCE_LENGTH), minval=0.2, maxval=0.5)
    scalar_value = jnp.where(spike_draw[None], jnp.log(1.0 - objective_loss), 0.0) - decay_rate[:, None, None] * noisy_input
    return scalar_value.astype(jnp.float32)


def shard_levels(key, extent, cuts, smallest, largest):
    loudness = 1.0
    for position, parts in cuts:
        heights = jax.random.uniform(jax.random.fold_in(jax.random.fold_in(key, 6), position), (parts,), jnp.float32, smallest / len(cuts), largest / len(cuts))
        loudness = loudness * jnp.repeat(jnp.exp(heights), extent[position] // parts).reshape((-1,) + (1,) * (len(extent) - 1 - position))
    return loudness


def assign_block(rng, own, number, rows, number_of, top, most, skew):
    sequence = jax.random.permutation(rng, number_of)
    heavy_load, ordinary = load_shares(number_of, rows * top, most, skew, True), load_shares(number_of, rows * top, most, skew, False)
    places = jnp.arange(number_of)

    def named(lengths, rotation):
        used = int((lengths > 0).sum())
        fixed = max(1, used // 4)
        passed = fixed + (places - fixed + rotation * (used - fixed)) % max(1, number_of - fixed)
        return jnp.zeros((number_of,), jnp.int32).at[sequence[jnp.where(places < fixed, places, passed)]].set(jnp.asarray(lengths, jnp.int32))

    lengths = jnp.where(number % 4 == 0, named(heavy_load, number // 4), named(ordinary, number - number // 4 - 1))
    mixed = jax.random.permutation(jax.random.fold_in(own, 3), number_of)
    source_of, sink = mixed[0:number_of // 2 * 2:2], mixed[1:number_of // 2 * 2:2]
    room = jnp.minimum(lengths[source_of] - 1, most - lengths[sink]) // 2
    room = jnp.where((source_of == sequence[0]) | (sink == sequence[0]) | (lengths[sink] == 0), 0, jnp.maximum(room, 0))
    passed = jax.random.randint(jax.random.fold_in(own, 4), (number_of // 2,), 0, 1 << 20) % (room + 1)
    lengths = lengths.at[source_of].add(-passed).at[sink].add(passed)
    labels = jnp.searchsorted(jnp.cumsum(lengths), jnp.arange(rows * top), side="right").astype(jnp.int32)
    table = labels.reshape(top, rows).T
    table = table[jax.random.permutation(jax.random.fold_in(own, 1), rows)]
    rotation = jax.random.randint(jax.random.fold_in(own, 2), (rows, 1), 0, top)
    return jnp.take_along_axis(table, (jnp.arange(top)[None, :] + rotation) % top, axis=1)


def load_shares(count, total, bound, lean, full):
    loads = [(1 << 20) // math.isqrt(grade ** lean) + 1 for grade in range(1, count + 1)]
    largest = bound if full else min(bound, max(-(-total // count), total * loads[0] // sum(loads)))
    least = 1 if total - largest >= count - 1 else 0
    given, rest = [largest] + [least] * (count - 1), total - largest - least * (count - 1)
    while rest > 0:
        candidates = [i for i in range(1, count) if given[i] < largest] or [i for i in range(1, count) if given[i] < bound]
        pool, remaining = sum([loads[i] for i in candidates]), rest
        for i in candidates:
            extra = min(bound - given[i], max(1, remaining * loads[i] // pool), rest)
            given[i] = given[i] + extra
            rest = rest - extra
    return np.array(given)


def bell_draw(own_key, extent, scale, most, cuts=(), kind=jnp.bfloat16):
    factor_of = shard_levels(own_key, extent, cuts, -0.22, 0.18) if cuts else 1.0
    entries = jax.random.normal(own_key, extent, jnp.float32) * scale * factor_of
    return jnp.minimum(jnp.maximum(entries, -most), most).astype(kind)


def setup_inputs(seed: int = 0) -> dict:
    streams_of = jax.random.split(jax.random.key(seed), 18)
    ssd_input = bell_draw(streams_of[0], (SEQUENCE_LENGTH, SEQUENCE_COUNT, HEADS * HEAD_DIM), 1.0, 6.0, ((0, 16), (2, 8)))
    ssd_gate = bell_draw(streams_of[1], (SEQUENCE_LENGTH, SEQUENCE_COUNT, HEADS * HEAD_DIM), 1.0, 6.0, ((0, 16), (2, 8)))
    state_write = bell_draw(streams_of[2], (SEQUENCE_LENGTH, SEQUENCE_COUNT, GROUPS * STATE), 0.3, 2.0, ((0, 16), (2, 8)))
    state_read = bell_draw(streams_of[3], (SEQUENCE_LENGTH, SEQUENCE_COUNT, GROUPS * STATE), 0.3, 2.0, ((0, 16), (2, 8)))
    step_size = jnp.clip(jnp.exp(math.log(0.1) - 1.609438 * jax.random.uniform(streams_of[4], (HEADS, SEQUENCE_COUNT, SEQUENCE_LENGTH), jnp.float32) ** shard_levels(streams_of[4], (HEADS, SEQUENCE_COUNT, SEQUENCE_LENGTH), ((0, 8), (2, 16)), -0.2, 0.2)), 0.02, 0.1)
    decay_log = draw_decay_log(jax.random.fold_in(streams_of[17], 71), 0)
    skip_gain = jnp.clip(jnp.exp(math.log(2.0) - 1.3862944 * jax.random.uniform(streams_of[6], (HEADS,), jnp.float32) ** shard_levels(streams_of[6], (HEADS,), ((0, 8),), -0.2, 0.2)), 0.5, 2.0)
    norm_gain = jnp.clip(1.0 + 0.1 * jax.random.normal(streams_of[7], (HEADS * HEAD_DIM,), jnp.float32), 0.5, 1.5)
    w_out = bell_draw(streams_of[8], (HEADS * HEAD_DIM, D), (HEADS * HEAD_DIM) ** -0.5, 0.09375, ((0, 8),))
    resid = bell_draw(streams_of[9], (SEQUENCE_LENGTH, SEQUENCE_COUNT, D), 1.0, 6.0, ((0, 128),))
    moe_gain = jnp.clip(1.0 + 0.1 * jax.random.normal(streams_of[10], (D,), jnp.float32), 0.5, 1.5)
    w_gate = bell_draw(streams_of[11], (EXPERTS, D, FF), D ** -0.5, 0.125, ((0, 16), (2, 8)))
    w_up = bell_draw(streams_of[12], (EXPERTS, D, FF), D ** -0.5, 0.125, ((0, 16), (2, 8)))
    w_down = bell_draw(streams_of[13], (EXPERTS, FF, D), FF ** -0.5, 0.0625, ((0, 16), (1, 8)))
    routes_keys = jax.random.split(jax.random.fold_in(streams_of[14], 1), SEQUENCE_LENGTH * SEQUENCE_COUNT // TOK_DEV)
    routes_turns = jax.random.permutation(jax.random.fold_in(streams_of[14], 3), SEQUENCE_LENGTH * SEQUENCE_COUNT // TOK_DEV)
    routes = jax.vmap(lambda own, number: assign_block(jax.random.fold_in(streams_of[14], 2), own, number, TOK_DEV, EXPERTS, 2, CAP, 1))(routes_keys, routes_turns).reshape((SEQUENCE_LENGTH, SEQUENCE_COUNT, 2))
    gates = jnp.clip(0.2 + 0.8 * jax.random.uniform(streams_of[15], (SEQUENCE_LENGTH, SEQUENCE_COUNT, 2), jnp.float32) ** shard_levels(streams_of[15], (SEQUENCE_LENGTH, SEQUENCE_COUNT, 2), ((0, 128),), -0.2, 0.2), 0.2, 1.0)
    directions = bell_draw(streams_of[16], (NDIR, D), 1.0, 6.0, (), jnp.float32)
    return {"ssd_input": ssd_input, "ssd_gate": ssd_gate, "state_write": state_write, "state_read": state_read, "step_size": step_size, "decay_log": decay_log, "skip_gain": skip_gain, "norm_gain": norm_gain, "w_out": w_out, "resid": resid, "moe_gain": moe_gain, "w_gate": w_gate, "w_up": w_up, "w_down": w_down, "routes": routes, "gates": gates, "directions": directions}


def block_step(state, pieces):
    inputs, writes, reads, decay, steps = pieces
    cum = jnp.cumsum(decay, axis=-1)
    scores = jnp.einsum('tbgn,ubgn->bgtu', reads.astype(jnp.float32), writes.astype(jnp.float32))
    spread = cum[..., :, None] - cum[..., None, :]
    causal = jnp.tril(jnp.ones((BLOCK, BLOCK), dtype=bool))
    kernel = jnp.where(causal, jnp.exp(jnp.where(causal, spread, 0.0)), 0.0) * steps[..., None, :]
    weights = lax.optimization_barrier((kernel * scores[:, :, None]).astype(jnp.bfloat16))
    within = jnp.einsum('bgitu,ubgip->tbgip', weights.astype(jnp.float32), inputs.astype(jnp.float32))
    to_end = jnp.exp(cum[..., -1:] - cum) * steps
    scaled = lax.optimization_barrier((inputs.astype(jnp.float32) * jnp.transpose(to_end, (3, 0, 1, 2))[..., None]).astype(jnp.bfloat16))
    contrib = jnp.einsum('ubgip,ubgn->bgipn', scaled.astype(jnp.float32), writes.astype(jnp.float32))
    readout = jnp.einsum('bgipn,tbgn->tbgip', state, reads.astype(jnp.float32), precision=lax.Precision.HIGHEST)
    across = jnp.transpose(jnp.exp(cum), (3, 0, 1, 2))[..., None] * readout
    new_state = jnp.exp(cum[..., -1])[..., None, None] * state + contrib
    return (new_state, within + across)

def reference(ssd_input, ssd_gate, state_write, state_read, step_size, decay_log, skip_gain, norm_gain, w_out, resid, moe_gain, w_gate, w_up, w_down, routes, gates, directions):
    blocks = SEQUENCE_LENGTH // BLOCK
    per_group = HEADS // GROUPS
    inputs = ssd_input.reshape(blocks, BLOCK, SEQUENCE_COUNT, GROUPS, per_group, HEAD_DIM)
    writes = state_write.reshape(blocks, BLOCK, SEQUENCE_COUNT, GROUPS, STATE)
    reads = state_read.reshape(blocks, BLOCK, SEQUENCE_COUNT, GROUPS, STATE)

    def arrange(values):
        moved = jnp.transpose(values.reshape(HEADS, SEQUENCE_COUNT, blocks, BLOCK), (2, 1, 0, 3))
        return moved.reshape(blocks, SEQUENCE_COUNT, GROUPS, per_group, BLOCK)
    start = jnp.zeros((SEQUENCE_COUNT, GROUPS, per_group, HEAD_DIM, STATE), jnp.float32)
    final, outputs = lax.scan(block_step, start, (inputs, writes, reads, arrange(decay_log), arrange(step_size)))
    width = HEADS * HEAD_DIM
    ssd_out = outputs.reshape(SEQUENCE_LENGTH, SEQUENCE_COUNT, width) + jnp.repeat(skip_gain, HEAD_DIM) * ssd_input.astype(jnp.float32)
    gated = ssd_out * jax.nn.silu(ssd_gate.astype(jnp.float32))
    grouped = gated.reshape(SEQUENCE_LENGTH, SEQUENCE_COUNT, GROUPS, per_group * HEAD_DIM)
    factor = lax.rsqrt(lax.optimization_barrier(jnp.mean(grouped * grouped, axis=-1, keepdims=True)) + 1e-05)
    normed = ((grouped * factor).reshape(SEQUENCE_LENGTH, SEQUENCE_COUNT, width) * norm_gain).astype(jnp.bfloat16)
    tokens = SEQUENCE_LENGTH * SEQUENCE_COUNT
    flat_normed = normed.reshape(tokens, N_EXP, width // N_EXP)
    out_blocks = w_out.reshape(N_EXP, width // N_EXP, D)
    hidden_state = resid.reshape(tokens, D).astype(jnp.float32)
    for index in range(N_EXP):
        partial_sum = jnp.dot(flat_normed[:, index], out_blocks[index], preferred_element_type=jnp.float32)
        hidden_state = hidden_state + lax.optimization_barrier(partial_sum.astype(jnp.bfloat16)).astype(jnp.float32)
    scale = lax.rsqrt(lax.optimization_barrier(jnp.mean(hidden_state * hidden_state, axis=-1, keepdims=True)) + 1e-05)
    moe_in = (hidden_state * scale * moe_gain).astype(jnp.bfloat16)
    groups_tok = tokens // TOK_DEV
    picks = routes.reshape(groups_tok, TOK_DEV * 2)
    onehot = (picks[..., None] == jnp.arange(EXPERTS, dtype=jnp.int32)).astype(jnp.int32)
    before = jnp.cumsum(onehot, axis=1) - onehot
    rank = lax.optimization_barrier(jnp.sum(before * onehot, axis=-1))
    per_expert = groups_tok * CAP
    group_index = jnp.arange(groups_tok, dtype=jnp.int32)[:, None]
    target = (picks * per_expert + group_index * CAP + rank).reshape(-1)
    source = jnp.repeat(jnp.arange(tokens, dtype=jnp.int32), 2)
    slots = jnp.zeros((EXPERTS * per_expert, D), jnp.bfloat16).at[target].set(moe_in[source])
    slots = slots.reshape(EXPERTS, per_expert, D)

    def one_expert(items):
        rows, gate_weight, up_weight, down_weight = items
        gate_value = jnp.dot(rows, gate_weight, preferred_element_type=jnp.float32)
        up_value = jnp.dot(rows, up_weight, preferred_element_type=jnp.float32)
        hidden = (jax.nn.silu(gate_value) * up_value).astype(jnp.bfloat16)
        hidden_blocks = hidden.reshape(per_expert, N_EXP, FF // N_EXP)
        down_blocks = down_weight.reshape(N_EXP, FF // N_EXP, D)
        total = jnp.zeros((per_expert, D), jnp.float32)
        for index in range(N_EXP):
            part_sum = jnp.dot(hidden_blocks[:, index], down_blocks[index], preferred_element_type=jnp.float32)
            total = total + lax.optimization_barrier(part_sum.astype(jnp.bfloat16)).astype(jnp.float32)
        return total.astype(jnp.bfloat16)
    results = lax.map(one_expert, (slots, w_gate, w_up, w_down)).reshape(EXPERTS * per_expert, D)
    picked = results[target].astype(jnp.float32).reshape(tokens, 2, D)
    weights = gates.reshape(tokens, 2)
    combined = hidden_state + lax.optimization_barrier(jnp.sum(weights[..., None] * picked, axis=1))
    for index in range(NDIR):
        direction = directions[index]
        along = jnp.dot(combined, direction, precision=lax.Precision.HIGHEST) / (jnp.sum(direction * direction) + 1e-06)
        combined = combined - along[:, None] * direction[None, :]
    return combined.astype(jnp.bfloat16).reshape(SEQUENCE_LENGTH, SEQUENCE_COUNT, D)
```

```python
import jax
import jax.numpy as jnp
from jax import lax
from jax.sharding import PartitionSpec as P

D = 2048
HEADS = 64
HEAD_DIM = 64
STATE = 128
GROUPS = 8
BLOCK = 256


def on_device(
    ssd_input,
    ssd_gate,
    state_write,
    state_read,
    step_size,
    decay_log,
    skip_gain,
    norm_gain,
    w_out,
    resid,
    moe_gain,
    w_gate,
    w_up,
    w_down,
    routes,
    gates,
    directions,
):
    length_dev, seqs, width_dev = ssd_input.shape
    heads_dev = decay_log.shape[0]
    per_group = HEADS // GROUPS
    groups_dev = heads_dev // per_group
    blocks = length_dev // BLOCK
    inputs = ssd_input.reshape(blocks, BLOCK, seqs, groups_dev, per_group, HEAD_DIM)
    writes = state_write.reshape(blocks, BLOCK, seqs, groups_dev, STATE)
    reads = state_read.reshape(blocks, BLOCK, seqs, groups_dev, STATE)

    def arrange(values):
        moved = jnp.transpose(values.reshape(heads_dev, seqs, blocks, BLOCK), (2, 1, 0, 3))
        return moved.reshape(blocks, seqs, groups_dev, per_group, BLOCK)

    decays = jnp.cumsum(arrange(decay_log), axis=-1)
    steps_in = arrange(step_size)
    scores = jnp.einsum("ctbgn,cubgn->cbgtu", reads, writes, preferred_element_type=jnp.float32)
    row_pos = lax.broadcasted_iota(jnp.int32, (BLOCK, BLOCK), 0)
    col_pos = lax.broadcasted_iota(jnp.int32, (BLOCK, BLOCK), 1)
    causal = row_pos >= col_pos
    spread = decays[..., :, None] - decays[..., None, :]
    kernel = (
        jnp.where(causal, jnp.exp(jnp.where(causal, spread, 0.0)), 0.0) * steps_in[..., None, :]
    )
    weights = (kernel * scores[:, :, :, None]).astype(jnp.bfloat16)
    within = jnp.einsum(
        "cbgitu,cubgip->ctbgip", weights, inputs, preferred_element_type=jnp.float32
    )
    to_end = jnp.exp(decays[..., -1:] - decays) * steps_in
    scaled = (inputs * jnp.transpose(to_end, (0, 4, 1, 2, 3))[..., None]).astype(jnp.bfloat16)
    contrib = jnp.einsum("cubgip,cubgn->cbgipn", scaled, writes, preferred_element_type=jnp.float32)
    through = jnp.exp(decays[..., -1])
    running = jnp.zeros(contrib.shape[1:], jnp.float32)
    carried = jnp.ones(through.shape[1:], jnp.float32)
    starts = []
    prefixes = []
    for index in range(blocks):
        starts.append(running)
        prefixes.append(carried)
        running = through[index][..., None, None] * running + contrib[index]
        carried = carried * through[index]

    ranks = lax.axis_size("seq")
    flat_carried = carried.reshape(ranks, 1, 1)
    high = lax.reduce_precision(flat_carried, 8, 7)
    middle = lax.reduce_precision(flat_carried - high, 8, 7)
    low = flat_carried - high - middle
    row = lax.broadcasted_iota(jnp.int32, (ranks, 8, STATE), 1)
    extra = jnp.where(row == 0, high, jnp.where(row == 1, middle, jnp.where(row == 2, low, 0.0)))
    parcel = jnp.concatenate(
        [running.reshape(ranks, HEAD_DIM, STATE), extra], axis=1
    ).astype(jnp.bfloat16)
    parcels = lax.all_to_all(parcel, "seq", split_axis=0, concat_axis=0, tiled=True).astype(
        jnp.float32
    )
    state = jnp.zeros((HEAD_DIM, STATE), jnp.float32)
    states = [state]
    for rank in range(ranks - 1):
        factor = parcels[rank, HEAD_DIM] + parcels[rank, HEAD_DIM + 1] + parcels[rank, HEAD_DIM + 2]
        state = factor[None, :] * state + parcels[rank, :HEAD_DIM]
        states.append(state)
    entering = (
        lax.all_to_all(
            jnp.stack(states).astype(jnp.bfloat16), "seq", split_axis=0, concat_axis=0, tiled=True
        )
        .astype(jnp.float32)
        .reshape(running.shape)
    )
    begin = jnp.stack(starts) + jnp.stack(prefixes)[..., None, None] * entering[None]
    readout = jnp.einsum(
        "cbgipn,ctbgn->ctbgip", begin, reads.astype(jnp.float32), precision=lax.Precision.HIGHEST
    )
    across = jnp.transpose(jnp.exp(decays), (0, 4, 1, 2, 3))[..., None] * readout
    ssd_out = (within + across).reshape(length_dev, seqs, width_dev) + jnp.repeat(
        skip_gain, HEAD_DIM
    ) * ssd_input.astype(jnp.float32)
    gated = ssd_out * jax.nn.silu(ssd_gate.astype(jnp.float32))
    grouped = gated.reshape(length_dev, seqs, groups_dev, per_group * HEAD_DIM)
    factor = lax.rsqrt(jnp.mean(grouped * grouped, axis=-1, keepdims=True) + 1e-05)
    normed = ((grouped * factor).reshape(length_dev, seqs, width_dev) * norm_gain).astype(
        jnp.bfloat16
    )
    flat_normed = normed.reshape(length_dev * seqs, width_dev)
    columns = lax.axis_size("exp")
    rows_keep = length_dev * seqs // columns
    piece = flat_normed
    mixed = lax.psum_scatter(
        jnp.dot(piece, w_out, preferred_element_type=jnp.float32).astype(jnp.bfloat16),
        "exp",
        scatter_dimension=0,
        tiled=True,
    ).astype(jnp.float32)
    hidden_state = resid.reshape(rows_keep, D).astype(jnp.float32) + mixed
    scale = lax.rsqrt(jnp.mean(hidden_state * hidden_state, axis=-1, keepdims=True) + 1e-05)
    moe_in = (hidden_state * scale * moe_gain).astype(jnp.bfloat16)
    experts = lax.axis_size("seq")
    capacity = max(2, 2 * rows_keep * 17 // (16 * experts))
    chosen = routes.reshape(rows_keep, 2)
    picks = chosen.reshape(-1)
    onehot = (picks[:, None] == jnp.arange(experts, dtype=jnp.int32)[None, :]).astype(jnp.int32)
    before = jnp.cumsum(onehot, axis=0) - onehot
    ranked = jnp.sum(before * onehot, axis=1)
    places = picks * capacity + ranked
    pairs = places.reshape(-1, 2)
    first = (capacity + 1) // 2
    returned = []
    for start, count in ((0, first), (first, capacity - first)):
        layout = (
            jnp.arange(experts, dtype=jnp.int32)[:, None] * capacity
            + start
            + jnp.arange(count, dtype=jnp.int32)[None, :]
        ).reshape(-1)
        select = jnp.any(layout[:, None, None] == pairs[None, :, :], axis=2).astype(jnp.bfloat16)
        slots = jnp.dot(select, moe_in, preferred_element_type=jnp.float32).astype(jnp.bfloat16)
        arrived = lax.all_to_all(
            slots.reshape(experts, count, D), "seq", split_axis=0, concat_axis=0, tiled=True
        )
        rows = lax.all_gather(arrived.reshape(experts * count, D), "exp", axis=0, tiled=True)
        gate_value = jnp.dot(rows, w_gate[0], preferred_element_type=jnp.float32)
        up_value = jnp.dot(rows, w_up[0], preferred_element_type=jnp.float32)
        hidden = (jax.nn.silu(gate_value) * up_value).astype(jnp.bfloat16)
        summed = lax.psum_scatter(
            jnp.dot(hidden, w_down[0], preferred_element_type=jnp.float32).astype(jnp.bfloat16),
            "exp",
            scatter_dimension=0,
            tiled=True,
        )
        returned.append(
            lax.all_to_all(
                summed.reshape(experts, count, D), "seq", split_axis=0, concat_axis=0, tiled=True
            )
        )
    returned = jnp.concatenate(returned, axis=1)
    picked = (
        jnp.take(returned.reshape(experts * capacity, D), places, axis=0)
        .astype(jnp.float32)
        .reshape(rows_keep, 2, D)
    )
    combined = hidden_state + jnp.sum(gates.reshape(rows_keep, 2)[..., None] * picked, axis=1)
    for index in range(directions.shape[0]):
        direction = directions[index]
        along = jnp.dot(combined, direction, precision=lax.Precision.HIGHEST) / (
            jnp.sum(direction * direction) + 1e-06
        )
        combined = combined - along[:, None] * direction[None, :]
    return combined.astype(jnp.bfloat16).reshape(length_dev // columns, seqs, D)


def solution(mesh):
    in_specs = (
        P("seq", None, "exp"),
        P("seq", None, "exp"),
        P("seq", None, "exp"),
        P("seq", None, "exp"),
        P("exp", None, "seq"),
        P("exp", None, "seq"),
        P("exp"),
        P("exp"),
        P("exp", None),
        P(("seq", "exp"), None, None),
        P(),
        P("seq", None, "exp"),
        P("seq", None, "exp"),
        P("seq", "exp", None),
        P(("seq", "exp"), None, None),
        P(("seq", "exp"), None, None),
        P(),
    )
    out_specs = P(("seq", "exp"), None, None)
    return jax.shard_map(
        on_device, mesh=mesh, in_specs=in_specs, out_specs=out_specs, check_vma=False
    )
```

```python
import functools

import jax
import jax.numpy as jnp
from jax import lax
from jax.experimental import pallas as pl
from jax.experimental.pallas import tpu as pltpu
from jax.sharding import PartitionSpec as P

D = 2048
HEADS = 64
HEAD_DIM = 64
STATE = 128
GROUPS = 8
BLOCK = 256
FOLD = 16
F32 = jnp.float32
BF16 = jnp.bfloat16


def dot_last(left, right, **options):
    return lax.dot_general(
        left, right, (((1,), (1,)), ((), ())), preferred_element_type=F32, **options
    )


def two_parts(values):
    high = values.astype(BF16)
    return high, (values - high.astype(F32)).astype(BF16)


def triangle():
    row = lax.broadcasted_iota(jnp.int32, (BLOCK, BLOCK), 0)
    col = lax.broadcasted_iota(jnp.int32, (BLOCK, BLOCK), 1)
    return row >= col


def spread_heads(columns, heads):
    rows = columns.shape[0]
    lane = lax.broadcasted_iota(jnp.int32, (rows, 2 * HEAD_DIM), 1)
    pieces = []
    for head in range(0, heads, 2):
        left = jnp.broadcast_to(columns[:, head : head + 1], (rows, 2 * HEAD_DIM))
        right = jnp.broadcast_to(columns[:, head + 1 : head + 2], (rows, 2 * HEAD_DIM))
        pieces.append(jnp.where(lane < HEAD_DIM, left, right))
    return jnp.concatenate(pieces, axis=1)


def over_rows(values):
    heads = values.shape[0]
    return jnp.broadcast_to(values[:, None, :], (heads, HEAD_DIM, STATE)).reshape(
        heads * HEAD_DIM, STATE
    )


def contrib_kernel(decay, step, inputs, writes, parcel, first, total, running):
    block = pl.program_id(1)
    heads = decay.shape[1]
    ones = triangle().astype(F32)
    decays = decay[0]
    cum_row = dot_last(decays, ones, precision=lax.Precision.HIGHEST)
    end_row = jnp.broadcast_to(cum_row[:, BLOCK - 1 :], (heads, STATE))
    to_end_row = jnp.exp(cum_row[:, BLOCK - 1 :] - cum_row) * step[0]
    to_end = jnp.transpose(to_end_row)
    scaled = (inputs[0].astype(F32) * spread_heads(to_end, heads)).astype(BF16)
    contrib = lax.dot_general(
        scaled, writes[0], (((0,), (0,)), ((), ())), preferred_element_type=F32
    )

    @pl.when(block == 0)
    def _():
        first[0] = contrib
        running[...] = contrib
        total[...] = end_row

    @pl.when(block > 0)
    def _():
        running[...] = over_rows(jnp.exp(end_row)) * running[...] + contrib
        total[...] = total[...] + end_row

    @pl.when(block == pl.num_programs(1) - 1)
    def _():
        carried = jnp.exp(total[...])
        high, rest = two_parts(carried)
        middle, low = two_parts(carried - high.astype(F32))
        row = lax.broadcasted_iota(jnp.int32, (heads, 8, STATE), 1)
        wide = lambda part: jnp.broadcast_to(part.astype(F32)[:, None, :], (heads, 8, STATE))
        extra = jnp.where(
            row == 0,
            wide(high),
            jnp.where(row == 1, wide(middle), jnp.where(row == 2, wide(low), 0.0)),
        )
        parcel[:, :HEAD_DIM, :] = running[...].reshape(heads, HEAD_DIM, STATE).astype(BF16)
        parcel[:, HEAD_DIM:, :] = extra.astype(BF16)


def contrib_call(decays, steps, inputs, writes):
    seqs, heads, length = decays.shape
    width = inputs.shape[2]
    blocks = length // BLOCK
    return pl.pallas_call(
        contrib_kernel,
        grid=(seqs, blocks),
        in_specs=[
            pl.BlockSpec((1, heads, BLOCK), lambda b, c: (b, 0, c)),
            pl.BlockSpec((1, heads, BLOCK), lambda b, c: (b, 0, c)),
            pl.BlockSpec((1, BLOCK, width), lambda b, c: (b, c, 0)),
            pl.BlockSpec((1, BLOCK, STATE), lambda b, c: (b, c, 0)),
        ],
        out_specs=[
            pl.BlockSpec((heads, HEAD_DIM + 8, STATE), lambda b, c: (b, 0, 0)),
            pl.BlockSpec((1, width, STATE), lambda b, c: (b, 0, 0)),
        ],
        out_shape=[
            jax.ShapeDtypeStruct((seqs * heads, HEAD_DIM + 8, STATE), BF16),
            jax.ShapeDtypeStruct((seqs, width, STATE), F32),
        ],
        scratch_shapes=[pltpu.VMEM((heads, STATE), F32), pltpu.VMEM((width, STATE), F32)],
        compiler_params=pltpu.CompilerParams(
            dimension_semantics=("arbitrary", "arbitrary"), vmem_limit_bytes=28 * 2**20
        ),
        cost_estimate=pl.CostEstimate(flops=10**9, bytes_accessed=2 * 2**20, transcendentals=8192),
        name="contrib",
    )(decays, steps, inputs, writes)


def within_kernel(decay, step, inputs, writes, reads, skip, within):
    heads = decay.shape[1]
    causal = triangle()
    ones = causal.astype(F32)
    log2e = 1.4426950408889634
    decays = decay[0]
    cum_row = dot_last(decays, ones, precision=lax.Precision.HIGHEST) * log2e
    cum_col = jnp.transpose(cum_row)
    steps = step[0]
    scores = dot_last(reads[0], writes[0])
    scores = jnp.where(causal, scores, 0.0)
    quad = 4 * HEAD_DIM
    lane = lax.broadcasted_iota(jnp.int32, (BLOCK, quad), 1)
    for start in range(0, heads, 4):
        columns = inputs[0][:, start * HEAD_DIM : start * HEAD_DIM + quad]
        total = skip[:, start * HEAD_DIM : start * HEAD_DIM + quad] * columns.astype(F32)
        for offset in range(4):
            head = start + offset
            gap = jnp.minimum(cum_col[:, head : head + 1] - cum_row[head : head + 1, :], 0.0)
            weights = (jnp.exp2(gap) * steps[head : head + 1, :] * scores).astype(BF16)
            own = (lane >= offset * HEAD_DIM) & (lane < (offset + 1) * HEAD_DIM)
            total = total + jnp.dot(
                weights,
                jnp.where(own, columns, jnp.zeros_like(columns)),
                preferred_element_type=F32,
            )
        within[0, :, start * HEAD_DIM : start * HEAD_DIM + quad] = total


def within_call(which, decays, steps, inputs, writes, reads, skip):
    seqs, heads, length = decays.shape
    width = inputs.shape[2]
    return pl.pallas_call(
        within_kernel,
        grid=(length // BLOCK,),
        in_specs=[
            pl.BlockSpec((1, heads, BLOCK), lambda c: (which, 0, c)),
            pl.BlockSpec((1, heads, BLOCK), lambda c: (which, 0, c)),
            pl.BlockSpec((1, BLOCK, width), lambda c: (which, c, 0)),
            pl.BlockSpec((1, BLOCK, STATE), lambda c: (which, c, 0)),
            pl.BlockSpec((1, BLOCK, STATE), lambda c: (which, c, 0)),
            pl.BlockSpec((1, width), lambda c: (0, 0)),
        ],
        out_specs=pl.BlockSpec((1, BLOCK, width), lambda c: (0, c, 0)),
        out_shape=jax.ShapeDtypeStruct((1, length, width), F32),
        compiler_params=pltpu.CompilerParams(
            dimension_semantics=("arbitrary",), vmem_limit_bytes=28 * 2**20
        ),
        cost_estimate=pl.CostEstimate(
            flops=3 * 10**9, bytes_accessed=2 * 2**20, transcendentals=2**20
        ),
        name="within",
    )(decays, steps, inputs, writes, reads, skip)


def scan_kernel(parcels, states):
    ranks = parcels.shape[0]
    state = jnp.zeros((HEAD_DIM, STATE), F32)
    for rank in range(ranks):
        states[rank] = state.astype(BF16)
        if rank < ranks - 1:
            extra = parcels[rank, HEAD_DIM:, :].astype(F32)
            factor = extra[0:1] + extra[1:2] + extra[2:3]
            state = factor * state + parcels[rank, :HEAD_DIM, :].astype(F32)


def scan_call(parcels):
    ranks = parcels.shape[0]
    return pl.pallas_call(
        scan_kernel,
        out_shape=jax.ShapeDtypeStruct((ranks, HEAD_DIM, STATE), BF16),
        cost_estimate=pl.CostEstimate(flops=10**6, bytes_accessed=2**19, transcendentals=0),
        name="scan",
    )(parcels)


def mixer_kernel(
    place, decay, reads, entering, first, within, gate, gain, weight, kept, passed, held, sems
):
    block = pl.program_id(0)
    blocks = pl.num_programs(0)
    heads = decay.shape[1]
    width = gate.shape[2]
    chips, keep = kept.shape[0], kept.shape[1]
    ones = triangle().astype(F32)
    decays = decay[0]
    before = block > 0
    cum_row = dot_last(decays[:, BLOCK:], ones, precision=lax.Precision.HIGHEST)
    head_row = dot_last(decays[:, :BLOCK], ones, precision=lax.Precision.HIGHEST)
    prefix = jnp.exp(jnp.broadcast_to(head_row[:, BLOCK - 1 :], (heads, STATE)))
    arrived = entering[...].astype(F32).reshape(width, STATE)
    begin = jnp.where(before, over_rows(prefix) * arrived + first[0], arrived)
    cum = jnp.transpose(jnp.exp(jnp.where(before, cum_row, head_row)))
    high, low = two_parts(begin)
    vectors = reads[0]
    readout = dot_last(vectors, high) + dot_last(vectors, low)
    ssd_out = within[0] + spread_heads(cum, heads) * readout
    gates = gate[0].astype(F32)
    gated = ssd_out * (gates / (1.0 + jnp.exp(-gates)))
    factor = lax.rsqrt(jnp.mean(gated * gated, axis=-1, keepdims=True) + 1e-05)
    normed = (gated * factor * gain[...]).astype(BF16)
    product = jnp.dot(normed, weight[...], preferred_element_type=F32).astype(BF16)
    held[block] = product.reshape(held.shape[1], keep, D)
    pieces = held.shape[1]
    chip, core = lax.div(place[0], 2), lax.rem(place[0], 2)

    def piece(step, index, target):
        distance = lax.rem(step * (pieces // 2) + index // 2 - chip + chips, chips)
        return pltpu.make_async_copy(
            held.at[step, index], target.at[distance], sems.at[step, index]
        )

    for index in range(pieces):

        @pl.when(core == index % 2)
        def _():
            piece(block, index, kept).start()

        @pl.when(core != index % 2)
        def _():
            piece(block, index, passed).start()

    @pl.when(block == blocks - 1)
    def _():
        for step in range(held.shape[0]):
            for index in range(pieces):
                piece(step, index, kept).wait()


def mixer_call(which, place, decays, reads, entering, first, within, gate, gain, weight, columns):
    seqs, heads, length = decays.shape
    width = gate.shape[2]
    blocks = length // BLOCK
    keep = length // columns
    anywhere = pl.BlockSpec(memory_space=pl.ANY)
    return pl.pallas_call(
        mixer_kernel,
        grid=(blocks,),
        in_specs=[
            pl.BlockSpec(memory_space=pltpu.SMEM),
            pl.BlockSpec((1, heads, length), lambda c: (which, 0, 0)),
            pl.BlockSpec((1, BLOCK, STATE), lambda c: (which, c, 0)),
            pl.BlockSpec((heads, HEAD_DIM, STATE), lambda c: (which, 0, 0)),
            pl.BlockSpec((1, width, STATE), lambda c: (which, 0, 0)),
            pl.BlockSpec((1, BLOCK, width), lambda c: (0, c, 0)),
            pl.BlockSpec((1, BLOCK, width), lambda c: (which, c, 0)),
            pl.BlockSpec((1, width), lambda c: (0, 0)),
            pl.BlockSpec((width, D), lambda c: (0, 0)),
        ],
        out_specs=[anywhere, anywhere],
        out_shape=[jax.ShapeDtypeStruct((columns // 2, keep, D), BF16)] * 2,
        scratch_shapes=[
            pltpu.VMEM((blocks, columns // blocks, keep, D), BF16),
            pltpu.SemaphoreType.DMA((blocks, columns // blocks)),
        ],
        compiler_params=pltpu.CompilerParams(
            dimension_semantics=("arbitrary",), vmem_limit_bytes=28 * 2**20
        ),
        cost_estimate=pl.CostEstimate(
            flops=2 * 10**9, bytes_accessed=6 * 2**20, transcendentals=2**18
        ),
        name="mixer",
    )(place, decays, reads, entering, first, within, gate, gain, weight)


def unfold(rows, folded):
    pieces = [folded[pl.ds(part, rows, stride=FOLD), :].astype(BF16) for part in range(FOLD)]
    return jnp.concatenate(pieces, axis=1)


def fold(values, folded):
    rows = values.shape[0]
    for part in range(FOLD):
        folded[pl.ds(part, rows, stride=FOLD), :] = values[:, part * 128 : (part + 1) * 128]


def dispatch_kernel(
    residual, gain, places, own_top, got_top, own_bottom, got_bottom, *refs
):
    others = refs[:4]
    hidden, packed, folded = refs[4:]
    half = own_top.shape[1]
    for index, (own, got) in enumerate(((own_top, got_top), (own_bottom, got_bottom))):
        span = pl.ds(index * half, half)
        hidden[span, :] = (
            residual[span, :].astype(F32)
            + (own[0].astype(F32) + got[0].astype(F32))
            + others[2 * index][...].astype(F32)
            + others[2 * index + 1][...].astype(F32)
        )
    state = hidden[...]
    scale = lax.rsqrt(jnp.mean(state * state, axis=-1, keepdims=True) + 1e-05)
    moe_in = (state * scale * gain[...]).astype(BF16)
    rows = packed.shape[0]
    slot = lax.broadcasted_iota(jnp.int32, (rows + rows // FOLD, state.shape[0]), 0)
    chosen = (slot == places[0:1, :]) | (slot == places[1:2, :])
    select = jnp.where(chosen, 1.0, 0.0).astype(BF16)
    slots = jnp.dot(select, moe_in, preferred_element_type=F32)
    packed[:, :D] = slots[:rows].astype(BF16)
    fold(slots[rows:], folded)
    packed[:, D:] = folded[...].astype(BF16)


def dispatch_call(residual, gain, places, owns, others, experts):
    rows, half = residual.shape[0], residual.shape[0] // 2
    count = experts * FOLD
    whole = lambda shape: pl.BlockSpec(shape, lambda i: (0,) * len(shape))
    return pl.pallas_call(
        dispatch_kernel,
        grid=(1,),
        in_specs=[whole(residual.shape), whole(gain.shape), whole(places.shape)]
        + [whole((1, half, D))] * 4
        + [whole((half, D))] * 4,
        out_specs=[whole((rows, D)), whole((count, D + 128))],
        out_shape=[
            jax.ShapeDtypeStruct((rows, D), F32),
            jax.ShapeDtypeStruct((count, D + 128), BF16),
        ],
        scratch_shapes=[pltpu.VMEM((count, 128), F32)],
        compiler_params=pltpu.CompilerParams(vmem_limit_bytes=24 * 2**20),
        cost_estimate=pl.CostEstimate(
            flops=2 * 10**8, bytes_accessed=5 * 2**20, transcendentals=0
        ),
        name="dispatch",
    )(residual, gain, places, *owns, *others)


def combine_kernel(returned, places, gates, hidden, directions, out, folded, values):
    slots, rows = values.shape[0], hidden.shape[0]
    count = returned.shape[0]
    folded[...] = returned[:, D:].astype(F32)
    values[:count, :] = returned[:, :D]
    values[count:, :] = unfold(slots - count, folded)
    slot = lax.broadcasted_iota(jnp.int32, (rows, slots), 1)
    zero = jnp.zeros((rows, slots), F32)
    mix = jnp.where(slot == places[:, 0:1], gates[:, 0:1], zero) + jnp.where(
        slot == places[:, 1:2], gates[:, 1:2], zero
    )
    high, rest = two_parts(mix)
    middle, low = two_parts(mix - high.astype(F32))
    parts = jnp.concatenate([high, middle, low], axis=0)
    product = jnp.dot(parts, values[...], preferred_element_type=F32)
    combined = hidden[...] + (
        product[:rows] + product[rows : 2 * rows] + product[2 * rows :]
    )
    for index in range(directions.shape[0]):
        direction = directions[index : index + 1, :]
        norm = jnp.sum(direction * direction, axis=1, keepdims=True) + 1e-06
        along = jnp.sum(combined * direction, axis=1, keepdims=True) / norm
        combined = combined - along * direction
    out[...] = combined.astype(BF16)


def combine_call(returned, places, gates, hidden, directions):
    rows = hidden.shape[0]
    count = returned.shape[0]
    return pl.pallas_call(
        combine_kernel,
        out_shape=jax.ShapeDtypeStruct((rows, D), BF16),
        scratch_shapes=[
            pltpu.VMEM((count, 128), F32),
            pltpu.VMEM((count + count // FOLD, D), BF16),
        ],
        compiler_params=pltpu.CompilerParams(vmem_limit_bytes=24 * 2**20),
        cost_estimate=pl.CostEstimate(flops=10**9, bytes_accessed=4 * 2**20, transcendentals=0),
        name="combine",
    )(returned, places, gates, hidden, directions)


def expert_kernel(counts, *refs):
    number = len(counts)
    parts = refs[:number]
    gate, up, down, kept, passed = refs[number : number + 5]
    values, extra, folded, hidden, tail, main_sems, extra_sems = refs[number + 5 :]
    places = [sum(counts[:index]) for index in range(number)]
    count = sum(counts)
    lone = count // FOLD
    loads, extras = [], []
    for index, (part, place, size) in enumerate(zip(parts, places, counts)):
        span = pl.ds(place, size)
        extras.append(
            pltpu.make_async_copy(
                part.at[:, pl.ds(D, 128)], extra.at[span, :], extra_sems.at[index]
            )
        )
        loads.append(
            pltpu.make_async_copy(
                part.at[:, pl.ds(0, D)], values.at[span, :], main_sems.at[index]
            )
        )
    for load in extras + loads:
        load.start()
    for load in extras:
        load.wait()
    folded[...] = extra[...].astype(F32)
    values[count:, :] = unfold(lone, folded)
    for load in loads:
        load.wait()
    units = down.shape[0]
    whole = units // 256 * 256

    def open_units(start, size):
        span = pl.ds(start, size)
        first = jnp.dot(values[...], gate[:, span], preferred_element_type=F32)
        second = jnp.dot(values[...], up[:, span], preferred_element_type=F32)
        hidden[:, span] = (first / (1.0 + jnp.exp(-first)) * second).astype(BF16)

    @pl.loop(0, whole // 256)
    def _(index):
        open_units(pl.multiple_of(index * 256, 256), 256)

    if units > whole:
        open_units(whole, units - whole)
    half = kept.shape[0]

    @pl.loop(0, D // 256)
    def _(index):
        span = pl.ds(pl.multiple_of(index * 256, 256), 256)
        result = jnp.dot(hidden[...], down[:, span], preferred_element_type=F32)
        kept[:, span] = result[:half].astype(BF16)
        passed[:, span] = result[half:count].astype(BF16)
        tail[:, span] = result[count:]

    fold(tail[...], folded)
    kept[:, D:] = folded[:half, :].astype(BF16)
    passed[:, D:] = folded[half:, :].astype(BF16)


def expert_call(parts, gate, up, down):
    counts = tuple(part.shape[0] for part in parts)
    count = sum(counts)
    rows = count + count // FOLD
    units = down.shape[0]
    anywhere = pl.BlockSpec(memory_space=pl.ANY)
    near = pl.BlockSpec(memory_space=pltpu.VMEM)
    return pl.pallas_call(
        functools.partial(expert_kernel, counts),
        in_specs=[anywhere] * len(parts) + [near] * 3,
        out_specs=[near, near],
        out_shape=[jax.ShapeDtypeStruct((count // 2, D + 128), BF16)] * 2,
        scratch_shapes=[
            pltpu.VMEM((rows, D), BF16),
            pltpu.VMEM((count, 128), BF16),
            pltpu.VMEM((count, 128), F32),
            pltpu.VMEM((rows, units), BF16),
            pltpu.VMEM((count // FOLD, D), F32),
            pltpu.SemaphoreType.DMA((len(parts),)),
            pltpu.SemaphoreType.DMA((len(parts),)),
        ],
        compiler_params=pltpu.CompilerParams(vmem_limit_bytes=24 * 2**20),
        cost_estimate=pl.CostEstimate(
            flops=6 * rows * D * units,
            bytes_accessed=4 * rows * D + 6 * D * units,
            transcendentals=rows * units,
        ),
        name="expert",
    )(*parts, gate, up, down)


def from_before(values):
    size = lax.axis_size("exp")
    return lax.ppermute(values, "exp", [(i, (i + 2) % size) for i in range(size)])


def from_after(values):
    size = lax.axis_size("exp")
    return lax.ppermute(values, "exp", [(i, (i - 2) % size) for i in range(size)])


def from_sibling(values):
    size = lax.axis_size("exp")
    return lax.ppermute(values, "exp", [(i, i ^ 1) for i in range(size)])


def add_up(*terms):
    total = terms[0].astype(F32)
    for term in terms[1:]:
        total = total + term.astype(F32)
    return total.astype(BF16)


def after(values, *earlier):
    return lax.optimization_barrier((tuple(values), earlier))[0]


def expert_layer(own, gate, up, down):
    half = own.shape[0] // 2
    top, bottom = own[:half], own[half:]
    own_other = from_sibling(own)
    before_top = from_before(top)
    after_bottom = from_after(bottom)
    call = functools.partial(expert_call, gate=gate, up=up, down=down)
    kept_own, passed = call((own, own_other))
    before_top, after_bottom, kept_own, passed, top, bottom = after(
        (before_top, after_bottom, kept_own, passed, top, bottom)
    )
    got_own = from_sibling(passed)
    others = from_sibling(before_top), from_sibling(after_bottom)
    far_top = from_before(before_top)
    far_bottom = from_after(after_bottom)
    before_bottom = from_before(bottom)
    after_top = from_after(top)
    kept, passed = call((before_top, after_bottom, *others))
    far_top, far_bottom, got_own, kept, passed = after(
        (far_top, far_bottom, got_own, kept, passed)
    )
    got = from_sibling(passed)
    others = from_sibling(far_top), from_sibling(far_bottom)
    near_top, near_bottom = add_up(kept[:half], got[:half]), add_up(kept[half:], got[half:])
    near_top, near_bottom, far_top, far_bottom = after(
        (near_top, near_bottom, far_top, far_bottom)
    )
    top_after = from_after(near_top)
    bottom_before = from_before(near_bottom)
    kept, passed = call((far_top, far_bottom, *others))
    after_top, before_bottom, kept, passed = after((after_top, before_bottom, kept, passed))
    late = from_sibling(after_top), from_sibling(before_bottom)
    got = from_sibling(passed)
    far_top, far_bottom = add_up(kept[:half], got[:half]), add_up(kept[half:], got[half:])
    far_top, far_bottom, after_top, before_bottom = after(
        (far_top, far_bottom, after_top, before_bottom)
    )
    relay_top = from_before(far_top)
    relay_bottom = from_after(far_bottom)
    kept, passed = call((after_top, before_bottom, *late))
    relay_top, relay_bottom, top_after, bottom_before, kept, passed = after(
        (relay_top, relay_bottom, top_after, bottom_before, kept, passed)
    )
    got = from_sibling(passed)
    top_before = from_before(add_up(kept[:half], got[:half], relay_top))
    bottom_after = from_after(add_up(kept[half:], got[half:], relay_bottom))
    return jnp.concatenate(
        [
            add_up(kept_own[:half], got_own[:half], top_after, top_before),
            add_up(kept_own[half:], got_own[half:], bottom_before, bottom_after),
        ],
        axis=0,
    )


def on_device(
    ssd_input,
    ssd_gate,
    state_write,
    state_read,
    step_size,
    decay_log,
    skip_gain,
    norm_gain,
    w_out,
    resid,
    moe_gain,
    w_gate,
    w_up,
    w_down,
    routes,
    gates,
    directions,
):
    length_dev, seqs, width_dev = ssd_input.shape
    heads_dev = decay_log.shape[0]
    experts = lax.axis_size("seq")
    columns = lax.axis_size("exp")
    rows_keep = length_dev * seqs // columns

    def swap(values):
        return jnp.transpose(values, (1, 0, 2))

    decays, steps = swap(decay_log), swap(step_size)
    inputs, writes, reads = swap(ssd_input), swap(state_write), swap(state_read)
    parcel, first = contrib_call(decays, steps, inputs, writes)
    parcels = lax.all_to_all(parcel, "seq", split_axis=0, concat_axis=0, tiled=True)
    skip = jnp.repeat(skip_gain, HEAD_DIM)[None, :]
    within_early = within_call(0, decays, steps, inputs, writes, reads, skip)
    (parcels,) = after((parcels,), within_early)
    entering = lax.all_to_all(
        scan_call(parcels), "seq", split_axis=0, concat_axis=0, tiled=True
    )
    within_late = within_call(1, decays, steps, inputs, writes, reads, skip)
    gating = swap(ssd_gate)
    (entering,) = after((entering,), within_late, gating)
    place = lax.axis_index("exp").astype(jnp.int32)[None]
    shared = (decays, reads, entering, first)
    kept, passed = mixer_call(
        0, place, *shared, within_early, gating, norm_gain[None, :], w_out, columns
    )
    got = from_sibling(passed)
    (gating,) = after((gating,), kept)
    kept_late, passed = mixer_call(
        1, place, *shared, within_late, gating, norm_gain[None, :], w_out, columns
    )
    got_late = from_sibling(passed)
    relay_top = from_before(add_up(kept[2], got[2]))
    top_after = from_after(add_up(kept[3], got[3]))
    relay_bottom = from_after(add_up(kept_late[2], got_late[2]))
    bottom_before = from_before(add_up(kept_late[1], got_late[1]))
    top_before = from_before(add_up(kept[1], got[1], relay_top))
    bottom_after = from_after(add_up(kept_late[3], got_late[3], relay_bottom))
    capacity = max(2, 2 * rows_keep * 17 // (16 * experts))
    assert capacity == FOLD + 1
    picks = swap(routes).reshape(-1)
    onehot = (picks[:, None] == jnp.arange(experts, dtype=jnp.int32)[None, :]).astype(jnp.int32)
    before = jnp.cumsum(onehot, axis=0) - onehot
    ranked = jnp.sum(before * onehot, axis=1)
    places = jnp.where(
        ranked < FOLD, picks * FOLD + ranked, experts * FOLD + picks
    ).reshape(rows_keep, 2)
    hidden_state, packed = dispatch_call(
        swap(resid).reshape(rows_keep, D),
        moe_gain[None, :],
        places.T,
        (kept, got, kept_late, got_late),
        (top_after, top_before, bottom_before, bottom_after),
        experts,
    )
    arrived = lax.all_to_all(
        packed.reshape(experts, FOLD, D + 128), "seq", split_axis=0, concat_axis=0, tiled=True
    )
    summed = expert_layer(arrived.reshape(packed.shape), w_gate[0], w_up[0], w_down[0])
    returned = lax.all_to_all(
        summed.reshape(experts, FOLD, D + 128), "seq", split_axis=0, concat_axis=0, tiled=True
    )
    combined = combine_call(
        returned.reshape(packed.shape),
        places,
        swap(gates).reshape(rows_keep, 2),
        hidden_state,
        directions,
    )
    return swap(combined.reshape(seqs, length_dev // columns, D))


def solution(mesh):
    in_specs = (
        P("seq", None, "exp"),
        P("seq", None, "exp"),
        P("seq", None, "exp"),
        P("seq", None, "exp"),
        P("exp", None, "seq"),
        P("exp", None, "seq"),
        P("exp"),
        P("exp"),
        P("exp", None),
        P(("seq", "exp"), None, None),
        P(),
        P("seq", None, "exp"),
        P("seq", None, "exp"),
        P("seq", "exp", None),
        P(("seq", "exp"), None, None),
        P(("seq", "exp"), None, None),
        P(),
    )
    out_specs = P(("seq", "exp"), None, None)
    return jax.shard_map(
        on_device, mesh=mesh, in_specs=in_specs, out_specs=out_specs, check_vma=False
    )
```

```python
import functools

import jax
import jax.numpy as jnp
from jax import lax
from jax.experimental import pallas as pl
from jax.experimental.pallas import tpu as pltpu
from jax.sharding import PartitionSpec as P

D = 2048
HEADS = 64
HEAD_DIM = 64
STATE = 128
GROUPS = 8
BLOCK = 256
FOLD = 16
F32 = jnp.float32
BF16 = jnp.bfloat16


def dot_last(left, right, **options):
    return lax.dot_general(
        left, right, (((1,), (1,)), ((), ())), preferred_element_type=F32, **options
    )


def two_parts(values):
    high = values.astype(BF16)
    return high, (values - high.astype(F32)).astype(BF16)


def triangle():
    row = lax.broadcasted_iota(jnp.int32, (BLOCK, BLOCK), 0)
    col = lax.broadcasted_iota(jnp.int32, (BLOCK, BLOCK), 1)
    return row >= col


def spread_heads(columns, heads):
    rows = columns.shape[0]
    lane = lax.broadcasted_iota(jnp.int32, (rows, 2 * HEAD_DIM), 1)
    pieces = []
    for head in range(0, heads, 2):
        left = jnp.broadcast_to(columns[:, head : head + 1], (rows, 2 * HEAD_DIM))
        right = jnp.broadcast_to(columns[:, head + 1 : head + 2], (rows, 2 * HEAD_DIM))
        pieces.append(jnp.where(lane < HEAD_DIM, left, right))
    return jnp.concatenate(pieces, axis=1)


def over_rows(values):
    heads = values.shape[0]
    return jnp.broadcast_to(values[:, None, :], (heads, HEAD_DIM, STATE)).reshape(
        heads * HEAD_DIM, STATE
    )


def contrib_kernel(decay, step, inputs, writes, parcel, first, total, running):
    block = pl.program_id(1)
    heads = decay.shape[1]
    ones = triangle().astype(F32)
    decays = decay[0]
    cum_row = dot_last(decays, ones, precision=lax.Precision.HIGHEST)
    end_row = jnp.broadcast_to(cum_row[:, BLOCK - 1 :], (heads, STATE))
    to_end_row = jnp.exp(cum_row[:, BLOCK - 1 :] - cum_row) * step[0]
    to_end = jnp.transpose(to_end_row)
    scaled = (inputs[0].astype(F32) * spread_heads(to_end, heads)).astype(BF16)
    contrib = lax.dot_general(
        scaled, writes[0], (((0,), (0,)), ((), ())), preferred_element_type=F32
    )

    @pl.when(block == 0)
    def _():
        first[0] = contrib
        running[...] = contrib
        total[...] = end_row

    @pl.when(block > 0)
    def _():
        running[...] = over_rows(jnp.exp(end_row)) * running[...] + contrib
        total[...] = total[...] + end_row

    @pl.when(block == pl.num_programs(1) - 1)
    def _():
        carried = jnp.exp(total[...])
        high, rest = two_parts(carried)
        middle, low = two_parts(carried - high.astype(F32))
        row = lax.broadcasted_iota(jnp.int32, (heads, 8, STATE), 1)
        wide = lambda part: jnp.broadcast_to(part.astype(F32)[:, None, :], (heads, 8, STATE))
        extra = jnp.where(
            row == 0,
            wide(high),
            jnp.where(row == 1, wide(middle), jnp.where(row == 2, wide(low), 0.0)),
        )
        parcel[:, :HEAD_DIM, :] = running[...].reshape(heads, HEAD_DIM, STATE).astype(BF16)
        parcel[:, HEAD_DIM:, :] = extra.astype(BF16)


def contrib_call(decays, steps, inputs, writes):
    seqs, heads, length = decays.shape
    width = inputs.shape[2]
    blocks = length // BLOCK
    return pl.pallas_call(
        contrib_kernel,
        grid=(seqs, blocks),
        in_specs=[
            pl.BlockSpec((1, heads, BLOCK), lambda b, c: (b, 0, c)),
            pl.BlockSpec((1, heads, BLOCK), lambda b, c: (b, 0, c)),
            pl.BlockSpec((1, BLOCK, width), lambda b, c: (b, c, 0)),
            pl.BlockSpec((1, BLOCK, STATE), lambda b, c: (b, c, 0)),
        ],
        out_specs=[
            pl.BlockSpec((heads, HEAD_DIM + 8, STATE), lambda b, c: (b, 0, 0)),
            pl.BlockSpec((1, width, STATE), lambda b, c: (b, 0, 0)),
        ],
        out_shape=[
            jax.ShapeDtypeStruct((seqs * heads, HEAD_DIM + 8, STATE), BF16),
            jax.ShapeDtypeStruct((seqs, width, STATE), F32),
        ],
        scratch_shapes=[pltpu.VMEM((heads, STATE), F32), pltpu.VMEM((width, STATE), F32)],
        compiler_params=pltpu.CompilerParams(
            dimension_semantics=("arbitrary", "arbitrary"), vmem_limit_bytes=16 * 2**20
        ),
        cost_estimate=pl.CostEstimate(flops=10**9, bytes_accessed=2 * 2**20, transcendentals=8192),
        name="contrib",
    )(decays, steps, inputs, writes)


def within_kernel(decay, step, inputs, writes, reads, skip, within):
    heads = decay.shape[1]
    causal = triangle()
    ones = causal.astype(F32)
    log2e = 1.4426950408889634
    decays = decay[0]
    cum_row = dot_last(decays, ones, precision=lax.Precision.HIGHEST) * log2e
    cum_col = jnp.transpose(cum_row)
    steps = step[0]
    scores = dot_last(reads[0], writes[0])
    scores = jnp.where(causal, scores, 0.0)
    quad = 4 * HEAD_DIM
    lane = lax.broadcasted_iota(jnp.int32, (BLOCK, quad), 1)
    for start in range(0, heads, 4):
        columns = inputs[0][:, start * HEAD_DIM : start * HEAD_DIM + quad]
        total = skip[:, start * HEAD_DIM : start * HEAD_DIM + quad] * columns.astype(F32)
        for offset in range(4):
            head = start + offset
            gap = jnp.minimum(cum_col[:, head : head + 1] - cum_row[head : head + 1, :], 0.0)
            weights = (jnp.exp2(gap) * steps[head : head + 1, :] * scores).astype(BF16)
            own = (lane >= offset * HEAD_DIM) & (lane < (offset + 1) * HEAD_DIM)
            total = total + jnp.dot(
                weights,
                jnp.where(own, columns, jnp.zeros_like(columns)),
                preferred_element_type=F32,
            )
        within[0, :, start * HEAD_DIM : start * HEAD_DIM + quad] = total


def within_call(which, decays, steps, inputs, writes, reads, skip):
    seqs, heads, length = decays.shape
    width = inputs.shape[2]
    return pl.pallas_call(
        within_kernel,
        grid=(length // BLOCK,),
        in_specs=[
            pl.BlockSpec((1, heads, BLOCK), lambda c: (which, 0, c)),
            pl.BlockSpec((1, heads, BLOCK), lambda c: (which, 0, c)),
            pl.BlockSpec((1, BLOCK, width), lambda c: (which, c, 0)),
            pl.BlockSpec((1, BLOCK, STATE), lambda c: (which, c, 0)),
            pl.BlockSpec((1, BLOCK, STATE), lambda c: (which, c, 0)),
            pl.BlockSpec((1, width), lambda c: (0, 0)),
        ],
        out_specs=pl.BlockSpec((1, BLOCK, width), lambda c: (0, c, 0)),
        out_shape=jax.ShapeDtypeStruct((1, length, width), F32),
        compiler_params=pltpu.CompilerParams(
            dimension_semantics=("arbitrary",), vmem_limit_bytes=16 * 2**20
        ),
        cost_estimate=pl.CostEstimate(
            flops=3 * 10**9, bytes_accessed=2 * 2**20, transcendentals=2**20
        ),
        name="within",
    )(decays, steps, inputs, writes, reads, skip)


def scan_kernel(parcels, states):
    ranks = parcels.shape[0]
    state = jnp.zeros((HEAD_DIM, STATE), F32)
    for rank in range(ranks):
        states[rank] = state.astype(BF16)
        if rank < ranks - 1:
            extra = parcels[rank, HEAD_DIM:, :].astype(F32)
            factor = extra[0:1] + extra[1:2] + extra[2:3]
            state = factor * state + parcels[rank, :HEAD_DIM, :].astype(F32)


def scan_call(parcels):
    ranks = parcels.shape[0]
    return pl.pallas_call(
        scan_kernel,
        out_shape=jax.ShapeDtypeStruct((ranks, HEAD_DIM, STATE), BF16),
        cost_estimate=pl.CostEstimate(flops=10**6, bytes_accessed=2**19, transcendentals=0),
        name="scan",
    )(parcels)


def mixer_kernel(
    place, decay, reads, entering, first, within, gate, gain, weight, kept, passed, held, sems
):
    block = pl.program_id(0)
    blocks = pl.num_programs(0)
    heads = decay.shape[1]
    width = gate.shape[2]
    chips, keep = kept.shape[0], kept.shape[1]
    ones = triangle().astype(F32)
    decays = decay[0]
    before = block > 0
    cum_row = dot_last(decays[:, BLOCK:], ones, precision=lax.Precision.HIGHEST)
    head_row = dot_last(decays[:, :BLOCK], ones, precision=lax.Precision.HIGHEST)
    prefix = jnp.exp(jnp.broadcast_to(head_row[:, BLOCK - 1 :], (heads, STATE)))
    arrived = entering[...].astype(F32).reshape(width, STATE)
    begin = jnp.where(before, over_rows(prefix) * arrived + first[0], arrived)
    cum = jnp.transpose(jnp.exp(jnp.where(before, cum_row, head_row)))
    high, low = two_parts(begin)
    vectors = reads[0]
    readout = dot_last(vectors, high) + dot_last(vectors, low)
    ssd_out = within[0] + spread_heads(cum, heads) * readout
    gates = gate[0].astype(F32)
    gated = ssd_out * (gates / (1.0 + jnp.exp(-gates)))
    factor = lax.rsqrt(jnp.mean(gated * gated, axis=-1, keepdims=True) + 1e-05)
    normed = (gated * factor * gain[...]).astype(BF16)
    product = jnp.dot(normed, weight[...], preferred_element_type=F32).astype(BF16)
    held[block] = product.reshape(held.shape[1], keep, D)
    pieces = held.shape[1]
    chip, core = lax.div(place[0], 2), lax.rem(place[0], 2)

    def piece(step, index, target):
        distance = lax.rem(step * (pieces // 2) + index // 2 - chip + chips, chips)
        return pltpu.make_async_copy(
            held.at[step, index], target.at[distance], sems.at[step, index]
        )

    for index in range(pieces):

        @pl.when(core == index % 2)
        def _():
            piece(block, index, kept).start()

        @pl.when(core != index % 2)
        def _():
            piece(block, index, passed).start()

    @pl.when(block == blocks - 1)
    def _():
        for step in range(held.shape[0]):
            for index in range(pieces):
                piece(step, index, kept).wait()


def mixer_call(which, place, decays, reads, entering, first, within, gate, gain, weight, columns):
    seqs, heads, length = decays.shape
    width = gate.shape[2]
    blocks = length // BLOCK
    keep = length // columns
    anywhere = pl.BlockSpec(memory_space=pl.ANY)
    return pl.pallas_call(
        mixer_kernel,
        grid=(blocks,),
        in_specs=[
            pl.BlockSpec(memory_space=pltpu.SMEM),
            pl.BlockSpec((1, heads, length), lambda c: (which, 0, 0)),
            pl.BlockSpec((1, BLOCK, STATE), lambda c: (which, c, 0)),
            pl.BlockSpec((heads, HEAD_DIM, STATE), lambda c: (which, 0, 0)),
            pl.BlockSpec((1, width, STATE), lambda c: (which, 0, 0)),
            pl.BlockSpec((1, BLOCK, width), lambda c: (0, c, 0)),
            pl.BlockSpec((1, BLOCK, width), lambda c: (which, c, 0)),
            pl.BlockSpec((1, width), lambda c: (0, 0)),
            pl.BlockSpec((width, D), lambda c: (0, 0)),
        ],
        out_specs=[anywhere, anywhere],
        out_shape=[jax.ShapeDtypeStruct((columns // 2, keep, D), BF16)] * 2,
        scratch_shapes=[
            pltpu.VMEM((blocks, columns // blocks, keep, D), BF16),
            pltpu.SemaphoreType.DMA((blocks, columns // blocks)),
        ],
        compiler_params=pltpu.CompilerParams(
            dimension_semantics=("arbitrary",), vmem_limit_bytes=16 * 2**20
        ),
        cost_estimate=pl.CostEstimate(
            flops=2 * 10**9, bytes_accessed=6 * 2**20, transcendentals=2**18
        ),
        name="mixer",
    )(place, decays, reads, entering, first, within, gate, gain, weight)


def unfold(rows, folded):
    pieces = [folded[pl.ds(part, rows, stride=FOLD), :].astype(BF16) for part in range(FOLD)]
    return jnp.concatenate(pieces, axis=1)


def fold(values, folded):
    rows = values.shape[0]
    for part in range(FOLD):
        folded[pl.ds(part, rows, stride=FOLD), :] = values[:, part * 128 : (part + 1) * 128]


def dispatch_kernel(
    residual, gain, places, own_top, got_top, own_bottom, got_bottom, *refs
):
    others = refs[:4]
    hidden, packed, folded = refs[4:]
    half = own_top.shape[1]
    for index, (own, got) in enumerate(((own_top, got_top), (own_bottom, got_bottom))):
        span = pl.ds(index * half, half)
        hidden[span, :] = (
            residual[span, :].astype(F32)
            + (own[0].astype(F32) + got[0].astype(F32))
            + others[2 * index][...].astype(F32)
            + others[2 * index + 1][...].astype(F32)
        )
    state = hidden[...]
    scale = lax.rsqrt(jnp.mean(state * state, axis=-1, keepdims=True) + 1e-05)
    moe_in = (state * scale * gain[...]).astype(BF16)
    rows = packed.shape[0]
    slot = lax.broadcasted_iota(jnp.int32, (rows + rows // FOLD, state.shape[0]), 0)
    chosen = (slot == places[0:1, :]) | (slot == places[1:2, :])
    select = jnp.where(chosen, 1.0, 0.0).astype(BF16)
    slots = jnp.dot(select, moe_in, preferred_element_type=F32)
    packed[:, :D] = slots[:rows].astype(BF16)
    fold(slots[rows:], folded)
    packed[:, D:] = folded[...].astype(BF16)


def dispatch_call(residual, gain, places, owns, others, experts):
    rows, half = residual.shape[0], residual.shape[0] // 2
    count = experts * FOLD
    whole = lambda shape: pl.BlockSpec(shape, lambda i: (0,) * len(shape))
    return pl.pallas_call(
        dispatch_kernel,
        grid=(1,),
        in_specs=[whole(residual.shape), whole(gain.shape), whole(places.shape)]
        + [whole((1, half, D))] * 4
        + [whole((half, D))] * 4,
        out_specs=[whole((rows, D)), whole((count, D + 128))],
        out_shape=[
            jax.ShapeDtypeStruct((rows, D), F32),
            jax.ShapeDtypeStruct((count, D + 128), BF16),
        ],
        scratch_shapes=[pltpu.VMEM((count, 128), F32)],
        compiler_params=pltpu.CompilerParams(vmem_limit_bytes=24 * 2**20),
        cost_estimate=pl.CostEstimate(
            flops=2 * 10**8, bytes_accessed=5 * 2**20, transcendentals=0
        ),
        name="dispatch",
    )(residual, gain, places, *owns, *others)


def combine_kernel(returned, places, gates, hidden, directions, out, folded, values):
    slots, rows = values.shape[0], hidden.shape[0]
    count = returned.shape[0]
    folded[...] = returned[:, D:].astype(F32)
    values[:count, :] = returned[:, :D]
    values[count:, :] = unfold(slots - count, folded)
    slot = lax.broadcasted_iota(jnp.int32, (rows, slots), 1)
    zero = jnp.zeros((rows, slots), F32)
    mix = jnp.where(slot == places[:, 0:1], gates[:, 0:1], zero) + jnp.where(
        slot == places[:, 1:2], gates[:, 1:2], zero
    )
    high, rest = two_parts(mix)
    middle, low = two_parts(mix - high.astype(F32))
    parts = jnp.concatenate([high, middle, low], axis=0)
    product = jnp.dot(parts, values[...], preferred_element_type=F32)
    combined = hidden[...] + (
        product[:rows] + product[rows : 2 * rows] + product[2 * rows :]
    )
    for index in range(directions.shape[0]):
        direction = directions[index : index + 1, :]
        norm = jnp.sum(direction * direction, axis=1, keepdims=True) + 1e-06
        along = jnp.sum(combined * direction, axis=1, keepdims=True) / norm
        combined = combined - along * direction
    out[...] = combined.astype(BF16)


def combine_call(returned, places, gates, hidden, directions):
    rows = hidden.shape[0]
    count = returned.shape[0]
    return pl.pallas_call(
        combine_kernel,
        out_shape=jax.ShapeDtypeStruct((rows, D), BF16),
        scratch_shapes=[
            pltpu.VMEM((count, 128), F32),
            pltpu.VMEM((count + count // FOLD, D), BF16),
        ],
        compiler_params=pltpu.CompilerParams(vmem_limit_bytes=24 * 2**20),
        cost_estimate=pl.CostEstimate(flops=10**9, bytes_accessed=4 * 2**20, transcendentals=0),
        name="combine",
    )(returned, places, gates, hidden, directions)


def expert_kernel(counts, *refs):
    number = len(counts)
    parts = refs[:number]
    gate, up, down, kept, passed = refs[number : number + 5]
    values, extra, folded, hidden, tail, main_sems, extra_sems = refs[number + 5 :]
    places = [sum(counts[:index]) for index in range(number)]
    count = sum(counts)
    lone = count // FOLD
    loads, extras = [], []
    for index, (part, place, size) in enumerate(zip(parts, places, counts)):
        span = pl.ds(place, size)
        extras.append(
            pltpu.make_async_copy(
                part.at[:, pl.ds(D, 128)], extra.at[span, :], extra_sems.at[index]
            )
        )
        loads.append(
            pltpu.make_async_copy(
                part.at[:, pl.ds(0, D)], values.at[span, :], main_sems.at[index]
            )
        )
    for load in extras + loads:
        load.start()
    for load in extras:
        load.wait()
    folded[...] = extra[...].astype(F32)
    values[count:, :] = unfold(lone, folded)
    for load in loads:
        load.wait()
    units = down.shape[0]
    whole = units // 256 * 256

    def open_units(start, size):
        span = pl.ds(start, size)
        first = jnp.dot(values[...], gate[:, span], preferred_element_type=F32)
        second = jnp.dot(values[...], up[:, span], preferred_element_type=F32)
        hidden[:, span] = (first / (1.0 + jnp.exp(-first)) * second).astype(BF16)

    @pl.loop(0, whole // 256)
    def _(index):
        open_units(pl.multiple_of(index * 256, 256), 256)

    if units > whole:
        open_units(whole, units - whole)
    half = kept.shape[0]

    @pl.loop(0, D // 1024)
    def _(index):
        span = pl.ds(pl.multiple_of(index * 1024, 1024), 1024)
        result = jnp.dot(hidden[...], down[:, span], preferred_element_type=F32)
        kept[:, span] = result[:half].astype(BF16)
        passed[:, span] = result[half:count].astype(BF16)
        tail[:, span] = result[count:]

    fold(tail[...], folded)
    kept[:, D:] = folded[:half, :].astype(BF16)
    passed[:, D:] = folded[half:, :].astype(BF16)


def expert_call(parts, gate, up, down):
    counts = tuple(part.shape[0] for part in parts)
    count = sum(counts)
    rows = count + count // FOLD
    units = down.shape[0]
    anywhere = pl.BlockSpec(memory_space=pl.ANY)
    near = pl.BlockSpec(memory_space=pltpu.VMEM)
    return pl.pallas_call(
        functools.partial(expert_kernel, counts),
        in_specs=[anywhere] * len(parts) + [near] * 3,
        out_specs=[near, near],
        out_shape=[jax.ShapeDtypeStruct((count // 2, D + 128), BF16)] * 2,
        scratch_shapes=[
            pltpu.VMEM((rows, D), BF16),
            pltpu.VMEM((count, 128), BF16),
            pltpu.VMEM((count, 128), F32),
            pltpu.VMEM((rows, units), BF16),
            pltpu.VMEM((count // FOLD, D), F32),
            pltpu.SemaphoreType.DMA((len(parts),)),
            pltpu.SemaphoreType.DMA((len(parts),)),
        ],
        compiler_params=pltpu.CompilerParams(vmem_limit_bytes=24 * 2**20),
        cost_estimate=pl.CostEstimate(
            flops=6 * rows * D * units,
            bytes_accessed=4 * rows * D + 6 * D * units,
            transcendentals=rows * units,
        ),
        name="expert",
    )(*parts, gate, up, down)


def settle_kernel(kept, got, top_after, top_before, bottom_before, bottom_after, out):
    half = top_after.shape[0]
    for index, others in enumerate(((top_after, top_before), (bottom_before, bottom_after))):
        span = pl.ds(index * half, half)
        total = kept[span, :].astype(F32) + got[span, :].astype(F32)
        for other in others:
            total = total + other[...].astype(F32)
        out[span, :] = total.astype(BF16)


def settle_call(*arrays):
    return pl.pallas_call(
        settle_kernel,
        out_shape=jax.ShapeDtypeStruct(arrays[0].shape, BF16),
        compiler_params=pltpu.CompilerParams(vmem_limit_bytes=16 * 2**20),
        cost_estimate=pl.CostEstimate(flops=2 * 10**6, bytes_accessed=5 * 2**20, transcendentals=0),
        name="settle",
    )(*arrays)


def from_before(values):
    size = lax.axis_size("exp")
    return lax.ppermute(values, "exp", [(i, (i + 2) % size) for i in range(size)])


def from_after(values):
    size = lax.axis_size("exp")
    return lax.ppermute(values, "exp", [(i, (i - 2) % size) for i in range(size)])


def from_sibling(values):
    size = lax.axis_size("exp")
    return lax.ppermute(values, "exp", [(i, i ^ 1) for i in range(size)])


def add_up(*terms):
    total = terms[0].astype(F32)
    for term in terms[1:]:
        total = total + term.astype(F32)
    return total.astype(BF16)


def after(values, *earlier):
    return lax.optimization_barrier((tuple(values), earlier))[0]


def expert_layer(own, gate, up, down):
    half = own.shape[0] // 2
    top, bottom = own[:half], own[half:]
    own_other = from_sibling(own)
    before_top = from_before(top)
    after_bottom = from_after(bottom)
    call = functools.partial(expert_call, gate=gate, up=up, down=down)
    kept_own, passed = call((own, own_other))
    before_top, after_bottom, kept_own, passed, top, bottom = after(
        (before_top, after_bottom, kept_own, passed, top, bottom)
    )
    got_own = from_sibling(passed)
    others = from_sibling(before_top), from_sibling(after_bottom)
    far_top = from_before(before_top)
    far_bottom = from_after(after_bottom)
    before_bottom = from_before(bottom)
    after_top = from_after(top)
    kept, passed = call((before_top, after_bottom, *others))
    far_top, far_bottom, got_own, kept, passed = after(
        (far_top, far_bottom, got_own, kept, passed)
    )
    got = from_sibling(passed)
    others = from_sibling(far_top), from_sibling(far_bottom)
    near_top, near_bottom = add_up(kept[:half], got[:half]), add_up(kept[half:], got[half:])
    near_top, near_bottom, far_top, far_bottom = after(
        (near_top, near_bottom, far_top, far_bottom)
    )
    top_after = from_after(near_top)
    bottom_before = from_before(near_bottom)
    kept, passed = call((far_top, far_bottom, *others))
    after_top, before_bottom, kept, passed = after((after_top, before_bottom, kept, passed))
    late = from_sibling(after_top), from_sibling(before_bottom)
    got = from_sibling(passed)
    far_top, far_bottom = add_up(kept[:half], got[:half]), add_up(kept[half:], got[half:])
    far_top, far_bottom, after_top, before_bottom = after(
        (far_top, far_bottom, after_top, before_bottom)
    )
    relay_top = from_before(far_top)
    relay_bottom = from_after(far_bottom)
    kept, passed = call((after_top, before_bottom, *late))
    relay_top, relay_bottom, kept, passed = after((relay_top, relay_bottom, kept, passed))
    got = from_sibling(passed)
    top_before = from_before(add_up(kept[:half], got[:half], relay_top))
    bottom_after = from_after(add_up(kept[half:], got[half:], relay_bottom))
    return settle_call(
        kept_own, got_own, top_after, top_before, bottom_before, bottom_after
    )


def on_device(
    ssd_input,
    ssd_gate,
    state_write,
    state_read,
    step_size,
    decay_log,
    skip_gain,
    norm_gain,
    w_out,
    resid,
    moe_gain,
    w_gate,
    w_up,
    w_down,
    routes,
    gates,
    directions,
):
    length_dev, seqs, width_dev = ssd_input.shape
    heads_dev = decay_log.shape[0]
    experts = lax.axis_size("seq")
    columns = lax.axis_size("exp")
    rows_keep = length_dev * seqs // columns

    def swap(values):
        return jnp.transpose(values, (1, 0, 2))

    decays, steps = swap(decay_log), swap(step_size)
    inputs, writes, reads = swap(ssd_input), swap(state_write), swap(state_read)
    parcel, first = contrib_call(decays, steps, inputs, writes)
    parcels = lax.all_to_all(parcel, "seq", split_axis=0, concat_axis=0, tiled=True)
    skip = jnp.repeat(skip_gain, HEAD_DIM)[None, :]
    within_early = within_call(0, decays, steps, inputs, writes, reads, skip)
    (parcels,) = after((parcels,), within_early)
    entering = lax.all_to_all(
        scan_call(parcels), "seq", split_axis=0, concat_axis=0, tiled=True
    )
    within_late = within_call(1, decays, steps, inputs, writes, reads, skip)
    gating = swap(ssd_gate)
    (entering,) = after((entering,), within_late, gating)
    place = lax.axis_index("exp").astype(jnp.int32)[None]
    shared = (decays, reads, entering, first)
    kept, passed = mixer_call(
        0, place, *shared, within_early, gating, norm_gain[None, :], w_out, columns
    )
    got = from_sibling(passed)
    (place,) = after((place,), kept)
    kept_late, passed = mixer_call(
        1, place, *shared, within_late, gating, norm_gain[None, :], w_out, columns
    )
    got_late = from_sibling(passed)
    relay_top = from_before(add_up(kept[2], got[2]))
    top_after = from_after(add_up(kept[3], got[3]))
    relay_bottom = from_after(add_up(kept_late[2], got_late[2]))
    bottom_before = from_before(add_up(kept_late[1], got_late[1]))
    top_before = from_before(add_up(kept[1], got[1], relay_top))
    bottom_after = from_after(add_up(kept_late[3], got_late[3], relay_bottom))
    capacity = max(2, 2 * rows_keep * 17 // (16 * experts))
    assert capacity == FOLD + 1
    picks = swap(routes).reshape(-1)
    onehot = (picks[:, None] == jnp.arange(experts, dtype=jnp.int32)[None, :]).astype(jnp.int32)
    before = jnp.cumsum(onehot, axis=0) - onehot
    ranked = jnp.sum(before * onehot, axis=1)
    places = jnp.where(
        ranked < FOLD, picks * FOLD + ranked, experts * FOLD + picks
    ).reshape(rows_keep, 2)
    hidden_state, packed = dispatch_call(
        swap(resid).reshape(rows_keep, D),
        moe_gain[None, :],
        places.T,
        (kept, got, kept_late, got_late),
        (top_after, top_before, bottom_before, bottom_after),
        experts,
    )
    arrived = lax.all_to_all(
        packed.reshape(experts, FOLD, D + 128), "seq", split_axis=0, concat_axis=0, tiled=True
    )
    summed = expert_layer(arrived.reshape(packed.shape), w_gate[0], w_up[0], w_down[0])
    returned = lax.all_to_all(
        summed.reshape(experts, FOLD, D + 128), "seq", split_axis=0, concat_axis=0, tiled=True
    )
    combined = combine_call(
        returned.reshape(packed.shape),
        places,
        swap(gates).reshape(rows_keep, 2),
        hidden_state,
        directions,
    )
    return swap(combined.reshape(seqs, length_dev // columns, D))


def solution(mesh):
    in_specs = (
        P("seq", None, "exp"),
        P("seq", None, "exp"),
        P("seq", None, "exp"),
        P("seq", None, "exp"),
        P("exp", None, "seq"),
        P("exp", None, "seq"),
        P("exp"),
        P("exp"),
        P("exp", None),
        P(("seq", "exp"), None, None),
        P(),
        P("seq", None, "exp"),
        P("seq", None, "exp"),
        P("seq", "exp", None),
        P(("seq", "exp"), None, None),
        P(("seq", "exp"), None, None),
        P(),
    )
    out_specs = P(("seq", "exp"), None, None)
    return jax.shard_map(
        on_device, mesh=mesh, in_specs=in_specs, out_specs=out_specs, check_vma=False
    )
```

```python
import functools

import jax
import jax.numpy as jnp
from jax import lax
from jax.experimental import pallas as pl
from jax.experimental.pallas import tpu as pltpu
from jax.sharding import PartitionSpec as P

D = 2048
HEADS = 64
HEAD_DIM = 64
STATE = 128
GROUPS = 8
BLOCK = 256
FOLD = 16
F32 = jnp.float32
BF16 = jnp.bfloat16


def dot_last(left, right, **options):
    return lax.dot_general(
        left, right, (((1,), (1,)), ((), ())), preferred_element_type=F32, **options
    )


def two_parts(values):
    high = values.astype(BF16)
    return high, (values - high.astype(F32)).astype(BF16)


def triangle():
    row = lax.broadcasted_iota(jnp.int32, (BLOCK, BLOCK), 0)
    col = lax.broadcasted_iota(jnp.int32, (BLOCK, BLOCK), 1)
    return row >= col


def spread_heads(columns, heads):
    rows = columns.shape[0]
    lane = lax.broadcasted_iota(jnp.int32, (rows, 2 * HEAD_DIM), 1)
    pieces = []
    for head in range(0, heads, 2):
        left = jnp.broadcast_to(columns[:, head : head + 1], (rows, 2 * HEAD_DIM))
        right = jnp.broadcast_to(columns[:, head + 1 : head + 2], (rows, 2 * HEAD_DIM))
        pieces.append(jnp.where(lane < HEAD_DIM, left, right))
    return jnp.concatenate(pieces, axis=1)


def over_rows(values):
    heads = values.shape[0]
    return jnp.broadcast_to(values[:, None, :], (heads, HEAD_DIM, STATE)).reshape(
        heads * HEAD_DIM, STATE
    )


def contrib_kernel(decay, step, inputs, writes, parcel, first, total, running):
    block = pl.program_id(1)
    heads = decay.shape[1]
    ones = triangle().astype(F32)
    decays = decay[0]
    cum_row = dot_last(decays, ones, precision=lax.Precision.HIGHEST)
    end_row = jnp.broadcast_to(cum_row[:, BLOCK - 1 :], (heads, STATE))
    to_end_row = jnp.exp(cum_row[:, BLOCK - 1 :] - cum_row) * step[0]
    to_end = jnp.transpose(to_end_row)
    scaled = (inputs[0].astype(F32) * spread_heads(to_end, heads)).astype(BF16)
    contrib = lax.dot_general(
        scaled, writes[0], (((0,), (0,)), ((), ())), preferred_element_type=F32
    )

    @pl.when(block == 0)
    def _():
        first[0] = contrib
        running[...] = contrib
        total[...] = end_row

    @pl.when(block > 0)
    def _():
        running[...] = over_rows(jnp.exp(end_row)) * running[...] + contrib
        total[...] = total[...] + end_row

    @pl.when(block == pl.num_programs(1) - 1)
    def _():
        carried = jnp.exp(total[...])
        high, rest = two_parts(carried)
        middle, low = two_parts(carried - high.astype(F32))
        row = lax.broadcasted_iota(jnp.int32, (heads, 8, STATE), 1)
        wide = lambda part: jnp.broadcast_to(part.astype(F32)[:, None, :], (heads, 8, STATE))
        extra = jnp.where(
            row == 0,
            wide(high),
            jnp.where(row == 1, wide(middle), jnp.where(row == 2, wide(low), 0.0)),
        )
        parcel[:, :HEAD_DIM, :] = running[...].reshape(heads, HEAD_DIM, STATE).astype(BF16)
        parcel[:, HEAD_DIM:, :] = extra.astype(BF16)


def contrib_call(decays, steps, inputs, writes):
    seqs, heads, length = decays.shape
    width = inputs.shape[2]
    blocks = length // BLOCK
    return pl.pallas_call(
        contrib_kernel,
        grid=(seqs, blocks),
        in_specs=[
            pl.BlockSpec((1, heads, BLOCK), lambda b, c: (b, 0, c)),
            pl.BlockSpec((1, heads, BLOCK), lambda b, c: (b, 0, c)),
            pl.BlockSpec((1, BLOCK, width), lambda b, c: (b, c, 0)),
            pl.BlockSpec((1, BLOCK, STATE), lambda b, c: (b, c, 0)),
        ],
        out_specs=[
            pl.BlockSpec((heads, HEAD_DIM + 8, STATE), lambda b, c: (b, 0, 0)),
            pl.BlockSpec((1, width, STATE), lambda b, c: (b, 0, 0)),
        ],
        out_shape=[
            jax.ShapeDtypeStruct((seqs * heads, HEAD_DIM + 8, STATE), BF16),
            jax.ShapeDtypeStruct((seqs, width, STATE), F32),
        ],
        scratch_shapes=[pltpu.VMEM((heads, STATE), F32), pltpu.VMEM((width, STATE), F32)],
        compiler_params=pltpu.CompilerParams(
            dimension_semantics=("arbitrary", "arbitrary"), vmem_limit_bytes=16 * 2**20
        ),
        cost_estimate=pl.CostEstimate(flops=10**9, bytes_accessed=2 * 2**20, transcendentals=8192),
        name="contrib",
    )(decays, steps, inputs, writes)


def within_kernel(decay, step, inputs, writes, reads, skip, within):
    heads = decay.shape[1]
    causal = triangle()
    ones = causal.astype(F32)
    log2e = 1.4426950408889634
    decays = decay[0]
    cum_row = dot_last(decays, ones, precision=lax.Precision.HIGHEST) * log2e
    cum_col = jnp.transpose(cum_row)
    steps = step[0]
    scores = dot_last(reads[0], writes[0])
    scores = jnp.where(causal, scores, 0.0)
    quad = 4 * HEAD_DIM
    lane = lax.broadcasted_iota(jnp.int32, (BLOCK, quad), 1)
    for start in range(0, heads, 4):
        columns = inputs[0][:, start * HEAD_DIM : start * HEAD_DIM + quad]
        total = skip[:, start * HEAD_DIM : start * HEAD_DIM + quad] * columns.astype(F32)
        for offset in range(4):
            head = start + offset
            gap = jnp.minimum(cum_col[:, head : head + 1] - cum_row[head : head + 1, :], 0.0)
            weights = (jnp.exp2(gap) * steps[head : head + 1, :] * scores).astype(BF16)
            own = (lane >= offset * HEAD_DIM) & (lane < (offset + 1) * HEAD_DIM)
            total = total + jnp.dot(
                weights,
                jnp.where(own, columns, jnp.zeros_like(columns)),
                preferred_element_type=F32,
            )
        within[0, :, start * HEAD_DIM : start * HEAD_DIM + quad] = total


def within_call(which, decays, steps, inputs, writes, reads, skip):
    seqs, heads, length = decays.shape
    width = inputs.shape[2]
    return pl.pallas_call(
        within_kernel,
        grid=(length // BLOCK,),
        in_specs=[
            pl.BlockSpec((1, heads, BLOCK), lambda c: (which, 0, c)),
            pl.BlockSpec((1, heads, BLOCK), lambda c: (which, 0, c)),
            pl.BlockSpec((1, BLOCK, width), lambda c: (which, c, 0)),
            pl.BlockSpec((1, BLOCK, STATE), lambda c: (which, c, 0)),
            pl.BlockSpec((1, BLOCK, STATE), lambda c: (which, c, 0)),
            pl.BlockSpec((1, width), lambda c: (0, 0)),
        ],
        out_specs=pl.BlockSpec((1, BLOCK, width), lambda c: (0, c, 0)),
        out_shape=jax.ShapeDtypeStruct((1, length, width), F32),
        compiler_params=pltpu.CompilerParams(
            dimension_semantics=("arbitrary",), vmem_limit_bytes=16 * 2**20
        ),
        cost_estimate=pl.CostEstimate(
            flops=3 * 10**9, bytes_accessed=2 * 2**20, transcendentals=2**20
        ),
        name="within",
    )(decays, steps, inputs, writes, reads, skip)


def scan_kernel(parcels, states):
    ranks = parcels.shape[0]
    state = jnp.zeros((HEAD_DIM, STATE), F32)
    for rank in range(ranks):
        states[rank] = state.astype(BF16)
        if rank < ranks - 1:
            extra = parcels[rank, HEAD_DIM:, :].astype(F32)
            factor = extra[0:1] + extra[1:2] + extra[2:3]
            state = factor * state + parcels[rank, :HEAD_DIM, :].astype(F32)


def scan_call(parcels):
    ranks = parcels.shape[0]
    return pl.pallas_call(
        scan_kernel,
        out_shape=jax.ShapeDtypeStruct((ranks, HEAD_DIM, STATE), BF16),
        cost_estimate=pl.CostEstimate(flops=10**6, bytes_accessed=2**19, transcendentals=0),
        name="scan",
    )(parcels)


def mixer_kernel(
    place, decay, reads, entering, first, within, gate, gain, weight, kept, passed, held, sems
):
    block = pl.program_id(0)
    blocks = pl.num_programs(0)
    heads = decay.shape[1]
    width = gate.shape[2]
    chips, keep = kept.shape[0], kept.shape[1]
    ones = triangle().astype(F32)
    decays = decay[0]
    before = block > 0
    cum_row = dot_last(decays[:, BLOCK:], ones, precision=lax.Precision.HIGHEST)
    head_row = dot_last(decays[:, :BLOCK], ones, precision=lax.Precision.HIGHEST)
    prefix = jnp.exp(jnp.broadcast_to(head_row[:, BLOCK - 1 :], (heads, STATE)))
    arrived = entering[...].astype(F32).reshape(width, STATE)
    begin = jnp.where(before, over_rows(prefix) * arrived + first[0], arrived)
    cum = jnp.transpose(jnp.exp(jnp.where(before, cum_row, head_row)))
    high, low = two_parts(begin)
    vectors = reads[0]
    readout = dot_last(vectors, high) + dot_last(vectors, low)
    ssd_out = within[0] + spread_heads(cum, heads) * readout
    gates = gate[0].astype(F32)
    gated = ssd_out * (gates / (1.0 + jnp.exp(-gates)))
    factor = lax.rsqrt(jnp.mean(gated * gated, axis=-1, keepdims=True) + 1e-05)
    normed = (gated * factor * gain[...]).astype(BF16)
    product = jnp.dot(normed, weight[...], preferred_element_type=F32).astype(BF16)
    held[block] = product.reshape(held.shape[1], keep, D)
    pieces = held.shape[1]
    chip, core = lax.div(place[0], 2), lax.rem(place[0], 2)

    def piece(step, index, target):
        distance = lax.rem(step * (pieces // 2) + index // 2 - chip + chips, chips)
        return pltpu.make_async_copy(
            held.at[step, index], target.at[distance], sems.at[step, index]
        )

    for index in range(pieces):

        @pl.when(core == index % 2)
        def _():
            piece(block, index, kept).start()

        @pl.when(core != index % 2)
        def _():
            piece(block, index, passed).start()

    @pl.when(block == blocks - 1)
    def _():
        for step in range(held.shape[0]):
            for index in range(pieces):
                piece(step, index, kept).wait()


def mixer_call(which, place, decays, reads, entering, first, within, gate, gain, weight, columns):
    seqs, heads, length = decays.shape
    width = gate.shape[2]
    blocks = length // BLOCK
    keep = length // columns
    anywhere = pl.BlockSpec(memory_space=pl.ANY)
    return pl.pallas_call(
        mixer_kernel,
        grid=(blocks,),
        in_specs=[
            pl.BlockSpec(memory_space=pltpu.SMEM),
            pl.BlockSpec((1, heads, length), lambda c: (which, 0, 0)),
            pl.BlockSpec((1, BLOCK, STATE), lambda c: (which, c, 0)),
            pl.BlockSpec((heads, HEAD_DIM, STATE), lambda c: (which, 0, 0)),
            pl.BlockSpec((1, width, STATE), lambda c: (which, 0, 0)),
            pl.BlockSpec((1, BLOCK, width), lambda c: (0, c, 0)),
            pl.BlockSpec((1, BLOCK, width), lambda c: (which, c, 0)),
            pl.BlockSpec((1, width), lambda c: (0, 0)),
            pl.BlockSpec((width, D), lambda c: (0, 0)),
        ],
        out_specs=[anywhere, anywhere],
        out_shape=[jax.ShapeDtypeStruct((columns // 2, keep, D), BF16)] * 2,
        scratch_shapes=[
            pltpu.VMEM((blocks, columns // blocks, keep, D), BF16),
            pltpu.SemaphoreType.DMA((blocks, columns // blocks)),
        ],
        compiler_params=pltpu.CompilerParams(
            dimension_semantics=("arbitrary",), vmem_limit_bytes=48 * 2**20
        ),
        cost_estimate=pl.CostEstimate(
            flops=2 * 10**9, bytes_accessed=6 * 2**20, transcendentals=2**18
        ),
        name="mixer",
    )(place, decays, reads, entering, first, within, gate, gain, weight)


def unfold(rows, folded):
    pieces = [folded[pl.ds(part, rows, stride=FOLD), :].astype(BF16) for part in range(FOLD)]
    return jnp.concatenate(pieces, axis=1)


def fold(values, folded):
    rows = values.shape[0]
    for part in range(FOLD):
        folded[pl.ds(part, rows, stride=FOLD), :] = values[:, part * 128 : (part + 1) * 128]


def dispatch_kernel(
    residual, gain, places, own_top, got_top, own_bottom, got_bottom, *refs
):
    others = refs[:4]
    hidden, packed, folded = refs[4:]
    half = own_top.shape[1]
    for index, (own, got) in enumerate(((own_top, got_top), (own_bottom, got_bottom))):
        span = pl.ds(index * half, half)
        hidden[span, :] = (
            residual[span, :].astype(F32)
            + (own[0].astype(F32) + got[0].astype(F32))
            + others[2 * index][...].astype(F32)
            + others[2 * index + 1][...].astype(F32)
        )
    state = hidden[...]
    scale = lax.rsqrt(jnp.mean(state * state, axis=-1, keepdims=True) + 1e-05)
    moe_in = (state * scale * gain[...]).astype(BF16)
    rows = packed.shape[0]
    slot = lax.broadcasted_iota(jnp.int32, (rows + rows // FOLD, state.shape[0]), 0)
    chosen = (slot == places[0:1, :]) | (slot == places[1:2, :])
    select = jnp.where(chosen, 1.0, 0.0).astype(BF16)
    slots = jnp.dot(select, moe_in, preferred_element_type=F32)
    packed[:, :D] = slots[:rows].astype(BF16)
    fold(slots[rows:], folded)
    packed[:, D:] = folded[...].astype(BF16)


def dispatch_call(residual, gain, places, owns, others, experts):
    rows, half = residual.shape[0], residual.shape[0] // 2
    count = experts * FOLD
    whole = lambda shape: pl.BlockSpec(shape, lambda i: (0,) * len(shape))
    return pl.pallas_call(
        dispatch_kernel,
        grid=(1,),
        in_specs=[whole(residual.shape), whole(gain.shape), whole(places.shape)]
        + [whole((1, half, D))] * 4
        + [whole((half, D))] * 4,
        out_specs=[whole((rows, D)), whole((count, D + 128))],
        out_shape=[
            jax.ShapeDtypeStruct((rows, D), F32),
            jax.ShapeDtypeStruct((count, D + 128), BF16),
        ],
        scratch_shapes=[pltpu.VMEM((count, 128), F32)],
        compiler_params=pltpu.CompilerParams(vmem_limit_bytes=24 * 2**20),
        cost_estimate=pl.CostEstimate(
            flops=2 * 10**8, bytes_accessed=5 * 2**20, transcendentals=0
        ),
        name="dispatch",
    )(residual, gain, places, *owns, *others)


def combine_kernel(returned, places, gates, hidden, directions, out, folded, values):
    slots, rows = values.shape[0], hidden.shape[0]
    count = returned.shape[0]
    folded[...] = returned[:, D:].astype(F32)
    values[:count, :] = returned[:, :D]
    values[count:, :] = unfold(slots - count, folded)
    slot = lax.broadcasted_iota(jnp.int32, (rows, slots), 1)
    zero = jnp.zeros((rows, slots), F32)
    mix = jnp.where(slot == places[:, 0:1], gates[:, 0:1], zero) + jnp.where(
        slot == places[:, 1:2], gates[:, 1:2], zero
    )
    high, rest = two_parts(mix)
    middle, low = two_parts(mix - high.astype(F32))
    parts = jnp.concatenate([high, middle, low], axis=0)
    product = jnp.dot(parts, values[...], preferred_element_type=F32)
    combined = hidden[...] + (
        product[:rows] + product[rows : 2 * rows] + product[2 * rows :]
    )
    for index in range(directions.shape[0]):
        direction = directions[index : index + 1, :]
        norm = jnp.sum(direction * direction, axis=1, keepdims=True) + 1e-06
        along = jnp.sum(combined * direction, axis=1, keepdims=True) / norm
        combined = combined - along * direction
    out[...] = combined.astype(BF16)


def combine_call(returned, places, gates, hidden, directions):
    rows = hidden.shape[0]
    count = returned.shape[0]
    return pl.pallas_call(
        combine_kernel,
        out_shape=jax.ShapeDtypeStruct((rows, D), BF16),
        scratch_shapes=[
            pltpu.VMEM((count, 128), F32),
            pltpu.VMEM((count + count // FOLD, D), BF16),
        ],
        compiler_params=pltpu.CompilerParams(vmem_limit_bytes=24 * 2**20),
        cost_estimate=pl.CostEstimate(flops=10**9, bytes_accessed=4 * 2**20, transcendentals=0),
        name="combine",
    )(returned, places, gates, hidden, directions)


def expert_kernel(counts, *refs):
    number = len(counts)
    parts = refs[:number]
    gate, up, down, kept, passed = refs[number : number + 5]
    values, extra, folded, hidden, tail, main_sems, extra_sems = refs[number + 5 :]
    places = [sum(counts[:index]) for index in range(number)]
    count = sum(counts)
    lone = count // FOLD
    loads, extras = [], []
    for index, (part, place, size) in enumerate(zip(parts, places, counts)):
        span = pl.ds(place, size)
        extras.append(
            pltpu.make_async_copy(
                part.at[:, pl.ds(D, 128)], extra.at[span, :], extra_sems.at[index]
            )
        )
        loads.append(
            pltpu.make_async_copy(
                part.at[:, pl.ds(0, D)], values.at[span, :], main_sems.at[index]
            )
        )
    for load in extras + loads:
        load.start()
    for load in extras:
        load.wait()
    folded[...] = extra[...].astype(F32)
    values[count:, :] = unfold(lone, folded)
    for load in loads:
        load.wait()
    units = down.shape[0]
    whole = units // 256 * 256

    def open_units(start, size):
        span = pl.ds(start, size)
        first = jnp.dot(values[...], gate[:, span], preferred_element_type=F32)
        second = jnp.dot(values[...], up[:, span], preferred_element_type=F32)
        hidden[:, span] = (first / (1.0 + jnp.exp(-first)) * second).astype(BF16)

    @pl.loop(0, whole // 256)
    def _(index):
        open_units(pl.multiple_of(index * 256, 256), 256)

    if units > whole:
        open_units(whole, units - whole)
    half = kept.shape[0]

    @pl.loop(0, D // 1024)
    def _(index):
        span = pl.ds(pl.multiple_of(index * 1024, 1024), 1024)
        result = jnp.dot(hidden[...], down[:, span], preferred_element_type=F32)
        kept[:, span] = result[:half].astype(BF16)
        passed[:, span] = result[half:count].astype(BF16)
        tail[:, span] = result[count:]

    fold(tail[...], folded)
    kept[:, D:] = folded[:half, :].astype(BF16)
    passed[:, D:] = folded[half:, :].astype(BF16)


def expert_call(parts, gate, up, down):
    counts = tuple(part.shape[0] for part in parts)
    count = sum(counts)
    rows = count + count // FOLD
    units = down.shape[0]
    anywhere = pl.BlockSpec(memory_space=pl.ANY)
    near = pl.BlockSpec(memory_space=pltpu.VMEM)
    return pl.pallas_call(
        functools.partial(expert_kernel, counts),
        in_specs=[anywhere] * len(parts) + [near] * 3,
        out_specs=[near, near],
        out_shape=[jax.ShapeDtypeStruct((count // 2, D + 128), BF16)] * 2,
        scratch_shapes=[
            pltpu.VMEM((rows, D), BF16),
            pltpu.VMEM((count, 128), BF16),
            pltpu.VMEM((count, 128), F32),
            pltpu.VMEM((rows, units), BF16),
            pltpu.VMEM((count // FOLD, D), F32),
            pltpu.SemaphoreType.DMA((len(parts),)),
            pltpu.SemaphoreType.DMA((len(parts),)),
        ],
        compiler_params=pltpu.CompilerParams(vmem_limit_bytes=24 * 2**20),
        cost_estimate=pl.CostEstimate(
            flops=6 * rows * D * units,
            bytes_accessed=4 * rows * D + 6 * D * units,
            transcendentals=rows * units,
        ),
        name="expert",
    )(*parts, gate, up, down)


def settle_kernel(kept, got, top_after, top_before, bottom_before, bottom_after, out):
    half = top_after.shape[0]
    for index, others in enumerate(((top_after, top_before), (bottom_before, bottom_after))):
        span = pl.ds(index * half, half)
        total = kept[span, :].astype(F32) + got[span, :].astype(F32)
        for other in others:
            total = total + other[...].astype(F32)
        out[span, :] = total.astype(BF16)


def settle_call(*arrays):
    return pl.pallas_call(
        settle_kernel,
        out_shape=jax.ShapeDtypeStruct(arrays[0].shape, BF16),
        compiler_params=pltpu.CompilerParams(vmem_limit_bytes=16 * 2**20),
        cost_estimate=pl.CostEstimate(flops=2 * 10**6, bytes_accessed=5 * 2**20, transcendentals=0),
        name="settle",
    )(*arrays)


def from_before(values):
    size = lax.axis_size("exp")
    return lax.ppermute(values, "exp", [(i, (i + 2) % size) for i in range(size)])


def from_after(values):
    size = lax.axis_size("exp")
    return lax.ppermute(values, "exp", [(i, (i - 2) % size) for i in range(size)])


def from_sibling(values):
    size = lax.axis_size("exp")
    return lax.ppermute(values, "exp", [(i, i ^ 1) for i in range(size)])


def add_up(*terms):
    total = terms[0].astype(F32)
    for term in terms[1:]:
        total = total + term.astype(F32)
    return total.astype(BF16)


def after(values, *earlier):
    return lax.optimization_barrier((tuple(values), earlier))[0]


def expert_layer(own, gate, up, down):
    half = own.shape[0] // 2
    top, bottom = own[:half], own[half:]
    own_other = from_sibling(own)
    before_top = from_before(top)
    after_bottom = from_after(bottom)
    call = functools.partial(expert_call, gate=gate, up=up, down=down)
    kept_own, passed = call((own, own_other))
    before_top, after_bottom, kept_own, passed, top, bottom = after(
        (before_top, after_bottom, kept_own, passed, top, bottom)
    )
    got_own = from_sibling(passed)
    others = from_sibling(before_top), from_sibling(after_bottom)
    far_top = from_before(before_top)
    far_bottom = from_after(after_bottom)
    before_bottom = from_before(bottom)
    after_top = from_after(top)
    kept, passed = call((before_top, after_bottom, *others))
    far_top, far_bottom, got_own, kept, passed = after(
        (far_top, far_bottom, got_own, kept, passed)
    )
    got = from_sibling(passed)
    others = from_sibling(far_top), from_sibling(far_bottom)
    near_top, near_bottom = add_up(kept[:half], got[:half]), add_up(kept[half:], got[half:])
    near_top, near_bottom, far_top, far_bottom = after(
        (near_top, near_bottom, far_top, far_bottom)
    )
    top_after = from_after(near_top)
    bottom_before = from_before(near_bottom)
    kept, passed = call((far_top, far_bottom, *others))
    after_top, before_bottom, top_after, bottom_before, kept, passed = after(
        (after_top, before_bottom, top_after, bottom_before, kept, passed)
    )
    late = from_sibling(after_top), from_sibling(before_bottom)
    got = from_sibling(passed)
    far_top, far_bottom = add_up(kept[:half], got[:half]), add_up(kept[half:], got[half:])
    far_top, far_bottom, after_top, before_bottom = after(
        (far_top, far_bottom, after_top, before_bottom)
    )
    relay_top = from_before(far_top)
    relay_bottom = from_after(far_bottom)
    kept, passed = call((after_top, before_bottom, *late))
    relay_top, relay_bottom, kept, passed = after((relay_top, relay_bottom, kept, passed))
    got = from_sibling(passed)
    top_before = from_before(add_up(kept[:half], got[:half], relay_top))
    bottom_after = from_after(add_up(kept[half:], got[half:], relay_bottom))
    return settle_call(
        kept_own, got_own, top_after, top_before, bottom_before, bottom_after
    )


def on_device(
    ssd_input,
    ssd_gate,
    state_write,
    state_read,
    step_size,
    decay_log,
    skip_gain,
    norm_gain,
    w_out,
    resid,
    moe_gain,
    w_gate,
    w_up,
    w_down,
    routes,
    gates,
    directions,
):
    length_dev, seqs, width_dev = ssd_input.shape
    heads_dev = decay_log.shape[0]
    experts = lax.axis_size("seq")
    columns = lax.axis_size("exp")
    rows_keep = length_dev * seqs // columns

    def swap(values):
        return jnp.transpose(values, (1, 0, 2))

    decays, steps = swap(decay_log), swap(step_size)
    inputs, writes, reads = swap(ssd_input), swap(state_write), swap(state_read)
    parcel, first = contrib_call(decays, steps, inputs, writes)
    parcels = lax.all_to_all(parcel, "seq", split_axis=0, concat_axis=0, tiled=True)
    skip = jnp.repeat(skip_gain, HEAD_DIM)[None, :]
    within_early = within_call(0, decays, steps, inputs, writes, reads, skip)
    (parcels,) = after((parcels,), within_early)
    entering = lax.all_to_all(
        scan_call(parcels), "seq", split_axis=0, concat_axis=0, tiled=True
    )
    within_late = within_call(1, decays, steps, inputs, writes, reads, skip)
    gating = swap(ssd_gate)
    (entering,) = after((entering,), within_late, gating)
    place = lax.axis_index("exp").astype(jnp.int32)[None]
    shared = (decays, reads, entering, first)
    kept, passed = mixer_call(
        0, place, *shared, within_early, gating, norm_gain[None, :], w_out, columns
    )
    got = from_sibling(passed)
    (place,) = after((place,), kept)
    kept_late, passed = mixer_call(
        1, place, *shared, within_late, gating, norm_gain[None, :], w_out, columns
    )
    got_late = from_sibling(passed)
    relay_top = from_before(add_up(kept[2], got[2]))
    top_after = from_after(add_up(kept[3], got[3]))
    relay_bottom = from_after(add_up(kept_late[2], got_late[2]))
    bottom_before = from_before(add_up(kept_late[1], got_late[1]))
    top_before = from_before(add_up(kept[1], got[1], relay_top))
    bottom_after = from_after(add_up(kept_late[3], got_late[3], relay_bottom))
    capacity = max(2, 2 * rows_keep * 17 // (16 * experts))
    assert capacity == FOLD + 1
    picks = swap(routes).reshape(-1)
    onehot = (picks[:, None] == jnp.arange(experts, dtype=jnp.int32)[None, :]).astype(jnp.int32)
    before = jnp.cumsum(onehot, axis=0) - onehot
    ranked = jnp.sum(before * onehot, axis=1)
    places = jnp.where(
        ranked < FOLD, picks * FOLD + ranked, experts * FOLD + picks
    ).reshape(rows_keep, 2)
    hidden_state, packed = dispatch_call(
        swap(resid).reshape(rows_keep, D),
        moe_gain[None, :],
        places.T,
        (kept, got, kept_late, got_late),
        (top_after, top_before, bottom_before, bottom_after),
        experts,
    )
    arrived = lax.all_to_all(
        packed.reshape(experts, FOLD, D + 128), "seq", split_axis=0, concat_axis=0, tiled=True
    )
    summed = expert_layer(arrived.reshape(packed.shape), w_gate[0], w_up[0], w_down[0])
    returned = lax.all_to_all(
        summed.reshape(experts, FOLD, D + 128), "seq", split_axis=0, concat_axis=0, tiled=True
    )
    combined = combine_call(
        returned.reshape(packed.shape),
        places,
        swap(gates).reshape(rows_keep, 2),
        hidden_state,
        directions,
    )
    return swap(combined.reshape(seqs, length_dev // columns, D))


def solution(mesh):
    in_specs = (
        P("seq", None, "exp"),
        P("seq", None, "exp"),
        P("seq", None, "exp"),
        P("seq", None, "exp"),
        P("exp", None, "seq"),
        P("exp", None, "seq"),
        P("exp"),
        P("exp"),
        P("exp", None),
        P(("seq", "exp"), None, None),
        P(),
        P("seq", None, "exp"),
        P("seq", None, "exp"),
        P("seq", "exp", None),
        P(("seq", "exp"), None, None),
        P(("seq", "exp"), None, None),
        P(),
    )
    out_specs = P(("seq", "exp"), None, None)
    return jax.shard_map(
        on_device, mesh=mesh, in_specs=in_specs, out_specs=out_specs, check_vma=False
    )
```

```python
import functools

import jax
import jax.numpy as jnp
from jax import lax
from jax.experimental import pallas as pl
from jax.experimental.pallas import tpu as pltpu
from jax.sharding import PartitionSpec as P

D = 2048
HEADS = 64
HEAD_DIM = 64
STATE = 128
GROUPS = 8
BLOCK = 256
FOLD = 16
F32 = jnp.float32
BF16 = jnp.bfloat16


def dot_last(left, right, **options):
    return lax.dot_general(
        left, right, (((1,), (1,)), ((), ())), preferred_element_type=F32, **options
    )


def two_parts(values):
    high = values.astype(BF16)
    return high, (values - high.astype(F32)).astype(BF16)


def triangle():
    row = lax.broadcasted_iota(jnp.int32, (BLOCK, BLOCK), 0)
    col = lax.broadcasted_iota(jnp.int32, (BLOCK, BLOCK), 1)
    return row >= col


def running_sums(decays):
    heads = decays.shape[0]
    high, rest = two_parts(decays)
    middle, low = two_parts(decays - high.astype(F32))
    parts = jnp.concatenate(
        [high.astype(F32), middle.astype(F32), low.astype(F32)], axis=0
    ).astype(BF16)
    ones = jnp.where(triangle(), 1.0, 0.0).astype(BF16)
    sums = dot_last(parts, ones)
    return sums[:heads] + sums[heads : 2 * heads] + sums[2 * heads :]


def spread_heads(columns, heads):
    rows = columns.shape[0]
    lane = lax.broadcasted_iota(jnp.int32, (rows, 2 * HEAD_DIM), 1)
    pieces = []
    for head in range(0, heads, 2):
        left = jnp.broadcast_to(columns[:, head : head + 1], (rows, 2 * HEAD_DIM))
        right = jnp.broadcast_to(columns[:, head + 1 : head + 2], (rows, 2 * HEAD_DIM))
        pieces.append(jnp.where(lane < HEAD_DIM, left, right))
    return jnp.concatenate(pieces, axis=1)


def over_rows(values):
    heads = values.shape[0]
    return jnp.broadcast_to(values[:, None, :], (heads, HEAD_DIM, STATE)).reshape(
        heads * HEAD_DIM, STATE
    )


def contrib_kernel(decay, step, inputs, writes, parcel, first, total, running):
    block = pl.program_id(1)
    heads = decay.shape[1]
    cum_row = running_sums(decay[0])
    end_row = jnp.broadcast_to(cum_row[:, BLOCK - 1 :], (heads, STATE))
    to_end_row = jnp.exp(cum_row[:, BLOCK - 1 :] - cum_row) * step[0]
    to_end = jnp.transpose(to_end_row)
    scaled = (inputs[0].astype(F32) * spread_heads(to_end, heads)).astype(BF16)
    contrib = lax.dot_general(
        scaled, writes[0], (((0,), (0,)), ((), ())), preferred_element_type=F32
    )

    @pl.when(block == 0)
    def _():
        first[0] = contrib
        running[...] = contrib
        total[...] = end_row

    @pl.when(block > 0)
    def _():
        running[...] = over_rows(jnp.exp(end_row)) * running[...] + contrib
        total[...] = total[...] + end_row

    @pl.when(block == pl.num_programs(1) - 1)
    def _():
        carried = jnp.exp(total[...])
        high, rest = two_parts(carried)
        middle, low = two_parts(carried - high.astype(F32))
        row = lax.broadcasted_iota(jnp.int32, (heads, 8, STATE), 1)
        wide = lambda part: jnp.broadcast_to(part.astype(F32)[:, None, :], (heads, 8, STATE))
        extra = jnp.where(
            row == 0,
            wide(high),
            jnp.where(row == 1, wide(middle), jnp.where(row == 2, wide(low), 0.0)),
        )
        parcel[:, :HEAD_DIM, :] = running[...].reshape(heads, HEAD_DIM, STATE).astype(BF16)
        parcel[:, HEAD_DIM:, :] = extra.astype(BF16)


def contrib_call(decays, steps, inputs, writes):
    seqs, heads, length = decays.shape
    width = inputs.shape[2]
    blocks = length // BLOCK
    return pl.pallas_call(
        contrib_kernel,
        grid=(seqs, blocks),
        in_specs=[
            pl.BlockSpec((1, heads, BLOCK), lambda b, c: (b, 0, c)),
            pl.BlockSpec((1, heads, BLOCK), lambda b, c: (b, 0, c)),
            pl.BlockSpec((1, BLOCK, width), lambda b, c: (b, c, 0)),
            pl.BlockSpec((1, BLOCK, STATE), lambda b, c: (b, c, 0)),
        ],
        out_specs=[
            pl.BlockSpec((heads, HEAD_DIM + 8, STATE), lambda b, c: (b, 0, 0)),
            pl.BlockSpec((1, width, STATE), lambda b, c: (b, 0, 0)),
        ],
        out_shape=[
            jax.ShapeDtypeStruct((seqs * heads, HEAD_DIM + 8, STATE), BF16),
            jax.ShapeDtypeStruct((seqs, width, STATE), F32),
        ],
        scratch_shapes=[pltpu.VMEM((heads, STATE), F32), pltpu.VMEM((width, STATE), F32)],
        compiler_params=pltpu.CompilerParams(
            dimension_semantics=("arbitrary", "arbitrary"), vmem_limit_bytes=16 * 2**20
        ),
        cost_estimate=pl.CostEstimate(flops=10**9, bytes_accessed=2 * 2**20, transcendentals=8192),
        name="contrib",
    )(decays, steps, inputs, writes)


def within_kernel(decay, step, inputs, writes, reads, skip, first, within, factor):
    block = pl.program_id(0)
    heads = decay.shape[1]
    causal = triangle()
    log2e = 1.4426950408889634
    later = block > 0
    decays = jnp.where(later, decay[0, :, BLOCK:], decay[0, :, :BLOCK])
    ended = jnp.where(later, jnp.sum(decay[0, :, :BLOCK], axis=1, keepdims=True), 0.0)
    plain_row = running_sums(decays)
    factor[0] = jnp.transpose(jnp.exp(plain_row + ended))
    cum_row = plain_row * log2e
    cum_col = jnp.transpose(cum_row)
    steps = step[0]
    scores = dot_last(reads[0], writes[0])
    scores = jnp.where(causal, scores, 0.0)
    quad = 4 * HEAD_DIM
    lane = lax.broadcasted_iota(jnp.int32, (BLOCK, quad), 1)
    for start in range(0, heads, 4):
        columns = inputs[0][:, start * HEAD_DIM : start * HEAD_DIM + quad]
        total = skip[:, start * HEAD_DIM : start * HEAD_DIM + quad] * columns.astype(F32)
        for offset in range(4):
            head = start + offset
            gap = jnp.minimum(cum_col[:, head : head + 1] - cum_row[head : head + 1, :], 0.0)
            weights = (jnp.exp2(gap) * steps[head : head + 1, :] * scores).astype(BF16)
            own = (lane >= offset * HEAD_DIM) & (lane < (offset + 1) * HEAD_DIM)
            total = total + jnp.dot(
                weights,
                jnp.where(own, columns, jnp.zeros_like(columns)),
                preferred_element_type=F32,
            )
        within[0, :, start * HEAD_DIM : start * HEAD_DIM + quad] = total

    @pl.when(later)
    def _():
        high, low = two_parts(first[0])
        readout = dot_last(reads[0], high) + dot_last(reads[0], low)
        within[0] = within[0] + spread_heads(jnp.exp2(cum_col), heads) * readout


def within_call(which, decays, steps, inputs, writes, reads, skip, first):
    seqs, heads, length = decays.shape
    width = inputs.shape[2]
    assert length == 2 * BLOCK
    return pl.pallas_call(
        within_kernel,
        grid=(length // BLOCK,),
        in_specs=[
            pl.BlockSpec((1, heads, length), lambda c: (which, 0, 0)),
            pl.BlockSpec((1, heads, BLOCK), lambda c: (which, 0, c)),
            pl.BlockSpec((1, BLOCK, width), lambda c: (which, c, 0)),
            pl.BlockSpec((1, BLOCK, STATE), lambda c: (which, c, 0)),
            pl.BlockSpec((1, BLOCK, STATE), lambda c: (which, c, 0)),
            pl.BlockSpec((1, width), lambda c: (0, 0)),
            pl.BlockSpec((1, width, STATE), lambda c: (which, 0, 0)),
        ],
        out_specs=[
            pl.BlockSpec((1, BLOCK, width), lambda c: (0, c, 0)),
            pl.BlockSpec((1, BLOCK, heads), lambda c: (0, c, 0)),
        ],
        out_shape=[
            jax.ShapeDtypeStruct((1, length, width), F32),
            jax.ShapeDtypeStruct((1, length, heads), F32),
        ],
        compiler_params=pltpu.CompilerParams(
            dimension_semantics=("arbitrary",), vmem_limit_bytes=16 * 2**20
        ),
        cost_estimate=pl.CostEstimate(
            flops=3 * 10**9, bytes_accessed=2 * 2**20, transcendentals=2**20
        ),
        name="within",
    )(decays, steps, inputs, writes, reads, skip, first)


def scan_kernel(parcels, states):
    ranks = parcels.shape[0]
    state = jnp.zeros((HEAD_DIM, STATE), F32)
    for rank in range(ranks):
        states[rank] = state.astype(BF16)
        if rank < ranks - 1:
            extra = parcels[rank, HEAD_DIM:, :].astype(F32)
            factor = extra[0:1] + extra[1:2] + extra[2:3]
            state = factor * state + parcels[rank, :HEAD_DIM, :].astype(F32)


def scan_call(parcels):
    ranks = parcels.shape[0]
    return pl.pallas_call(
        scan_kernel,
        out_shape=jax.ShapeDtypeStruct((ranks, HEAD_DIM, STATE), BF16),
        cost_estimate=pl.CostEstimate(flops=10**6, bytes_accessed=2**19, transcendentals=0),
        name="scan",
    )(parcels)


def mixer_kernel(
    place, factors, reads, entering, within, gate, gain, weight, kept, passed, held, sems
):
    block = pl.program_id(0)
    blocks = pl.num_programs(0)
    heads = factors.shape[2]
    width = gate.shape[2]
    chips, keep = kept.shape[0], kept.shape[1]
    readout = dot_last(reads[0], entering[...].reshape(width, STATE))
    ssd_out = within[0] + spread_heads(factors[0], heads) * readout
    gates = gate[0].astype(F32)
    gated = ssd_out * (gates / (1.0 + jnp.exp(-gates)))
    factor = lax.rsqrt(jnp.mean(gated * gated, axis=-1, keepdims=True) + 1e-05)
    normed = (gated * factor * gain[...]).astype(BF16)
    product = jnp.dot(normed, weight[...], preferred_element_type=F32).astype(BF16)
    held[block] = product.reshape(held.shape[1], keep, D)
    pieces = held.shape[1]
    chip, core = lax.div(place[0], 2), lax.rem(place[0], 2)

    def piece(step, index, target):
        distance = lax.rem(step * (pieces // 2) + index // 2 - chip + chips, chips)
        return pltpu.make_async_copy(
            held.at[step, index], target.at[distance], sems.at[step, index]
        )

    for index in range(pieces):

        @pl.when(core == index % 2)
        def _():
            piece(block, index, kept).start()

        @pl.when(core != index % 2)
        def _():
            piece(block, index, passed).start()

    @pl.when(block == blocks - 1)
    def _():
        for step in range(held.shape[0]):
            for index in range(pieces):
                piece(step, index, kept).wait()


def mixer_call(which, place, factors, reads, entering, within, gate, gain, weight, columns):
    _, length, heads = factors.shape
    width = gate.shape[2]
    blocks = length // BLOCK
    keep = length // columns
    anywhere = pl.BlockSpec(memory_space=pl.ANY)
    return pl.pallas_call(
        mixer_kernel,
        grid=(blocks,),
        in_specs=[
            pl.BlockSpec(memory_space=pltpu.SMEM),
            pl.BlockSpec((1, BLOCK, heads), lambda c: (0, c, 0)),
            pl.BlockSpec((1, BLOCK, STATE), lambda c: (which, c, 0)),
            pl.BlockSpec((heads, HEAD_DIM, STATE), lambda c: (which, 0, 0)),
            pl.BlockSpec((1, BLOCK, width), lambda c: (0, c, 0)),
            pl.BlockSpec((1, BLOCK, width), lambda c: (which, c, 0)),
            pl.BlockSpec((1, width), lambda c: (0, 0)),
            pl.BlockSpec((width, D), lambda c: (0, 0)),
        ],
        out_specs=[anywhere, anywhere],
        out_shape=[jax.ShapeDtypeStruct((columns // 2, keep, D), BF16)] * 2,
        scratch_shapes=[
            pltpu.VMEM((blocks, columns // blocks, keep, D), BF16),
            pltpu.SemaphoreType.DMA((blocks, columns // blocks)),
        ],
        compiler_params=pltpu.CompilerParams(
            dimension_semantics=("arbitrary",), vmem_limit_bytes=16 * 2**20
        ),
        cost_estimate=pl.CostEstimate(
            flops=2 * 10**9, bytes_accessed=6 * 2**20, transcendentals=2**18
        ),
        name="mixer",
    )(place, factors, reads, entering, within, gate, gain, weight)


def unfold(rows, folded):
    pieces = [folded[pl.ds(part, rows, stride=FOLD), :].astype(BF16) for part in range(FOLD)]
    return jnp.concatenate(pieces, axis=1)


def fold(values, folded):
    rows = values.shape[0]
    for part in range(FOLD):
        folded[pl.ds(part, rows, stride=FOLD), :] = values[:, part * 128 : (part + 1) * 128]


def dispatch_kernel(
    residual, gain, places, own_top, got_top, own_bottom, got_bottom, *refs
):
    others = refs[:4]
    hidden, packed, folded = refs[4:]
    half = own_top.shape[1]
    for index, (own, got) in enumerate(((own_top, got_top), (own_bottom, got_bottom))):
        span = pl.ds(index * half, half)
        hidden[span, :] = (
            residual[span, :].astype(F32)
            + (own[0].astype(F32) + got[0].astype(F32))
            + others[2 * index][...].astype(F32)
            + others[2 * index + 1][...].astype(F32)
        )
    state = hidden[...]
    scale = lax.rsqrt(jnp.mean(state * state, axis=-1, keepdims=True) + 1e-05)
    moe_in = (state * scale * gain[...]).astype(BF16)
    rows = packed.shape[0]
    slot = lax.broadcasted_iota(jnp.int32, (rows + rows // FOLD, state.shape[0]), 0)
    chosen = (slot == places[0:1, :]) | (slot == places[1:2, :])
    select = jnp.where(chosen, 1.0, 0.0).astype(BF16)
    slots = jnp.dot(select, moe_in, preferred_element_type=F32)
    packed[:, :D] = slots[:rows].astype(BF16)
    fold(slots[rows:], folded)
    packed[:, D:] = folded[...].astype(BF16)


def dispatch_call(residual, gain, places, owns, others, experts):
    rows, half = residual.shape[0], residual.shape[0] // 2
    count = experts * FOLD
    whole = lambda shape: pl.BlockSpec(shape, lambda i: (0,) * len(shape))
    return pl.pallas_call(
        dispatch_kernel,
        grid=(1,),
        in_specs=[whole(residual.shape), whole(gain.shape), whole(places.shape)]
        + [whole((1, half, D))] * 4
        + [whole((half, D))] * 4,
        out_specs=[whole((rows, D)), whole((count, D + 128))],
        out_shape=[
            jax.ShapeDtypeStruct((rows, D), F32),
            jax.ShapeDtypeStruct((count, D + 128), BF16),
        ],
        scratch_shapes=[pltpu.VMEM((count, 128), F32)],
        compiler_params=pltpu.CompilerParams(vmem_limit_bytes=24 * 2**20),
        cost_estimate=pl.CostEstimate(
            flops=2 * 10**8, bytes_accessed=5 * 2**20, transcendentals=0
        ),
        name="dispatch",
    )(residual, gain, places, *owns, *others)


def combine_kernel(returned, places, gates, hidden, directions, out, folded, values):
    slots, rows = values.shape[0], hidden.shape[0]
    count = returned.shape[0]
    folded[...] = returned[:, D:].astype(F32)
    values[:count, :] = returned[:, :D]
    values[count:, :] = unfold(slots - count, folded)
    slot = lax.broadcasted_iota(jnp.int32, (rows, slots), 1)
    zero = jnp.zeros((rows, slots), F32)
    mix = jnp.where(slot == places[:, 0:1], gates[:, 0:1], zero) + jnp.where(
        slot == places[:, 1:2], gates[:, 1:2], zero
    )
    high, rest = two_parts(mix)
    middle, low = two_parts(mix - high.astype(F32))
    parts = jnp.concatenate([high, middle, low], axis=0)
    product = jnp.dot(parts, values[...], preferred_element_type=F32)
    combined = hidden[...] + (
        product[:rows] + product[rows : 2 * rows] + product[2 * rows :]
    )
    for index in range(directions.shape[0]):
        direction = directions[index : index + 1, :]
        norm = jnp.sum(direction * direction, axis=1, keepdims=True) + 1e-06
        along = jnp.sum(combined * direction, axis=1, keepdims=True) / norm
        combined = combined - along * direction
    out[...] = combined.astype(BF16)


def combine_call(returned, places, gates, hidden, directions):
    rows = hidden.shape[0]
    count = returned.shape[0]
    return pl.pallas_call(
        combine_kernel,
        out_shape=jax.ShapeDtypeStruct((rows, D), BF16),
        scratch_shapes=[
            pltpu.VMEM((count, 128), F32),
            pltpu.VMEM((count + count // FOLD, D), BF16),
        ],
        compiler_params=pltpu.CompilerParams(vmem_limit_bytes=24 * 2**20),
        cost_estimate=pl.CostEstimate(flops=10**9, bytes_accessed=4 * 2**20, transcendentals=0),
        name="combine",
    )(returned, places, gates, hidden, directions)


def expert_kernel(counts, *refs):
    number = len(counts)
    parts = refs[:number]
    gate, up, down, kept, passed = refs[number : number + 5]
    values, extra, folded, hidden, tail, main_sems, extra_sems = refs[number + 5 :]
    places = [sum(counts[:index]) for index in range(number)]
    count = sum(counts)
    lone = count // FOLD
    loads, extras = [], []
    for index, (part, place, size) in enumerate(zip(parts, places, counts)):
        span = pl.ds(place, size)
        extras.append(
            pltpu.make_async_copy(
                part.at[:, pl.ds(D, 128)], extra.at[span, :], extra_sems.at[index]
            )
        )
        loads.append(
            pltpu.make_async_copy(
                part.at[:, pl.ds(0, D)], values.at[span, :], main_sems.at[index]
            )
        )
    for load in extras + loads:
        load.start()
    for load in extras:
        load.wait()
    folded[...] = extra[...].astype(F32)
    values[count:, :] = unfold(lone, folded)
    for load in loads:
        load.wait()
    units = down.shape[0]
    whole = units // 256 * 256

    def open_units(start, size):
        span = pl.ds(start, size)
        first = jnp.dot(values[...], gate[:, span], preferred_element_type=F32)
        second = jnp.dot(values[...], up[:, span], preferred_element_type=F32)
        hidden[:, span] = (first / (1.0 + jnp.exp(-first)) * second).astype(BF16)

    @pl.loop(0, whole // 256)
    def _(index):
        open_units(pl.multiple_of(index * 256, 256), 256)

    if units > whole:
        open_units(whole, units - whole)
    half = kept.shape[0]

    @pl.loop(0, D // 1024)
    def _(index):
        span = pl.ds(pl.multiple_of(index * 1024, 1024), 1024)
        result = jnp.dot(hidden[...], down[:, span], preferred_element_type=F32)
        kept[:, span] = result[:half].astype(BF16)
        passed[:, span] = result[half:count].astype(BF16)
        tail[:, span] = result[count:]

    fold(tail[...], folded)
    kept[:, D:] = folded[:half, :].astype(BF16)
    passed[:, D:] = folded[half:, :].astype(BF16)


def expert_call(parts, gate, up, down):
    counts = tuple(part.shape[0] for part in parts)
    count = sum(counts)
    rows = count + count // FOLD
    units = down.shape[0]
    anywhere = pl.BlockSpec(memory_space=pl.ANY)
    near = pl.BlockSpec(memory_space=pltpu.VMEM)
    return pl.pallas_call(
        functools.partial(expert_kernel, counts),
        in_specs=[anywhere] * len(parts) + [near] * 3,
        out_specs=[near, near],
        out_shape=[jax.ShapeDtypeStruct((count // 2, D + 128), BF16)] * 2,
        scratch_shapes=[
            pltpu.VMEM((rows, D), BF16),
            pltpu.VMEM((count, 128), BF16),
            pltpu.VMEM((count, 128), F32),
            pltpu.VMEM((rows, units), BF16),
            pltpu.VMEM((count // FOLD, D), F32),
            pltpu.SemaphoreType.DMA((len(parts),)),
            pltpu.SemaphoreType.DMA((len(parts),)),
        ],
        compiler_params=pltpu.CompilerParams(vmem_limit_bytes=24 * 2**20),
        cost_estimate=pl.CostEstimate(
            flops=6 * rows * D * units,
            bytes_accessed=4 * rows * D + 6 * D * units,
            transcendentals=rows * units,
        ),
        name="expert",
    )(*parts, gate, up, down)


def settle_kernel(kept, got, top_after, top_before, bottom_before, bottom_after, out):
    half = top_after.shape[0]
    for index, others in enumerate(((top_after, top_before), (bottom_before, bottom_after))):
        span = pl.ds(index * half, half)
        total = kept[span, :].astype(F32) + got[span, :].astype(F32)
        for other in others:
            total = total + other[...].astype(F32)
        out[span, :] = total.astype(BF16)


def settle_call(*arrays):
    return pl.pallas_call(
        settle_kernel,
        out_shape=jax.ShapeDtypeStruct(arrays[0].shape, BF16),
        compiler_params=pltpu.CompilerParams(vmem_limit_bytes=16 * 2**20),
        cost_estimate=pl.CostEstimate(flops=2 * 10**6, bytes_accessed=5 * 2**20, transcendentals=0),
        name="settle",
    )(*arrays)


def from_before(values):
    size = lax.axis_size("exp")
    return lax.ppermute(values, "exp", [(i, (i + 2) % size) for i in range(size)])


def from_after(values):
    size = lax.axis_size("exp")
    return lax.ppermute(values, "exp", [(i, (i - 2) % size) for i in range(size)])


def from_sibling(values):
    size = lax.axis_size("exp")
    return lax.ppermute(values, "exp", [(i, i ^ 1) for i in range(size)])


def add_up(*terms):
    total = terms[0].astype(F32)
    for term in terms[1:]:
        total = total + term.astype(F32)
    return total.astype(BF16)


def after(values, *earlier):
    return lax.optimization_barrier((tuple(values), earlier))[0]


def expert_layer(own, gate, up, down):
    half = own.shape[0] // 2
    top, bottom = own[:half], own[half:]
    own_other = from_sibling(own)
    before_top = from_before(top)
    after_bottom = from_after(bottom)
    call = functools.partial(expert_call, gate=gate, up=up, down=down)
    kept_own, passed = call((own, own_other))
    before_top, after_bottom, kept_own, passed, top, bottom = after(
        (before_top, after_bottom, kept_own, passed, top, bottom)
    )
    got_own = from_sibling(passed)
    others = from_sibling(before_top), from_sibling(after_bottom)
    far_top = from_before(before_top)
    far_bottom = from_after(after_bottom)
    before_bottom = from_before(bottom)
    after_top = from_after(top)
    kept, passed = call((before_top, after_bottom, *others))
    far_top, far_bottom, got_own, kept, passed = after(
        (far_top, far_bottom, got_own, kept, passed)
    )
    got = from_sibling(passed)
    others = from_sibling(far_top), from_sibling(far_bottom)
    near_top, near_bottom = add_up(kept[:half], got[:half]), add_up(kept[half:], got[half:])
    near_top, near_bottom, far_top, far_bottom = after(
        (near_top, near_bottom, far_top, far_bottom)
    )
    top_after = from_after(near_top)
    bottom_before = from_before(near_bottom)
    kept, passed = call((far_top, far_bottom, *others))
    after_top, before_bottom, kept, passed = after((after_top, before_bottom, kept, passed))
    late = from_sibling(after_top), from_sibling(before_bottom)
    got = from_sibling(passed)
    far_top, far_bottom = add_up(kept[:half], got[:half]), add_up(kept[half:], got[half:])
    far_top, far_bottom, after_top, before_bottom = after(
        (far_top, far_bottom, after_top, before_bottom)
    )
    relay_top = from_before(far_top)
    relay_bottom = from_after(far_bottom)
    kept, passed = call((after_top, before_bottom, *late))
    relay_top, relay_bottom, top_after, bottom_before, kept, passed = after(
        (relay_top, relay_bottom, top_after, bottom_before, kept, passed)
    )
    got = from_sibling(passed)
    top_before = from_before(add_up(kept[:half], got[:half], relay_top))
    bottom_after = from_after(add_up(kept[half:], got[half:], relay_bottom))
    return settle_call(
        kept_own, got_own, top_after, top_before, bottom_before, bottom_after
    )


def on_device(
    ssd_input,
    ssd_gate,
    state_write,
    state_read,
    step_size,
    decay_log,
    skip_gain,
    norm_gain,
    w_out,
    resid,
    moe_gain,
    w_gate,
    w_up,
    w_down,
    routes,
    gates,
    directions,
):
    length_dev, seqs, width_dev = ssd_input.shape
    heads_dev = decay_log.shape[0]
    experts = lax.axis_size("seq")
    columns = lax.axis_size("exp")
    rows_keep = length_dev * seqs // columns

    def swap(values):
        return jnp.transpose(values, (1, 0, 2))

    decays, steps = swap(decay_log), swap(step_size)
    inputs, writes, reads = swap(ssd_input), swap(state_write), swap(state_read)
    parcel, first = contrib_call(decays, steps, inputs, writes)
    parcels = lax.all_to_all(parcel, "seq", split_axis=0, concat_axis=0, tiled=True)
    skip = jnp.repeat(skip_gain, HEAD_DIM)[None, :]
    within_early, factor_early = within_call(
        0, decays, steps, inputs, writes, reads, skip, first
    )
    (parcels,) = after((parcels,), within_early)
    entering = lax.all_to_all(
        scan_call(parcels), "seq", split_axis=0, concat_axis=0, tiled=True
    )
    within_late, factor_late = within_call(
        1, decays, steps, inputs, writes, reads, skip, first
    )
    gating = swap(ssd_gate)
    (entering,) = after((entering,), within_late, gating)
    place = lax.axis_index("exp").astype(jnp.int32)[None]
    kept, passed = mixer_call(
        0, place, factor_early, reads, entering, within_early, gating, norm_gain[None, :], w_out, columns
    )
    got = from_sibling(passed)
    (place,) = after((place,), kept)
    kept_late, passed = mixer_call(
        1, place, factor_late, reads, entering, within_late, gating, norm_gain[None, :], w_out, columns
    )
    got_late = from_sibling(passed)
    relay_top = from_before(add_up(kept[2], got[2]))
    top_after = from_after(add_up(kept[3], got[3]))
    relay_bottom = from_after(add_up(kept_late[2], got_late[2]))
    bottom_before = from_before(add_up(kept_late[1], got_late[1]))
    top_before = from_before(add_up(kept[1], got[1], relay_top))
    bottom_after = from_after(add_up(kept_late[3], got_late[3], relay_bottom))
    capacity = max(2, 2 * rows_keep * 17 // (16 * experts))
    assert capacity == FOLD + 1
    picks = swap(routes).reshape(-1)
    onehot = (picks[:, None] == jnp.arange(experts, dtype=jnp.int32)[None, :]).astype(jnp.int32)
    before = jnp.cumsum(onehot, axis=0) - onehot
    ranked = jnp.sum(before * onehot, axis=1)
    places = jnp.where(
        ranked < FOLD, picks * FOLD + ranked, experts * FOLD + picks
    ).reshape(rows_keep, 2)
    hidden_state, packed = dispatch_call(
        swap(resid).reshape(rows_keep, D),
        moe_gain[None, :],
        places.T,
        (kept, got, kept_late, got_late),
        (top_after, top_before, bottom_before, bottom_after),
        experts,
    )
    arrived = lax.all_to_all(
        packed.reshape(experts, FOLD, D + 128), "seq", split_axis=0, concat_axis=0, tiled=True
    )
    summed = expert_layer(arrived.reshape(packed.shape), w_gate[0], w_up[0], w_down[0])
    returned = lax.all_to_all(
        summed.reshape(experts, FOLD, D + 128), "seq", split_axis=0, concat_axis=0, tiled=True
    )
    combined = combine_call(
        returned.reshape(packed.shape),
        places,
        swap(gates).reshape(rows_keep, 2),
        hidden_state,
        directions,
    )
    return swap(combined.reshape(seqs, length_dev // columns, D))


def solution(mesh):
    in_specs = (
        P("seq", None, "exp"),
        P("seq", None, "exp"),
        P("seq", None, "exp"),
        P("seq", None, "exp"),
        P("exp", None, "seq"),
        P("exp", None, "seq"),
        P("exp"),
        P("exp"),
        P("exp", None),
        P(("seq", "exp"), None, None),
        P(),
        P("seq", None, "exp"),
        P("seq", None, "exp"),
        P("seq", "exp", None),
        P(("seq", "exp"), None, None),
        P(("seq", "exp"), None, None),
        P(),
    )
    out_specs = P(("seq", "exp"), None, None)
    return jax.shard_map(
        on_device, mesh=mesh, in_specs=in_specs, out_specs=out_specs, check_vma=False
    )
```

```python
import functools

import jax
import jax.numpy as jnp
from jax import lax
from jax.experimental import pallas as pl
from jax.experimental.pallas import tpu as pltpu
from jax.sharding import PartitionSpec as P

D = 2048
HEADS = 64
HEAD_DIM = 64
STATE = 128
GROUPS = 8
BLOCK = 256
FOLD = 16
F32 = jnp.float32
BF16 = jnp.bfloat16


def dot_last(left, right, **options):
    return lax.dot_general(
        left, right, (((1,), (1,)), ((), ())), preferred_element_type=F32, **options
    )


def two_parts(values):
    high = values.astype(BF16)
    return high, (values - high.astype(F32)).astype(BF16)


def triangle():
    row = lax.broadcasted_iota(jnp.int32, (BLOCK, BLOCK), 0)
    col = lax.broadcasted_iota(jnp.int32, (BLOCK, BLOCK), 1)
    return row >= col


def running_sums(decays):
    heads = decays.shape[0]
    high, rest = two_parts(decays)
    middle, low = two_parts(decays - high.astype(F32))
    parts = jnp.concatenate(
        [high.astype(F32), middle.astype(F32), low.astype(F32)], axis=0
    ).astype(BF16)
    ones = jnp.where(triangle(), 1.0, 0.0).astype(BF16)
    sums = dot_last(parts, ones)
    return sums[:heads] + sums[heads : 2 * heads] + sums[2 * heads :]


def spread_heads(columns, heads):
    rows = columns.shape[0]
    lane = lax.broadcasted_iota(jnp.int32, (rows, 2 * HEAD_DIM), 1)
    pieces = []
    for head in range(0, heads, 2):
        left = jnp.broadcast_to(columns[:, head : head + 1], (rows, 2 * HEAD_DIM))
        right = jnp.broadcast_to(columns[:, head + 1 : head + 2], (rows, 2 * HEAD_DIM))
        pieces.append(jnp.where(lane < HEAD_DIM, left, right))
    return jnp.concatenate(pieces, axis=1)


def over_rows(values):
    heads = values.shape[0]
    return jnp.broadcast_to(values[:, None, :], (heads, HEAD_DIM, STATE)).reshape(
        heads * HEAD_DIM, STATE
    )


def contrib_kernel(decay, step, inputs, writes, parcel, first):
    heads, length = decay.shape[1], decay.shape[2]
    running = total = None
    for start in range(0, length, BLOCK):
        span = slice(start, start + BLOCK)
        cum_row = running_sums(decay[0, :, span])
        end = cum_row[:, BLOCK - 1 :]
        to_end = jnp.transpose(jnp.exp(end - cum_row) * step[0, :, span])
        scaled = (inputs[0, span, :].astype(F32) * spread_heads(to_end, heads)).astype(BF16)
        contrib = lax.dot_general(
            scaled, writes[0, span, :], (((0,), (0,)), ((), ())), preferred_element_type=F32
        )
        end_row = jnp.broadcast_to(end, (heads, STATE))
        if start == 0:
            first[0] = contrib
            running, total = contrib, end_row
        else:
            running = over_rows(jnp.exp(end_row)) * running + contrib
            total = total + end_row
    carried = jnp.exp(total)
    high, rest = two_parts(carried)
    middle, low = two_parts(carried - high.astype(F32))
    row = lax.broadcasted_iota(jnp.int32, (heads, 8, STATE), 1)
    wide = lambda part: jnp.broadcast_to(part.astype(F32)[:, None, :], (heads, 8, STATE))
    extra = jnp.where(
        row == 0,
        wide(high),
        jnp.where(row == 1, wide(middle), jnp.where(row == 2, wide(low), 0.0)),
    )
    parcel[:, :HEAD_DIM, :] = running.reshape(heads, HEAD_DIM, STATE).astype(BF16)
    parcel[:, HEAD_DIM:, :] = extra.astype(BF16)


def contrib_call(decays, steps, inputs, writes):
    seqs, heads, length = decays.shape
    width = inputs.shape[2]
    assert length == 2 * BLOCK
    return pl.pallas_call(
        contrib_kernel,
        grid=(seqs,),
        in_specs=[
            pl.BlockSpec((1, heads, length), lambda b: (b, 0, 0)),
            pl.BlockSpec((1, heads, length), lambda b: (b, 0, 0)),
            pl.BlockSpec((1, length, width), lambda b: (b, 0, 0)),
            pl.BlockSpec((1, length, STATE), lambda b: (b, 0, 0)),
        ],
        out_specs=[
            pl.BlockSpec((heads, HEAD_DIM + 8, STATE), lambda b: (b, 0, 0)),
            pl.BlockSpec((1, width, STATE), lambda b: (b, 0, 0)),
        ],
        out_shape=[
            jax.ShapeDtypeStruct((seqs * heads, HEAD_DIM + 8, STATE), BF16),
            jax.ShapeDtypeStruct((seqs, width, STATE), F32),
        ],
        compiler_params=pltpu.CompilerParams(
            dimension_semantics=("arbitrary",), vmem_limit_bytes=16 * 2**20
        ),
        cost_estimate=pl.CostEstimate(flops=10**9, bytes_accessed=2 * 2**20, transcendentals=8192),
        name="contrib",
    )(decays, steps, inputs, writes)


def within_kernel(decay, step, inputs, writes, reads, skip, first, within, factor):
    block = pl.program_id(0)
    heads = decay.shape[1]
    causal = triangle()
    log2e = 1.4426950408889634
    later = block > 0
    decays = jnp.where(later, decay[0, :, BLOCK:], decay[0, :, :BLOCK])
    ended = jnp.where(later, jnp.sum(decay[0, :, :BLOCK], axis=1, keepdims=True), 0.0)
    plain_row = running_sums(decays)
    factor[0] = jnp.transpose(jnp.exp(plain_row + ended))
    cum_row = plain_row * log2e
    cum_col = jnp.transpose(cum_row)
    steps = step[0]
    scores = dot_last(reads[0], writes[0])
    scores = jnp.where(causal, scores, 0.0)
    quad = 4 * HEAD_DIM
    lane = lax.broadcasted_iota(jnp.int32, (BLOCK, quad), 1)
    for start in range(0, heads, 4):
        columns = inputs[0][:, start * HEAD_DIM : start * HEAD_DIM + quad]
        total = skip[:, start * HEAD_DIM : start * HEAD_DIM + quad] * columns.astype(F32)
        for offset in range(4):
            head = start + offset
            gap = jnp.minimum(cum_col[:, head : head + 1] - cum_row[head : head + 1, :], 0.0)
            weights = (jnp.exp2(gap) * steps[head : head + 1, :] * scores).astype(BF16)
            own = (lane >= offset * HEAD_DIM) & (lane < (offset + 1) * HEAD_DIM)
            total = total + jnp.dot(
                weights,
                jnp.where(own, columns, jnp.zeros_like(columns)),
                preferred_element_type=F32,
            )
        within[0, :, start * HEAD_DIM : start * HEAD_DIM + quad] = total

    @pl.when(later)
    def _():
        high, low = two_parts(first[0])
        readout = dot_last(reads[0], high) + dot_last(reads[0], low)
        within[0] = within[0] + spread_heads(jnp.exp2(cum_col), heads) * readout


def within_call(which, decays, steps, inputs, writes, reads, skip, first):
    seqs, heads, length = decays.shape
    width = inputs.shape[2]
    assert length == 2 * BLOCK
    return pl.pallas_call(
        within_kernel,
        grid=(length // BLOCK,),
        in_specs=[
            pl.BlockSpec((1, heads, length), lambda c: (which, 0, 0)),
            pl.BlockSpec((1, heads, BLOCK), lambda c: (which, 0, c)),
            pl.BlockSpec((1, BLOCK, width), lambda c: (which, c, 0)),
            pl.BlockSpec((1, BLOCK, STATE), lambda c: (which, c, 0)),
            pl.BlockSpec((1, BLOCK, STATE), lambda c: (which, c, 0)),
            pl.BlockSpec((1, width), lambda c: (0, 0)),
            pl.BlockSpec((1, width, STATE), lambda c: (which, 0, 0)),
        ],
        out_specs=[
            pl.BlockSpec((1, BLOCK, width), lambda c: (0, c, 0)),
            pl.BlockSpec((1, BLOCK, heads), lambda c: (0, c, 0)),
        ],
        out_shape=[
            jax.ShapeDtypeStruct((1, length, width), F32),
            jax.ShapeDtypeStruct((1, length, heads), F32),
        ],
        compiler_params=pltpu.CompilerParams(
            dimension_semantics=("arbitrary",), vmem_limit_bytes=16 * 2**20
        ),
        cost_estimate=pl.CostEstimate(
            flops=3 * 10**9, bytes_accessed=2 * 2**20, transcendentals=2**20
        ),
        name="within",
    )(decays, steps, inputs, writes, reads, skip, first)


def scan_kernel(parcels, states):
    ranks = parcels.shape[0]
    state = jnp.zeros((HEAD_DIM, STATE), F32)
    for rank in range(ranks):
        states[rank] = state.astype(BF16)
        if rank < ranks - 1:
            extra = parcels[rank, HEAD_DIM:, :].astype(F32)
            factor = extra[0:1] + extra[1:2] + extra[2:3]
            state = factor * state + parcels[rank, :HEAD_DIM, :].astype(F32)


def scan_call(parcels):
    ranks = parcels.shape[0]
    return pl.pallas_call(
        scan_kernel,
        out_shape=jax.ShapeDtypeStruct((ranks, HEAD_DIM, STATE), BF16),
        cost_estimate=pl.CostEstimate(flops=10**6, bytes_accessed=2**19, transcendentals=0),
        name="scan",
    )(parcels)


def mixer_kernel(
    place, factors, reads, entering, within, gate, gain, weight, kept, passed, held, sems
):
    block = pl.program_id(0)
    blocks = pl.num_programs(0)
    heads = factors.shape[2]
    width = gate.shape[2]
    chips, keep = kept.shape[0], kept.shape[1]
    readout = dot_last(reads[0], entering[...].reshape(width, STATE))
    ssd_out = within[0] + spread_heads(factors[0], heads) * readout
    gates = gate[0].astype(F32)
    gated = ssd_out * (gates / (1.0 + jnp.exp(-gates)))
    factor = lax.rsqrt(jnp.mean(gated * gated, axis=-1, keepdims=True) + 1e-05)
    normed = (gated * factor * gain[...]).astype(BF16)
    product = jnp.dot(normed, weight[...], preferred_element_type=F32).astype(BF16)
    held[block] = product.reshape(held.shape[1], keep, D)
    pieces = held.shape[1]
    chip, core = lax.div(place[0], 2), lax.rem(place[0], 2)

    def piece(step, index, target):
        distance = lax.rem(step * (pieces // 2) + index // 2 - chip + chips, chips)
        return pltpu.make_async_copy(
            held.at[step, index], target.at[distance], sems.at[step, index]
        )

    for index in range(pieces):

        @pl.when(core == index % 2)
        def _():
            piece(block, index, kept).start()

        @pl.when(core != index % 2)
        def _():
            piece(block, index, passed).start()

    @pl.when(block == blocks - 1)
    def _():
        for step in range(held.shape[0]):
            for index in range(pieces):
                piece(step, index, kept).wait()


def mixer_call(which, place, factors, reads, entering, within, gate, gain, weight, columns):
    _, length, heads = factors.shape
    width = gate.shape[2]
    blocks = length // BLOCK
    keep = length // columns
    anywhere = pl.BlockSpec(memory_space=pl.ANY)
    return pl.pallas_call(
        mixer_kernel,
        grid=(blocks,),
        in_specs=[
            pl.BlockSpec(memory_space=pltpu.SMEM),
            pl.BlockSpec((1, BLOCK, heads), lambda c: (0, c, 0)),
            pl.BlockSpec((1, BLOCK, STATE), lambda c: (which, c, 0)),
            pl.BlockSpec((heads, HEAD_DIM, STATE), lambda c: (which, 0, 0)),
            pl.BlockSpec((1, BLOCK, width), lambda c: (0, c, 0)),
            pl.BlockSpec((1, BLOCK, width), lambda c: (which, c, 0)),
            pl.BlockSpec((1, width), lambda c: (0, 0)),
            pl.BlockSpec(memory_space=pltpu.VMEM),
        ],
        out_specs=[anywhere, anywhere],
        out_shape=[jax.ShapeDtypeStruct((columns // 2, keep, D), BF16)] * 2,
        scratch_shapes=[
            pltpu.VMEM((blocks, columns // blocks, keep, D), BF16),
            pltpu.SemaphoreType.DMA((blocks, columns // blocks)),
        ],
        compiler_params=pltpu.CompilerParams(
            dimension_semantics=("arbitrary",), vmem_limit_bytes=16 * 2**20
        ),
        cost_estimate=pl.CostEstimate(
            flops=2 * 10**9, bytes_accessed=6 * 2**20, transcendentals=2**18
        ),
        name="mixer",
    )(place, factors, reads, entering, within, gate, gain, weight)


def unfold(rows, folded):
    pieces = [folded[pl.ds(part, rows, stride=FOLD), :].astype(BF16) for part in range(FOLD)]
    return jnp.concatenate(pieces, axis=1)


def fold(values, folded):
    rows = values.shape[0]
    for part in range(FOLD):
        folded[pl.ds(part, rows, stride=FOLD), :] = values[:, part * 128 : (part + 1) * 128]


def dispatch_kernel(
    residual, gain, places, own_top, got_top, own_bottom, got_bottom, *refs
):
    others = refs[:4]
    hidden, packed, folded = refs[4:]
    half = own_top.shape[1]
    for index, (own, got) in enumerate(((own_top, got_top), (own_bottom, got_bottom))):
        span = pl.ds(index * half, half)
        hidden[span, :] = (
            residual[span, :].astype(F32)
            + (own[0].astype(F32) + got[0].astype(F32))
            + others[2 * index][...].astype(F32)
            + others[2 * index + 1][...].astype(F32)
        )
    state = hidden[...]
    scale = lax.rsqrt(jnp.mean(state * state, axis=-1, keepdims=True) + 1e-05)
    moe_in = (state * scale * gain[...]).astype(BF16)
    rows = packed.shape[0]
    slot = lax.broadcasted_iota(jnp.int32, (rows + rows // FOLD, state.shape[0]), 0)
    chosen = (slot == places[0:1, :]) | (slot == places[1:2, :])
    select = jnp.where(chosen, 1.0, 0.0).astype(BF16)
    slots = jnp.dot(select, moe_in, preferred_element_type=F32)
    packed[:, :D] = slots[:rows].astype(BF16)
    fold(slots[rows:], folded)
    packed[:, D:] = folded[...].astype(BF16)


def dispatch_call(residual, gain, places, owns, others, experts):
    rows, half = residual.shape[0], residual.shape[0] // 2
    count = experts * FOLD
    whole = lambda shape: pl.BlockSpec(shape, lambda i: (0,) * len(shape))
    return pl.pallas_call(
        dispatch_kernel,
        grid=(1,),
        in_specs=[whole(residual.shape), whole(gain.shape), whole(places.shape)]
        + [whole((1, half, D))] * 4
        + [whole((half, D))] * 4,
        out_specs=[whole((rows, D)), whole((count, D + 128))],
        out_shape=[
            jax.ShapeDtypeStruct((rows, D), F32),
            jax.ShapeDtypeStruct((count, D + 128), BF16),
        ],
        scratch_shapes=[pltpu.VMEM((count, 128), F32)],
        compiler_params=pltpu.CompilerParams(vmem_limit_bytes=24 * 2**20),
        cost_estimate=pl.CostEstimate(
            flops=2 * 10**8, bytes_accessed=5 * 2**20, transcendentals=0
        ),
        name="dispatch",
    )(residual, gain, places, *owns, *others)


def combine_kernel(returned, places, gates, hidden, directions, out, folded, values):
    slots, rows = values.shape[0], hidden.shape[0]
    count = returned.shape[0]
    folded[...] = returned[:, D:].astype(F32)
    values[:count, :] = returned[:, :D]
    values[count:, :] = unfold(slots - count, folded)
    slot = lax.broadcasted_iota(jnp.int32, (rows, slots), 1)
    zero = jnp.zeros((rows, slots), F32)
    mix = jnp.where(slot == places[:, 0:1], gates[:, 0:1], zero) + jnp.where(
        slot == places[:, 1:2], gates[:, 1:2], zero
    )
    high, rest = two_parts(mix)
    middle, low = two_parts(mix - high.astype(F32))
    parts = jnp.concatenate([high, middle, low], axis=0)
    product = jnp.dot(parts, values[...], preferred_element_type=F32)
    combined = hidden[...] + (
        product[:rows] + product[rows : 2 * rows] + product[2 * rows :]
    )
    for index in range(directions.shape[0]):
        direction = directions[index : index + 1, :]
        norm = jnp.sum(direction * direction, axis=1, keepdims=True) + 1e-06
        along = jnp.sum(combined * direction, axis=1, keepdims=True) / norm
        combined = combined - along * direction
    half = rows // 2
    out[:, 0, :] = combined[:half].astype(BF16)
    out[:, 1, :] = combined[half:].astype(BF16)


def combine_call(returned, places, gates, hidden, directions):
    rows = hidden.shape[0]
    count = returned.shape[0]
    return pl.pallas_call(
        combine_kernel,
        out_shape=jax.ShapeDtypeStruct((rows // 2, 2, D), BF16),
        scratch_shapes=[
            pltpu.VMEM((count, 128), F32),
            pltpu.VMEM((count + count // FOLD, D), BF16),
        ],
        compiler_params=pltpu.CompilerParams(vmem_limit_bytes=24 * 2**20),
        cost_estimate=pl.CostEstimate(flops=10**9, bytes_accessed=4 * 2**20, transcendentals=0),
        name="combine",
    )(returned, places, gates, hidden, directions)


def expert_kernel(counts, *refs):
    number = len(counts)
    parts = refs[:number]
    gate, up, down, kept, passed = refs[number : number + 5]
    values, extra, folded, hidden, tail, main_sems, extra_sems = refs[number + 5 :]
    places = [sum(counts[:index]) for index in range(number)]
    count = sum(counts)
    lone = count // FOLD
    loads, extras = [], []
    for index, (part, place, size) in enumerate(zip(parts, places, counts)):
        span = pl.ds(place, size)
        extras.append(
            pltpu.make_async_copy(
                part.at[:, pl.ds(D, 128)], extra.at[span, :], extra_sems.at[index]
            )
        )
        loads.append(
            pltpu.make_async_copy(
                part.at[:, pl.ds(0, D)], values.at[span, :], main_sems.at[index]
            )
        )
    for load in extras + loads:
        load.start()
    for load in extras:
        load.wait()
    folded[...] = extra[...].astype(F32)
    values[count:, :] = unfold(lone, folded)
    for load in loads:
        load.wait()
    units = down.shape[0]
    whole = units // 256 * 256

    def open_units(start, size):
        span = pl.ds(start, size)
        first = jnp.dot(values[...], gate[:, span], preferred_element_type=F32)
        second = jnp.dot(values[...], up[:, span], preferred_element_type=F32)
        hidden[:, span] = (first / (1.0 + jnp.exp(-first)) * second).astype(BF16)

    @pl.loop(0, whole // 256)
    def _(index):
        open_units(pl.multiple_of(index * 256, 256), 256)

    if units > whole:
        open_units(whole, units - whole)
    half = kept.shape[0]

    @pl.loop(0, D // 1024)
    def _(index):
        span = pl.ds(pl.multiple_of(index * 1024, 1024), 1024)
        result = jnp.dot(hidden[...], down[:, span], preferred_element_type=F32)
        kept[:, span] = result[:half].astype(BF16)
        passed[:, span] = result[half:count].astype(BF16)
        tail[:, span] = result[count:]

    fold(tail[...], folded)
    kept[:, D:] = folded[:half, :].astype(BF16)
    passed[:, D:] = folded[half:, :].astype(BF16)


def expert_call(parts, gate, up, down):
    counts = tuple(part.shape[0] for part in parts)
    count = sum(counts)
    rows = count + count // FOLD
    units = down.shape[0]
    anywhere = pl.BlockSpec(memory_space=pl.ANY)
    near = pl.BlockSpec(memory_space=pltpu.VMEM)
    return pl.pallas_call(
        functools.partial(expert_kernel, counts),
        in_specs=[anywhere] * len(parts) + [near] * 3,
        out_specs=[near, near],
        out_shape=[jax.ShapeDtypeStruct((count // 2, D + 128), BF16)] * 2,
        scratch_shapes=[
            pltpu.VMEM((rows, D), BF16),
            pltpu.VMEM((count, 128), BF16),
            pltpu.VMEM((count, 128), F32),
            pltpu.VMEM((rows, units), BF16),
            pltpu.VMEM((count // FOLD, D), F32),
            pltpu.SemaphoreType.DMA((len(parts),)),
            pltpu.SemaphoreType.DMA((len(parts),)),
        ],
        compiler_params=pltpu.CompilerParams(vmem_limit_bytes=24 * 2**20),
        cost_estimate=pl.CostEstimate(
            flops=6 * rows * D * units,
            bytes_accessed=4 * rows * D + 6 * D * units,
            transcendentals=rows * units,
        ),
        name="expert",
    )(*parts, gate, up, down)


def settle_kernel(kept, got, top_after, top_before, bottom_before, bottom_after, out):
    half = top_after.shape[0]
    for index, others in enumerate(((top_after, top_before), (bottom_before, bottom_after))):
        span = pl.ds(index * half, half)
        total = kept[span, :].astype(F32) + got[span, :].astype(F32)
        for other in others:
            total = total + other[...].astype(F32)
        out[span, :] = total.astype(BF16)


def settle_call(*arrays):
    return pl.pallas_call(
        settle_kernel,
        out_shape=jax.ShapeDtypeStruct(arrays[0].shape, BF16),
        compiler_params=pltpu.CompilerParams(vmem_limit_bytes=16 * 2**20),
        cost_estimate=pl.CostEstimate(flops=2 * 10**6, bytes_accessed=5 * 2**20, transcendentals=0),
        name="settle",
    )(*arrays)


def from_before(values):
    size = lax.axis_size("exp")
    return lax.ppermute(values, "exp", [(i, (i + 2) % size) for i in range(size)])


def from_after(values):
    size = lax.axis_size("exp")
    return lax.ppermute(values, "exp", [(i, (i - 2) % size) for i in range(size)])


def from_sibling(values):
    size = lax.axis_size("exp")
    return lax.ppermute(values, "exp", [(i, i ^ 1) for i in range(size)])


def add_up(*terms):
    total = terms[0].astype(F32)
    for term in terms[1:]:
        total = total + term.astype(F32)
    return total.astype(BF16)


def after(values, *earlier):
    return lax.optimization_barrier((tuple(values), earlier))[0]


def expert_layer(own, gate, up, down):
    half = own.shape[0] // 2
    top, bottom = own[:half], own[half:]
    own_other = from_sibling(own)
    before_top = from_before(top)
    after_bottom = from_after(bottom)
    call = functools.partial(expert_call, gate=gate, up=up, down=down)
    kept_own, passed = call((own, own_other))
    before_top, after_bottom, kept_own, passed, top, bottom = after(
        (before_top, after_bottom, kept_own, passed, top, bottom)
    )
    got_own = from_sibling(passed)
    others = from_sibling(before_top), from_sibling(after_bottom)
    far_top = from_before(before_top)
    far_bottom = from_after(after_bottom)
    before_bottom = from_before(bottom)
    after_top = from_after(top)
    kept, passed = call((before_top, after_bottom, *others))
    far_top, far_bottom, got_own, kept, passed = after(
        (far_top, far_bottom, got_own, kept, passed)
    )
    got = from_sibling(passed)
    others = from_sibling(far_top), from_sibling(far_bottom)
    near_top, near_bottom = add_up(kept[:half], got[:half]), add_up(kept[half:], got[half:])
    near_top, near_bottom, far_top, far_bottom = after(
        (near_top, near_bottom, far_top, far_bottom)
    )
    top_after = from_after(near_top)
    bottom_before = from_before(near_bottom)
    kept, passed = call((far_top, far_bottom, *others))
    after_top, before_bottom, kept, passed = after((after_top, before_bottom, kept, passed))
    late = from_sibling(after_top), from_sibling(before_bottom)
    got = from_sibling(passed)
    far_top, far_bottom = add_up(kept[:half], got[:half]), add_up(kept[half:], got[half:])
    far_top, far_bottom, after_top, before_bottom = after(
        (far_top, far_bottom, after_top, before_bottom)
    )
    relay_top = from_before(far_top)
    relay_bottom = from_after(far_bottom)
    kept, passed = call((after_top, before_bottom, *late))
    relay_top, relay_bottom, top_after, bottom_before, kept, passed = after(
        (relay_top, relay_bottom, top_after, bottom_before, kept, passed)
    )
    got = from_sibling(passed)
    top_before = from_before(add_up(kept[:half], got[:half], relay_top))
    bottom_after = from_after(add_up(kept[half:], got[half:], relay_bottom))
    return settle_call(
        kept_own, got_own, top_after, top_before, bottom_before, bottom_after
    )


def on_device(
    ssd_input,
    ssd_gate,
    state_write,
    state_read,
    step_size,
    decay_log,
    skip_gain,
    norm_gain,
    w_out,
    resid,
    moe_gain,
    w_gate,
    w_up,
    w_down,
    routes,
    gates,
    directions,
):
    length_dev, seqs, width_dev = ssd_input.shape
    heads_dev = decay_log.shape[0]
    experts = lax.axis_size("seq")
    columns = lax.axis_size("exp")
    rows_keep = length_dev * seqs // columns

    def swap(values):
        return jnp.transpose(values, (1, 0, 2))

    decays, steps = swap(decay_log), swap(step_size)
    inputs, writes, reads = swap(ssd_input), swap(state_write), swap(state_read)
    parcel, first = contrib_call(decays, steps, inputs, writes)
    parcels = lax.all_to_all(parcel, "seq", split_axis=0, concat_axis=0, tiled=True)
    skip = jnp.repeat(skip_gain, HEAD_DIM)[None, :]
    within_early, factor_early = within_call(
        0, decays, steps, inputs, writes, reads, skip, first
    )
    (parcels,) = after((parcels,), within_early)
    entering = lax.all_to_all(
        scan_call(parcels), "seq", split_axis=0, concat_axis=0, tiled=True
    )
    within_late, factor_late = within_call(
        1, decays, steps, inputs, writes, reads, skip, first
    )
    gating = swap(ssd_gate)
    (entering,) = after((entering,), within_late, gating)
    place = lax.axis_index("exp").astype(jnp.int32)[None]
    kept, passed = mixer_call(
        0, place, factor_early, reads, entering, within_early, gating, norm_gain[None, :], w_out, columns
    )
    got = from_sibling(passed)
    (place,) = after((place,), kept)
    kept_late, passed = mixer_call(
        1, place, factor_late, reads, entering, within_late, gating, norm_gain[None, :], w_out, columns
    )
    got_late = from_sibling(passed)
    relay_top = from_before(add_up(kept[2], got[2]))
    top_after = from_after(add_up(kept[3], got[3]))
    relay_bottom = from_after(add_up(kept_late[2], got_late[2]))
    bottom_before = from_before(add_up(kept_late[1], got_late[1]))
    top_before = from_before(add_up(kept[1], got[1], relay_top))
    bottom_after = from_after(add_up(kept_late[3], got_late[3], relay_bottom))
    capacity = max(2, 2 * rows_keep * 17 // (16 * experts))
    assert capacity == FOLD + 1
    picks = swap(routes).reshape(-1)
    onehot = (picks[:, None] == jnp.arange(experts, dtype=jnp.int32)[None, :]).astype(jnp.int32)
    before = jnp.cumsum(onehot, axis=0) - onehot
    ranked = jnp.sum(before * onehot, axis=1)
    places = jnp.where(
        ranked < FOLD, picks * FOLD + ranked, experts * FOLD + picks
    ).reshape(rows_keep, 2)
    hidden_state, packed = dispatch_call(
        swap(resid).reshape(rows_keep, D),
        moe_gain[None, :],
        places.T,
        (kept, got, kept_late, got_late),
        (top_after, top_before, bottom_before, bottom_after),
        experts,
    )
    arrived = lax.all_to_all(
        packed.reshape(experts, FOLD, D + 128), "seq", split_axis=0, concat_axis=0, tiled=True
    )
    summed = expert_layer(arrived.reshape(packed.shape), w_gate[0], w_up[0], w_down[0])
    returned = lax.all_to_all(
        summed.reshape(experts, FOLD, D + 128), "seq", split_axis=0, concat_axis=0, tiled=True
    )
    combined = combine_call(
        returned.reshape(packed.shape),
        places,
        swap(gates).reshape(rows_keep, 2),
        hidden_state,
        directions,
    )
    return combined


def solution(mesh):
    in_specs = (
        P("seq", None, "exp"),
        P("seq", None, "exp"),
        P("seq", None, "exp"),
        P("seq", None, "exp"),
        P("exp", None, "seq"),
        P("exp", None, "seq"),
        P("exp"),
        P("exp"),
        P("exp", None),
        P(("seq", "exp"), None, None),
        P(),
        P("seq", None, "exp"),
        P("seq", None, "exp"),
        P("seq", "exp", None),
        P(("seq", "exp"), None, None),
        P(("seq", "exp"), None, None),
        P(),
    )
    out_specs = P(("seq", "exp"), None, None)
    return jax.shard_map(
        on_device, mesh=mesh, in_specs=in_specs, out_specs=out_specs, check_vma=False
    )
```

```python
import functools

import jax
import jax.numpy as jnp
from jax import lax
from jax.experimental import pallas as pl
from jax.experimental.pallas import tpu as pltpu
from jax.sharding import PartitionSpec as P

D = 2048
HEADS = 64
HEAD_DIM = 64
STATE = 128
GROUPS = 8
BLOCK = 256
FOLD = 16
F32 = jnp.float32
BF16 = jnp.bfloat16


def dot_last(left, right, **options):
    return lax.dot_general(
        left, right, (((1,), (1,)), ((), ())), preferred_element_type=F32, **options
    )


def two_parts(values):
    high = values.astype(BF16)
    return high, (values - high.astype(F32)).astype(BF16)


def triangle():
    row = lax.broadcasted_iota(jnp.int32, (BLOCK, BLOCK), 0)
    col = lax.broadcasted_iota(jnp.int32, (BLOCK, BLOCK), 1)
    return row >= col


def running_sums(decays):
    heads = decays.shape[0]
    high, rest = two_parts(decays)
    middle, low = two_parts(decays - high.astype(F32))
    parts = jnp.concatenate(
        [high.astype(F32), middle.astype(F32), low.astype(F32)], axis=0
    ).astype(BF16)
    ones = jnp.where(triangle(), 1.0, 0.0).astype(BF16)
    sums = dot_last(parts, ones)
    return sums[:heads] + sums[heads : 2 * heads] + sums[2 * heads :]


def spread_heads(columns, heads):
    rows = columns.shape[0]
    lane = lax.broadcasted_iota(jnp.int32, (rows, 2 * HEAD_DIM), 1)
    pieces = []
    for head in range(0, heads, 2):
        left = jnp.broadcast_to(columns[:, head : head + 1], (rows, 2 * HEAD_DIM))
        right = jnp.broadcast_to(columns[:, head + 1 : head + 2], (rows, 2 * HEAD_DIM))
        pieces.append(jnp.where(lane < HEAD_DIM, left, right))
    return jnp.concatenate(pieces, axis=1)


def over_rows(values):
    heads = values.shape[0]
    return jnp.broadcast_to(values[:, None, :], (heads, HEAD_DIM, STATE)).reshape(
        heads * HEAD_DIM, STATE
    )


def contrib_kernel(decay, step, inputs, writes, parcel, first):
    heads, length = decay.shape[1], decay.shape[2]
    running = total = None
    for start in range(0, length, BLOCK):
        span = slice(start, start + BLOCK)
        cum_row = running_sums(decay[0, :, span])
        end = cum_row[:, BLOCK - 1 :]
        to_end = jnp.transpose(jnp.exp(end - cum_row) * step[0, :, span])
        scaled = (inputs[0, span, :].astype(F32) * spread_heads(to_end, heads)).astype(BF16)
        contrib = lax.dot_general(
            scaled, writes[0, span, :], (((0,), (0,)), ((), ())), preferred_element_type=F32
        )
        end_row = jnp.broadcast_to(end, (heads, STATE))
        if start == 0:
            first[0] = contrib
            running, total = contrib, end_row
        else:
            running = over_rows(jnp.exp(end_row)) * running + contrib
            total = total + end_row
    carried = jnp.exp(total)
    high, rest = two_parts(carried)
    middle, low = two_parts(carried - high.astype(F32))
    row = lax.broadcasted_iota(jnp.int32, (heads, 8, STATE), 1)
    wide = lambda part: jnp.broadcast_to(part.astype(F32)[:, None, :], (heads, 8, STATE))
    extra = jnp.where(
        row == 0,
        wide(high),
        jnp.where(row == 1, wide(middle), jnp.where(row == 2, wide(low), 0.0)),
    )
    parcel[:, :HEAD_DIM, :] = running.reshape(heads, HEAD_DIM, STATE).astype(BF16)
    parcel[:, HEAD_DIM:, :] = extra.astype(BF16)


def contrib_call(decays, steps, inputs, writes):
    seqs, heads, length = decays.shape
    width = inputs.shape[2]
    assert length == 2 * BLOCK
    return pl.pallas_call(
        contrib_kernel,
        grid=(seqs,),
        in_specs=[
            pl.BlockSpec((1, heads, length), lambda b: (b, 0, 0)),
            pl.BlockSpec((1, heads, length), lambda b: (b, 0, 0)),
            pl.BlockSpec((1, length, width), lambda b: (b, 0, 0)),
            pl.BlockSpec((1, length, STATE), lambda b: (b, 0, 0)),
        ],
        out_specs=[
            pl.BlockSpec((heads, HEAD_DIM + 8, STATE), lambda b: (b, 0, 0)),
            pl.BlockSpec((1, width, STATE), lambda b: (b, 0, 0)),
        ],
        out_shape=[
            jax.ShapeDtypeStruct((seqs * heads, HEAD_DIM + 8, STATE), BF16),
            jax.ShapeDtypeStruct((seqs, width, STATE), F32),
        ],
        compiler_params=pltpu.CompilerParams(
            dimension_semantics=("arbitrary",), vmem_limit_bytes=16 * 2**20
        ),
        cost_estimate=pl.CostEstimate(flops=10**9, bytes_accessed=2 * 2**20, transcendentals=8192),
        name="contrib",
    )(decays, steps, inputs, writes)


def within_kernel(decay, step, inputs, writes, reads, skip, first, within, factor):
    block = pl.program_id(0)
    heads = decay.shape[1]
    causal = triangle()
    log2e = 1.4426950408889634
    later = block > 0
    decays = jnp.where(later, decay[0, :, BLOCK:], decay[0, :, :BLOCK])
    ended = jnp.where(later, jnp.sum(decay[0, :, :BLOCK], axis=1, keepdims=True), 0.0)
    plain_row = running_sums(decays)
    factor[0] = jnp.transpose(jnp.exp(plain_row + ended))
    cum_row = plain_row * log2e
    cum_col = jnp.transpose(cum_row)
    steps = step[0]
    scores = dot_last(reads[0], writes[0])
    scores = jnp.where(causal, scores, 0.0)
    quad = 4 * HEAD_DIM
    lane = lax.broadcasted_iota(jnp.int32, (BLOCK, quad), 1)
    for start in range(0, heads, 4):
        columns = inputs[0][:, start * HEAD_DIM : start * HEAD_DIM + quad]
        total = skip[:, start * HEAD_DIM : start * HEAD_DIM + quad] * columns.astype(F32)
        for offset in range(4):
            head = start + offset
            gap = jnp.minimum(cum_col[:, head : head + 1] - cum_row[head : head + 1, :], 0.0)
            weights = (jnp.exp2(gap) * steps[head : head + 1, :] * scores).astype(BF16)
            own = (lane >= offset * HEAD_DIM) & (lane < (offset + 1) * HEAD_DIM)
            total = total + jnp.dot(
                weights,
                jnp.where(own, columns, jnp.zeros_like(columns)),
                preferred_element_type=F32,
            )
        within[0, :, start * HEAD_DIM : start * HEAD_DIM + quad] = total

    @pl.when(later)
    def _():
        high, low = two_parts(first[0])
        readout = dot_last(reads[0], high) + dot_last(reads[0], low)
        within[0] = within[0] + spread_heads(jnp.exp2(cum_col), heads) * readout


def within_call(which, decays, steps, inputs, writes, reads, skip, first):
    seqs, heads, length = decays.shape
    width = inputs.shape[2]
    assert length == 2 * BLOCK
    return pl.pallas_call(
        within_kernel,
        grid=(length // BLOCK,),
        in_specs=[
            pl.BlockSpec((1, heads, length), lambda c: (which, 0, 0)),
            pl.BlockSpec((1, heads, BLOCK), lambda c: (which, 0, c)),
            pl.BlockSpec((1, BLOCK, width), lambda c: (which, c, 0)),
            pl.BlockSpec((1, BLOCK, STATE), lambda c: (which, c, 0)),
            pl.BlockSpec((1, BLOCK, STATE), lambda c: (which, c, 0)),
            pl.BlockSpec((1, width), lambda c: (0, 0)),
            pl.BlockSpec((1, width, STATE), lambda c: (which, 0, 0)),
        ],
        out_specs=[
            pl.BlockSpec((1, BLOCK, width), lambda c: (0, c, 0)),
            pl.BlockSpec((1, BLOCK, heads), lambda c: (0, c, 0)),
        ],
        out_shape=[
            jax.ShapeDtypeStruct((1, length, width), F32),
            jax.ShapeDtypeStruct((1, length, heads), F32),
        ],
        compiler_params=pltpu.CompilerParams(
            dimension_semantics=("arbitrary",), vmem_limit_bytes=16 * 2**20
        ),
        cost_estimate=pl.CostEstimate(
            flops=3 * 10**9, bytes_accessed=2 * 2**20, transcendentals=2**20
        ),
        name="within",
    )(decays, steps, inputs, writes, reads, skip, first)


def scan_kernel(parcels, states):
    ranks = parcels.shape[0]
    state = jnp.zeros((HEAD_DIM, STATE), F32)
    for rank in range(ranks):
        states[rank] = state.astype(BF16)
        if rank < ranks - 1:
            extra = parcels[rank, HEAD_DIM:, :].astype(F32)
            factor = extra[0:1] + extra[1:2] + extra[2:3]
            state = factor * state + parcels[rank, :HEAD_DIM, :].astype(F32)


def scan_call(parcels):
    ranks = parcels.shape[0]
    return pl.pallas_call(
        scan_kernel,
        out_shape=jax.ShapeDtypeStruct((ranks, HEAD_DIM, STATE), BF16),
        cost_estimate=pl.CostEstimate(flops=10**6, bytes_accessed=2**19, transcendentals=0),
        name="scan",
    )(parcels)


def mixer_kernel(
    place, factors, reads, entering, within, gate, gain, weight, kept, passed, held, sems
):
    block = pl.program_id(0)
    blocks = pl.num_programs(0)
    heads = factors.shape[2]
    width = gate.shape[2]
    chips, keep = kept.shape[0], kept.shape[1]
    readout = dot_last(reads[0], entering[...].reshape(width, STATE))
    ssd_out = within[0] + spread_heads(factors[0], heads) * readout
    gates = gate[0].astype(F32)
    gated = ssd_out * (gates / (1.0 + jnp.exp(-gates)))
    factor = lax.rsqrt(jnp.mean(gated * gated, axis=-1, keepdims=True) + 1e-05)
    normed = (gated * factor * gain[...]).astype(BF16)

    @pl.loop(0, D // 512)
    def _(index):
        span = pl.ds(pl.multiple_of(index * 512, 512), 512)
        product = jnp.dot(normed, weight[:, span], preferred_element_type=F32).astype(BF16)
        held[block, :, :, span] = product.reshape(held.shape[1], keep, 512)

    pieces = held.shape[1]
    chip, core = lax.div(place[0], 2), lax.rem(place[0], 2)

    def piece(step, index, target):
        distance = lax.rem(step * (pieces // 2) + index // 2 - chip + chips, chips)
        return pltpu.make_async_copy(
            held.at[step, index], target.at[distance], sems.at[step, index]
        )

    for index in range(pieces):

        @pl.when(core == index % 2)
        def _():
            piece(block, index, kept).start()

        @pl.when(core != index % 2)
        def _():
            piece(block, index, passed).start()

    @pl.when(block == blocks - 1)
    def _():
        for step in range(held.shape[0]):
            for index in range(pieces):
                piece(step, index, kept).wait()


def mixer_call(which, place, factors, reads, entering, within, gate, gain, weight, columns):
    _, length, heads = factors.shape
    width = gate.shape[2]
    blocks = length // BLOCK
    keep = length // columns
    anywhere = pl.BlockSpec(memory_space=pl.ANY)
    return pl.pallas_call(
        mixer_kernel,
        grid=(blocks,),
        in_specs=[
            pl.BlockSpec(memory_space=pltpu.SMEM),
            pl.BlockSpec((1, BLOCK, heads), lambda c: (0, c, 0)),
            pl.BlockSpec((1, BLOCK, STATE), lambda c: (which, c, 0)),
            pl.BlockSpec((heads, HEAD_DIM, STATE), lambda c: (which, 0, 0)),
            pl.BlockSpec((1, BLOCK, width), lambda c: (0, c, 0)),
            pl.BlockSpec((1, BLOCK, width), lambda c: (which, c, 0)),
            pl.BlockSpec((1, width), lambda c: (0, 0)),
            pl.BlockSpec(memory_space=pltpu.VMEM),
        ],
        out_specs=[anywhere, anywhere],
        out_shape=[jax.ShapeDtypeStruct((columns // 2, keep, D), BF16)] * 2,
        scratch_shapes=[
            pltpu.VMEM((blocks, columns // blocks, keep, D), BF16),
            pltpu.SemaphoreType.DMA((blocks, columns // blocks)),
        ],
        compiler_params=pltpu.CompilerParams(
            dimension_semantics=("arbitrary",), vmem_limit_bytes=16 * 2**20
        ),
        cost_estimate=pl.CostEstimate(
            flops=2 * 10**9, bytes_accessed=6 * 2**20, transcendentals=2**18
        ),
        name="mixer",
    )(place, factors, reads, entering, within, gate, gain, weight)


def unfold(rows, folded):
    pieces = [folded[pl.ds(part, rows, stride=FOLD), :].astype(BF16) for part in range(FOLD)]
    return jnp.concatenate(pieces, axis=1)


def fold(values, folded):
    rows = values.shape[0]
    for part in range(FOLD):
        folded[pl.ds(part, rows, stride=FOLD), :] = values[:, part * 128 : (part + 1) * 128]


def dispatch_kernel(
    residual, gain, places, own_top, got_top, own_bottom, got_bottom, *refs
):
    others = refs[:4]
    hidden, packed, folded = refs[4:]
    half = own_top.shape[1]
    for index, (own, got) in enumerate(((own_top, got_top), (own_bottom, got_bottom))):
        span = pl.ds(index * half, half)
        hidden[span, :] = (
            residual[span, :].astype(F32)
            + (own[0].astype(F32) + got[0].astype(F32))
            + others[2 * index][...].astype(F32)
            + others[2 * index + 1][...].astype(F32)
        )
    state = hidden[...]
    scale = lax.rsqrt(jnp.mean(state * state, axis=-1, keepdims=True) + 1e-05)
    moe_in = (state * scale * gain[...]).astype(BF16)
    rows = packed.shape[0]
    slot = lax.broadcasted_iota(jnp.int32, (rows + rows // FOLD, state.shape[0]), 0)
    chosen = (slot == places[0:1, :]) | (slot == places[1:2, :])
    select = jnp.where(chosen, 1.0, 0.0).astype(BF16)
    slots = jnp.dot(select, moe_in, preferred_element_type=F32)
    packed[:, :D] = slots[:rows].astype(BF16)
    fold(slots[rows:], folded)
    packed[:, D:] = folded[...].astype(BF16)


def dispatch_call(residual, gain, places, owns, others, experts):
    rows, half = residual.shape[0], residual.shape[0] // 2
    count = experts * FOLD
    whole = lambda shape: pl.BlockSpec(shape, lambda i: (0,) * len(shape))
    return pl.pallas_call(
        dispatch_kernel,
        grid=(1,),
        in_specs=[whole(residual.shape), whole(gain.shape), whole(places.shape)]
        + [whole((1, half, D))] * 4
        + [whole((half, D))] * 4,
        out_specs=[whole((rows, D)), whole((count, D + 128))],
        out_shape=[
            jax.ShapeDtypeStruct((rows, D), F32),
            jax.ShapeDtypeStruct((count, D + 128), BF16),
        ],
        scratch_shapes=[pltpu.VMEM((count, 128), F32)],
        compiler_params=pltpu.CompilerParams(vmem_limit_bytes=24 * 2**20),
        cost_estimate=pl.CostEstimate(
            flops=2 * 10**8, bytes_accessed=5 * 2**20, transcendentals=0
        ),
        name="dispatch",
    )(residual, gain, places, *owns, *others)


def combine_kernel(returned, places, gates, hidden, directions, out, folded, values):
    slots, rows = values.shape[0], hidden.shape[0]
    count = returned.shape[0]
    folded[...] = returned[:, D:].astype(F32)
    values[:count, :] = returned[:, :D]
    values[count:, :] = unfold(slots - count, folded)
    slot = lax.broadcasted_iota(jnp.int32, (rows, slots), 1)
    zero = jnp.zeros((rows, slots), F32)
    mix = jnp.where(slot == places[:, 0:1], gates[:, 0:1], zero) + jnp.where(
        slot == places[:, 1:2], gates[:, 1:2], zero
    )
    high, rest = two_parts(mix)
    middle, low = two_parts(mix - high.astype(F32))
    parts = jnp.concatenate([high, middle, low], axis=0)
    product = jnp.dot(parts, values[...], preferred_element_type=F32)
    combined = hidden[...] + (
        product[:rows] + product[rows : 2 * rows] + product[2 * rows :]
    )
    for index in range(directions.shape[0]):
        direction = directions[index : index + 1, :]
        norm = jnp.sum(direction * direction, axis=1, keepdims=True) + 1e-06
        along = jnp.sum(combined * direction, axis=1, keepdims=True) / norm
        combined = combined - along * direction
    half = rows // 2
    out[:, 0, :] = combined[:half].astype(BF16)
    out[:, 1, :] = combined[half:].astype(BF16)


def combine_call(returned, places, gates, hidden, directions):
    rows = hidden.shape[0]
    count = returned.shape[0]
    return pl.pallas_call(
        combine_kernel,
        out_shape=jax.ShapeDtypeStruct((rows // 2, 2, D), BF16),
        scratch_shapes=[
            pltpu.VMEM((count, 128), F32),
            pltpu.VMEM((count + count // FOLD, D), BF16),
        ],
        compiler_params=pltpu.CompilerParams(vmem_limit_bytes=24 * 2**20),
        cost_estimate=pl.CostEstimate(flops=10**9, bytes_accessed=4 * 2**20, transcendentals=0),
        name="combine",
    )(returned, places, gates, hidden, directions)


def expert_kernel(counts, *refs):
    number = len(counts)
    parts = refs[:number]
    gate, up, down, kept, passed = refs[number : number + 5]
    values, extra, folded, hidden, tail, main_sems, extra_sems = refs[number + 5 :]
    places = [sum(counts[:index]) for index in range(number)]
    count = sum(counts)
    lone = count // FOLD
    loads, extras = [], []
    for index, (part, place, size) in enumerate(zip(parts, places, counts)):
        span = pl.ds(place, size)
        extras.append(
            pltpu.make_async_copy(
                part.at[:, pl.ds(D, 128)], extra.at[span, :], extra_sems.at[index]
            )
        )
        loads.append(
            pltpu.make_async_copy(
                part.at[:, pl.ds(0, D)], values.at[span, :], main_sems.at[index]
            )
        )
    for load in extras + loads:
        load.start()
    for load in extras:
        load.wait()
    folded[...] = extra[...].astype(F32)
    values[count:, :] = unfold(lone, folded)
    for load in loads:
        load.wait()
    units = down.shape[0]
    whole = units // 256 * 256

    def open_units(start, size):
        span = pl.ds(start, size)
        first = jnp.dot(values[...], gate[:, span], preferred_element_type=F32)
        second = jnp.dot(values[...], up[:, span], preferred_element_type=F32)
        hidden[:, span] = (first / (1.0 + jnp.exp(-first)) * second).astype(BF16)

    @pl.loop(0, whole // 256)
    def _(index):
        open_units(pl.multiple_of(index * 256, 256), 256)

    if units > whole:
        open_units(whole, units - whole)
    half = kept.shape[0]

    @pl.loop(0, D // 1024)
    def _(index):
        span = pl.ds(pl.multiple_of(index * 1024, 1024), 1024)
        result = jnp.dot(hidden[...], down[:, span], preferred_element_type=F32)
        kept[:, span] = result[:half].astype(BF16)
        passed[:, span] = result[half:count].astype(BF16)
        tail[:, span] = result[count:]

    fold(tail[...], folded)
    kept[:, D:] = folded[:half, :].astype(BF16)
    passed[:, D:] = folded[half:, :].astype(BF16)


def expert_call(parts, gate, up, down):
    counts = tuple(part.shape[0] for part in parts)
    count = sum(counts)
    rows = count + count // FOLD
    units = down.shape[0]
    anywhere = pl.BlockSpec(memory_space=pl.ANY)
    near = pl.BlockSpec(memory_space=pltpu.VMEM)
    return pl.pallas_call(
        functools.partial(expert_kernel, counts),
        in_specs=[anywhere] * len(parts) + [near] * 3,
        out_specs=[near, near],
        out_shape=[jax.ShapeDtypeStruct((count // 2, D + 128), BF16)] * 2,
        scratch_shapes=[
            pltpu.VMEM((rows, D), BF16),
            pltpu.VMEM((count, 128), BF16),
            pltpu.VMEM((count, 128), F32),
            pltpu.VMEM((rows, units), BF16),
            pltpu.VMEM((count // FOLD, D), F32),
            pltpu.SemaphoreType.DMA((len(parts),)),
            pltpu.SemaphoreType.DMA((len(parts),)),
        ],
        compiler_params=pltpu.CompilerParams(vmem_limit_bytes=24 * 2**20),
        cost_estimate=pl.CostEstimate(
            flops=6 * rows * D * units,
            bytes_accessed=4 * rows * D + 6 * D * units,
            transcendentals=rows * units,
        ),
        name="expert",
    )(*parts, gate, up, down)


def settle_kernel(kept, got, top_after, top_before, bottom_before, bottom_after, out):
    half = top_after.shape[0]
    for index, others in enumerate(((top_after, top_before), (bottom_before, bottom_after))):
        span = pl.ds(index * half, half)
        total = kept[span, :].astype(F32) + got[span, :].astype(F32)
        for other in others:
            total = total + other[...].astype(F32)
        out[span, :] = total.astype(BF16)


def settle_call(*arrays):
    return pl.pallas_call(
        settle_kernel,
        out_shape=jax.ShapeDtypeStruct(arrays[0].shape, BF16),
        compiler_params=pltpu.CompilerParams(vmem_limit_bytes=16 * 2**20),
        cost_estimate=pl.CostEstimate(flops=2 * 10**6, bytes_accessed=5 * 2**20, transcendentals=0),
        name="settle",
    )(*arrays)


def from_before(values):
    size = lax.axis_size("exp")
    return lax.ppermute(values, "exp", [(i, (i + 2) % size) for i in range(size)])


def from_after(values):
    size = lax.axis_size("exp")
    return lax.ppermute(values, "exp", [(i, (i - 2) % size) for i in range(size)])


def from_sibling(values):
    size = lax.axis_size("exp")
    return lax.ppermute(values, "exp", [(i, i ^ 1) for i in range(size)])


def add_up(*terms):
    total = terms[0].astype(F32)
    for term in terms[1:]:
        total = total + term.astype(F32)
    return total.astype(BF16)


def after(values, *earlier):
    return lax.optimization_barrier((tuple(values), earlier))[0]


def expert_layer(own, gate, up, down):
    half = own.shape[0] // 2
    top, bottom = own[:half], own[half:]
    own_other = from_sibling(own)
    before_top = from_before(top)
    after_bottom = from_after(bottom)
    call = functools.partial(expert_call, gate=gate, up=up, down=down)
    kept_own, passed = call((own, own_other))
    before_top, after_bottom, kept_own, passed, top, bottom = after(
        (before_top, after_bottom, kept_own, passed, top, bottom)
    )
    got_own = from_sibling(passed)
    others = from_sibling(before_top), from_sibling(after_bottom)
    far_top = from_before(before_top)
    far_bottom = from_after(after_bottom)
    before_bottom = from_before(bottom)
    after_top = from_after(top)
    kept, passed = call((before_top, after_bottom, *others))
    far_top, far_bottom, got_own, kept, passed = after(
        (far_top, far_bottom, got_own, kept, passed)
    )
    got = from_sibling(passed)
    others = from_sibling(far_top), from_sibling(far_bottom)
    near_top, near_bottom = add_up(kept[:half], got[:half]), add_up(kept[half:], got[half:])
    kept_top, kept_bottom = call((far_top, far_bottom))
    others = after(others, near_top, near_bottom, kept_top)
    top_after = from_after(near_top)
    bottom_before = from_before(near_bottom)
    passed_top, passed_bottom = call(others)
    late = from_sibling(after_top), from_sibling(before_bottom)
    far_top = add_up(kept_top, from_sibling(passed_top))
    far_bottom = add_up(kept_bottom, from_sibling(passed_bottom))
    far_top, far_bottom, after_top, before_bottom = after(
        (far_top, far_bottom, after_top, before_bottom)
    )
    relay_top = from_before(far_top)
    relay_bottom = from_after(far_bottom)
    kept, passed = call((after_top, before_bottom, *late))
    relay_top, relay_bottom, top_after, bottom_before, kept, passed = after(
        (relay_top, relay_bottom, top_after, bottom_before, kept, passed)
    )
    got = from_sibling(passed)
    top_before = from_before(add_up(kept[:half], got[:half], relay_top))
    bottom_after = from_after(add_up(kept[half:], got[half:], relay_bottom))
    return settle_call(
        kept_own, got_own, top_after, top_before, bottom_before, bottom_after
    )


def on_device(
    ssd_input,
    ssd_gate,
    state_write,
    state_read,
    step_size,
    decay_log,
    skip_gain,
    norm_gain,
    w_out,
    resid,
    moe_gain,
    w_gate,
    w_up,
    w_down,
    routes,
    gates,
    directions,
):
    length_dev, seqs, width_dev = ssd_input.shape
    heads_dev = decay_log.shape[0]
    experts = lax.axis_size("seq")
    columns = lax.axis_size("exp")
    rows_keep = length_dev * seqs // columns

    def swap(values):
        return jnp.transpose(values, (1, 0, 2))

    decays, steps = swap(decay_log), swap(step_size)
    inputs, writes, reads = swap(ssd_input), swap(state_write), swap(state_read)
    parcel, first = contrib_call(decays, steps, inputs, writes)
    parcels = lax.all_to_all(parcel, "seq", split_axis=0, concat_axis=0, tiled=True)
    skip = jnp.repeat(skip_gain, HEAD_DIM)[None, :]
    within_early, factor_early = within_call(
        0, decays, steps, inputs, writes, reads, skip, first
    )
    (parcels,) = after((parcels,), within_early)
    entering = lax.all_to_all(
        scan_call(parcels), "seq", split_axis=0, concat_axis=0, tiled=True
    )
    within_late, factor_late = within_call(
        1, decays, steps, inputs, writes, reads, skip, first
    )
    gating = swap(ssd_gate)
    (entering,) = after((entering,), within_late, gating)
    place = lax.axis_index("exp").astype(jnp.int32)[None]
    kept, passed = mixer_call(
        0, place, factor_early, reads, entering, within_early, gating, norm_gain[None, :], w_out, columns
    )
    got = from_sibling(passed)
    (place,) = after((place,), kept)
    kept_late, passed = mixer_call(
        1, place, factor_late, reads, entering, within_late, gating, norm_gain[None, :], w_out, columns
    )
    got_late = from_sibling(passed)
    relay_top = from_before(add_up(kept[2], got[2]))
    top_after = from_after(add_up(kept[3], got[3]))
    relay_bottom = from_after(add_up(kept_late[2], got_late[2]))
    bottom_before = from_before(add_up(kept_late[1], got_late[1]))
    top_before = from_before(add_up(kept[1], got[1], relay_top))
    bottom_after = from_after(add_up(kept_late[3], got_late[3], relay_bottom))
    capacity = max(2, 2 * rows_keep * 17 // (16 * experts))
    assert capacity == FOLD + 1
    picks = swap(routes).reshape(-1)
    onehot = (picks[:, None] == jnp.arange(experts, dtype=jnp.int32)[None, :]).astype(jnp.int32)
    before = jnp.cumsum(onehot, axis=0) - onehot
    ranked = jnp.sum(before * onehot, axis=1)
    places = jnp.where(
        ranked < FOLD, picks * FOLD + ranked, experts * FOLD + picks
    ).reshape(rows_keep, 2)
    hidden_state, packed = dispatch_call(
        swap(resid).reshape(rows_keep, D),
        moe_gain[None, :],
        places.T,
        (kept, got, kept_late, got_late),
        (top_after, top_before, bottom_before, bottom_after),
        experts,
    )
    arrived = lax.all_to_all(
        packed.reshape(experts, FOLD, D + 128), "seq", split_axis=0, concat_axis=0, tiled=True
    )
    summed = expert_layer(arrived.reshape(packed.shape), w_gate[0], w_up[0], w_down[0])
    returned = lax.all_to_all(
        summed.reshape(experts, FOLD, D + 128), "seq", split_axis=0, concat_axis=0, tiled=True
    )
    combined = combine_call(
        returned.reshape(packed.shape),
        places,
        swap(gates).reshape(rows_keep, 2),
        hidden_state,
        directions,
    )
    return combined


def solution(mesh):
    in_specs = (
        P("seq", None, "exp"),
        P("seq", None, "exp"),
        P("seq", None, "exp"),
        P("seq", None, "exp"),
        P("exp", None, "seq"),
        P("exp", None, "seq"),
        P("exp"),
        P("exp"),
        P("exp", None),
        P(("seq", "exp"), None, None),
        P(),
        P("seq", None, "exp"),
        P("seq", None, "exp"),
        P("seq", "exp", None),
        P(("seq", "exp"), None, None),
        P(("seq", "exp"), None, None),
        P(),
    )
    out_specs = P(("seq", "exp"), None, None)
    return jax.shard_map(
        on_device, mesh=mesh, in_specs=in_specs, out_specs=out_specs, check_vma=False
    )
```

```python
import functools

import jax
import jax.numpy as jnp
from jax import lax
from jax.experimental import pallas as pl
from jax.experimental.pallas import tpu as pltpu
from jax.sharding import PartitionSpec as P

D = 2048
HEADS = 64
HEAD_DIM = 64
STATE = 128
GROUPS = 8
BLOCK = 256
FOLD = 16
F32 = jnp.float32
BF16 = jnp.bfloat16


def dot_last(left, right, **options):
    return lax.dot_general(
        left, right, (((1,), (1,)), ((), ())), preferred_element_type=F32, **options
    )


def two_parts(values):
    high = values.astype(BF16)
    return high, (values - high.astype(F32)).astype(BF16)


def triangle():
    row = lax.broadcasted_iota(jnp.int32, (BLOCK, BLOCK), 0)
    col = lax.broadcasted_iota(jnp.int32, (BLOCK, BLOCK), 1)
    return row >= col


def running_sums(decays):
    heads = decays.shape[0]
    high, rest = two_parts(decays)
    middle, low = two_parts(decays - high.astype(F32))
    parts = jnp.concatenate(
        [high.astype(F32), middle.astype(F32), low.astype(F32)], axis=0
    ).astype(BF16)
    ones = jnp.where(triangle(), 1.0, 0.0).astype(BF16)
    sums = dot_last(parts, ones)
    return sums[:heads] + sums[heads : 2 * heads] + sums[2 * heads :]


def spread_heads(columns, heads):
    rows = columns.shape[0]
    lane = lax.broadcasted_iota(jnp.int32, (rows, 2 * HEAD_DIM), 1)
    pieces = []
    for head in range(0, heads, 2):
        left = jnp.broadcast_to(columns[:, head : head + 1], (rows, 2 * HEAD_DIM))
        right = jnp.broadcast_to(columns[:, head + 1 : head + 2], (rows, 2 * HEAD_DIM))
        pieces.append(jnp.where(lane < HEAD_DIM, left, right))
    return jnp.concatenate(pieces, axis=1)


def over_rows(values):
    heads = values.shape[0]
    return jnp.broadcast_to(values[:, None, :], (heads, HEAD_DIM, STATE)).reshape(
        heads * HEAD_DIM, STATE
    )


def contrib_kernel(decay, step, inputs, writes, parcel, first):
    heads, length = decay.shape[1], decay.shape[2]
    running = total = None
    for start in range(0, length, BLOCK):
        span = slice(start, start + BLOCK)
        cum_row = running_sums(decay[0, :, span])
        end = cum_row[:, BLOCK - 1 :]
        to_end = jnp.transpose(jnp.exp(end - cum_row) * step[0, :, span])
        scaled = (inputs[0, span, :].astype(F32) * spread_heads(to_end, heads)).astype(BF16)
        contrib = lax.dot_general(
            scaled, writes[0, span, :], (((0,), (0,)), ((), ())), preferred_element_type=F32
        )
        end_row = jnp.broadcast_to(end, (heads, STATE))
        if start == 0:
            first[0] = contrib
            running, total = contrib, end_row
        else:
            running = over_rows(jnp.exp(end_row)) * running + contrib
            total = total + end_row
    carried = jnp.exp(total)
    high, rest = two_parts(carried)
    middle, low = two_parts(carried - high.astype(F32))
    row = lax.broadcasted_iota(jnp.int32, (heads, 8, STATE), 1)
    wide = lambda part: jnp.broadcast_to(part.astype(F32)[:, None, :], (heads, 8, STATE))
    extra = jnp.where(
        row == 0,
        wide(high),
        jnp.where(row == 1, wide(middle), jnp.where(row == 2, wide(low), 0.0)),
    )
    parcel[:, :HEAD_DIM, :] = running.reshape(heads, HEAD_DIM, STATE).astype(BF16)
    parcel[:, HEAD_DIM:, :] = extra.astype(BF16)


def contrib_call(decays, steps, inputs, writes):
    seqs, heads, length = decays.shape
    width = inputs.shape[2]
    assert length == 2 * BLOCK
    return pl.pallas_call(
        contrib_kernel,
        grid=(seqs,),
        in_specs=[
            pl.BlockSpec((1, heads, length), lambda b: (b, 0, 0)),
            pl.BlockSpec((1, heads, length), lambda b: (b, 0, 0)),
            pl.BlockSpec((1, length, width), lambda b: (b, 0, 0)),
            pl.BlockSpec((1, length, STATE), lambda b: (b, 0, 0)),
        ],
        out_specs=[
            pl.BlockSpec((heads, HEAD_DIM + 8, STATE), lambda b: (b, 0, 0)),
            pl.BlockSpec((1, width, STATE), lambda b: (b, 0, 0)),
        ],
        out_shape=[
            jax.ShapeDtypeStruct((seqs * heads, HEAD_DIM + 8, STATE), BF16),
            jax.ShapeDtypeStruct((seqs, width, STATE), F32),
        ],
        compiler_params=pltpu.CompilerParams(
            dimension_semantics=("arbitrary",), vmem_limit_bytes=16 * 2**20
        ),
        cost_estimate=pl.CostEstimate(flops=10**9, bytes_accessed=2 * 2**20, transcendentals=8192),
        name="contrib",
    )(decays, steps, inputs, writes)


def within_kernel(decay, step, inputs, writes, reads, skip, first, within, factor):
    block = pl.program_id(0)
    heads = decay.shape[1]
    causal = triangle()
    log2e = 1.4426950408889634
    later = block > 0
    decays = jnp.where(later, decay[0, :, BLOCK:], decay[0, :, :BLOCK])
    ended = jnp.where(later, jnp.sum(decay[0, :, :BLOCK], axis=1, keepdims=True), 0.0)
    plain_row = running_sums(decays)
    factor[0] = jnp.transpose(jnp.exp(plain_row + ended))
    cum_row = plain_row * log2e
    cum_col = jnp.transpose(cum_row)
    steps = step[0]
    scores = dot_last(reads[0], writes[0])
    scores = jnp.where(causal, scores, 0.0)
    quad = 4 * HEAD_DIM
    lane = lax.broadcasted_iota(jnp.int32, (BLOCK, quad), 1)
    for start in range(0, heads, 4):
        columns = inputs[0][:, start * HEAD_DIM : start * HEAD_DIM + quad]
        total = skip[:, start * HEAD_DIM : start * HEAD_DIM + quad] * columns.astype(F32)
        for offset in range(4):
            head = start + offset
            gap = jnp.minimum(cum_col[:, head : head + 1] - cum_row[head : head + 1, :], 0.0)
            weights = (jnp.exp2(gap) * steps[head : head + 1, :] * scores).astype(BF16)
            own = (lane >= offset * HEAD_DIM) & (lane < (offset + 1) * HEAD_DIM)
            total = total + jnp.dot(
                weights,
                jnp.where(own, columns, jnp.zeros_like(columns)),
                preferred_element_type=F32,
            )
        within[0, :, start * HEAD_DIM : start * HEAD_DIM + quad] = total

    @pl.when(later)
    def _():
        high, low = two_parts(first[0])
        readout = dot_last(reads[0], high) + dot_last(reads[0], low)
        within[0] = within[0] + spread_heads(jnp.exp2(cum_col), heads) * readout


def within_call(which, decays, steps, inputs, writes, reads, skip, first):
    seqs, heads, length = decays.shape
    width = inputs.shape[2]
    assert length == 2 * BLOCK
    return pl.pallas_call(
        within_kernel,
        grid=(length // BLOCK,),
        in_specs=[
            pl.BlockSpec((1, heads, length), lambda c: (which, 0, 0)),
            pl.BlockSpec((1, heads, BLOCK), lambda c: (which, 0, c)),
            pl.BlockSpec((1, BLOCK, width), lambda c: (which, c, 0)),
            pl.BlockSpec((1, BLOCK, STATE), lambda c: (which, c, 0)),
            pl.BlockSpec((1, BLOCK, STATE), lambda c: (which, c, 0)),
            pl.BlockSpec((1, width), lambda c: (0, 0)),
            pl.BlockSpec((1, width, STATE), lambda c: (which, 0, 0)),
        ],
        out_specs=[
            pl.BlockSpec((1, BLOCK, width), lambda c: (0, c, 0)),
            pl.BlockSpec((1, BLOCK, heads), lambda c: (0, c, 0)),
        ],
        out_shape=[
            jax.ShapeDtypeStruct((1, length, width), F32),
            jax.ShapeDtypeStruct((1, length, heads), F32),
        ],
        compiler_params=pltpu.CompilerParams(
            dimension_semantics=("arbitrary",), vmem_limit_bytes=16 * 2**20
        ),
        cost_estimate=pl.CostEstimate(
            flops=3 * 10**9, bytes_accessed=2 * 2**20, transcendentals=2**20
        ),
        name="within",
    )(decays, steps, inputs, writes, reads, skip, first)


def scan_kernel(parcels, states):
    ranks = parcels.shape[0]
    state = jnp.zeros((HEAD_DIM, STATE), F32)
    for rank in range(ranks):
        states[rank] = state.astype(BF16)
        if rank < ranks - 1:
            extra = parcels[rank, HEAD_DIM:, :].astype(F32)
            factor = extra[0:1] + extra[1:2] + extra[2:3]
            state = factor * state + parcels[rank, :HEAD_DIM, :].astype(F32)


def scan_call(parcels):
    ranks = parcels.shape[0]
    return pl.pallas_call(
        scan_kernel,
        out_shape=jax.ShapeDtypeStruct((ranks, HEAD_DIM, STATE), BF16),
        cost_estimate=pl.CostEstimate(flops=10**6, bytes_accessed=2**19, transcendentals=0),
        name="scan",
    )(parcels)


def mixer_kernel(
    place, factors, reads, entering, within, gate, gain, weight, kept, passed, held, sems
):
    block = pl.program_id(0)
    blocks = pl.num_programs(0)
    heads = factors.shape[2]
    width = gate.shape[2]
    chips, keep = kept.shape[0], kept.shape[1]
    readout = dot_last(reads[0], entering[...].reshape(width, STATE))
    ssd_out = within[0] + spread_heads(factors[0], heads) * readout
    gates = gate[0].astype(F32)
    gated = ssd_out * (gates / (1.0 + jnp.exp(-gates)))
    factor = lax.rsqrt(jnp.mean(gated * gated, axis=-1, keepdims=True) + 1e-05)
    normed = (gated * factor * gain[...]).astype(BF16)
    product = jnp.dot(normed, weight[...], preferred_element_type=F32).astype(BF16)
    held[block] = product.reshape(held.shape[1], keep, D)
    pieces = held.shape[1]
    chip, core = lax.div(place[0], 2), lax.rem(place[0], 2)

    def piece(step, index, target):
        distance = lax.rem(step * (pieces // 2) + index // 2 - chip + chips, chips)
        return pltpu.make_async_copy(
            held.at[step, index], target.at[distance], sems.at[step, index]
        )

    for index in range(pieces):

        @pl.when(core == index % 2)
        def _():
            piece(block, index, kept).start()

        @pl.when(core != index % 2)
        def _():
            piece(block, index, passed).start()

    @pl.when(block == blocks - 1)
    def _():
        for step in range(held.shape[0]):
            for index in range(pieces):
                piece(step, index, kept).wait()


def mixer_call(which, place, factors, reads, entering, within, gate, gain, weight, columns):
    _, length, heads = factors.shape
    width = gate.shape[2]
    blocks = length // BLOCK
    keep = length // columns
    anywhere = pl.BlockSpec(memory_space=pl.ANY)
    return pl.pallas_call(
        mixer_kernel,
        grid=(blocks,),
        in_specs=[
            pl.BlockSpec(memory_space=pltpu.SMEM),
            pl.BlockSpec((1, BLOCK, heads), lambda c: (0, c, 0)),
            pl.BlockSpec((1, BLOCK, STATE), lambda c: (which, c, 0)),
            pl.BlockSpec((heads, HEAD_DIM, STATE), lambda c: (which, 0, 0)),
            pl.BlockSpec((1, BLOCK, width), lambda c: (0, c, 0)),
            pl.BlockSpec((1, BLOCK, width), lambda c: (which, c, 0)),
            pl.BlockSpec((1, width), lambda c: (0, 0)),
            pl.BlockSpec(memory_space=pltpu.VMEM),
        ],
        out_specs=[anywhere, anywhere],
        out_shape=[jax.ShapeDtypeStruct((columns // 2, keep, D), BF16)] * 2,
        scratch_shapes=[
            pltpu.VMEM((blocks, columns // blocks, keep, D), BF16),
            pltpu.SemaphoreType.DMA((blocks, columns // blocks)),
        ],
        compiler_params=pltpu.CompilerParams(
            dimension_semantics=("arbitrary",), vmem_limit_bytes=16 * 2**20
        ),
        cost_estimate=pl.CostEstimate(
            flops=2 * 10**9, bytes_accessed=6 * 2**20, transcendentals=2**18
        ),
        name="mixer",
    )(place, factors, reads, entering, within, gate, gain, weight)


def unfold(rows, folded):
    pieces = [folded[pl.ds(part, rows, stride=FOLD), :].astype(BF16) for part in range(FOLD)]
    return jnp.concatenate(pieces, axis=1)


def fold(values, folded):
    rows = values.shape[0]
    for part in range(FOLD):
        folded[pl.ds(part, rows, stride=FOLD), :] = values[:, part * 128 : (part + 1) * 128]


def dispatch_kernel(
    residual, gain, places, own_top, got_top, own_bottom, got_bottom, *refs
):
    others = refs[:4]
    hidden, packed, folded = refs[4:]
    half = own_top.shape[1]
    for index, (own, got) in enumerate(((own_top, got_top), (own_bottom, got_bottom))):
        span = pl.ds(index * half, half)
        hidden[span, :] = (
            residual[:, index, :].astype(F32)
            + (own[0].astype(F32) + got[0].astype(F32))
            + others[2 * index][...].astype(F32)
            + others[2 * index + 1][...].astype(F32)
        )
    state = hidden[...]
    scale = lax.rsqrt(jnp.mean(state * state, axis=-1, keepdims=True) + 1e-05)
    moe_in = (state * scale * gain[...]).astype(BF16)
    rows = packed.shape[0]
    slot = lax.broadcasted_iota(jnp.int32, (rows + rows // FOLD, state.shape[0]), 0)
    chosen = (slot == places[0:1, :]) | (slot == places[1:2, :])
    select = jnp.where(chosen, 1.0, 0.0).astype(BF16)
    slots = jnp.dot(select, moe_in, preferred_element_type=F32)
    packed[:, :D] = slots[:rows].astype(BF16)
    fold(slots[rows:], folded)
    packed[:, D:] = folded[...].astype(BF16)


def dispatch_call(residual, gain, places, owns, others, experts):
    rows, half = 2 * residual.shape[0], residual.shape[0]
    count = experts * FOLD
    whole = lambda shape: pl.BlockSpec(shape, lambda i: (0,) * len(shape))
    return pl.pallas_call(
        dispatch_kernel,
        grid=(1,),
        in_specs=[whole(residual.shape), whole(gain.shape), whole(places.shape)]
        + [whole((1, half, D))] * 4
        + [whole((half, D))] * 4,
        out_specs=[whole((rows, D)), whole((count, D + 128))],
        out_shape=[
            jax.ShapeDtypeStruct((rows, D), F32),
            jax.ShapeDtypeStruct((count, D + 128), BF16),
        ],
        scratch_shapes=[pltpu.VMEM((count, 128), F32)],
        compiler_params=pltpu.CompilerParams(vmem_limit_bytes=24 * 2**20),
        cost_estimate=pl.CostEstimate(
            flops=2 * 10**8, bytes_accessed=5 * 2**20, transcendentals=0
        ),
        name="dispatch",
    )(residual, gain, places, *owns, *others)


def combine_kernel(returned, places, gates, hidden, directions, out, folded, values):
    slots, rows = values.shape[0], hidden.shape[0]
    count = returned.shape[0]
    folded[...] = returned[:, D:].astype(F32)
    values[:count, :] = returned[:, :D]
    values[count:, :] = unfold(slots - count, folded)
    slot = lax.broadcasted_iota(jnp.int32, (rows, slots), 1)
    zero = jnp.zeros((rows, slots), F32)
    mix = jnp.where(slot == places[:, 0:1], gates[:, 0:1], zero) + jnp.where(
        slot == places[:, 1:2], gates[:, 1:2], zero
    )
    high, rest = two_parts(mix)
    middle, low = two_parts(mix - high.astype(F32))
    parts = jnp.concatenate([high, middle, low], axis=0)
    product = jnp.dot(parts, values[...], preferred_element_type=F32)
    combined = hidden[...] + (
        product[:rows] + product[rows : 2 * rows] + product[2 * rows :]
    )
    for index in range(directions.shape[0]):
        direction = directions[index : index + 1, :]
        norm = jnp.sum(direction * direction, axis=1, keepdims=True) + 1e-06
        along = jnp.sum(combined * direction, axis=1, keepdims=True) / norm
        combined = combined - along * direction
    half = rows // 2
    out[:, 0, :] = combined[:half].astype(BF16)
    out[:, 1, :] = combined[half:].astype(BF16)


def combine_call(returned, places, gates, hidden, directions):
    rows = hidden.shape[0]
    count = returned.shape[0]
    return pl.pallas_call(
        combine_kernel,
        out_shape=jax.ShapeDtypeStruct((rows // 2, 2, D), BF16),
        scratch_shapes=[
            pltpu.VMEM((count, 128), F32),
            pltpu.VMEM((count + count // FOLD, D), BF16),
        ],
        compiler_params=pltpu.CompilerParams(vmem_limit_bytes=24 * 2**20),
        cost_estimate=pl.CostEstimate(flops=10**9, bytes_accessed=4 * 2**20, transcendentals=0),
        name="combine",
    )(returned, places, gates, hidden, directions)


def expert_kernel(counts, *refs):
    number = len(counts)
    parts = refs[:number]
    gate, up, down, kept, passed = refs[number : number + 5]
    values, extra, folded, hidden, tail, main_sems, extra_sems = refs[number + 5 :]
    places = [sum(counts[:index]) for index in range(number)]
    count = sum(counts)
    lone = count // FOLD
    loads, extras = [], []
    for index, (part, place, size) in enumerate(zip(parts, places, counts)):
        span = pl.ds(place, size)
        extras.append(
            pltpu.make_async_copy(
                part.at[:, pl.ds(D, 128)], extra.at[span, :], extra_sems.at[index]
            )
        )
        loads.append(
            pltpu.make_async_copy(
                part.at[:, pl.ds(0, D)], values.at[span, :], main_sems.at[index]
            )
        )
    for load in extras + loads:
        load.start()
    for load in extras:
        load.wait()
    folded[...] = extra[...].astype(F32)
    values[count:, :] = unfold(lone, folded)
    for load in loads:
        load.wait()
    units = down.shape[0]
    whole = units // 256 * 256

    def open_units(start, size):
        span = pl.ds(start, size)
        first = jnp.dot(values[...], gate[:, span], preferred_element_type=F32)
        second = jnp.dot(values[...], up[:, span], preferred_element_type=F32)
        hidden[:, span] = (first / (1.0 + jnp.exp(-first)) * second).astype(BF16)

    @pl.loop(0, whole // 256)
    def _(index):
        open_units(pl.multiple_of(index * 256, 256), 256)

    if units > whole:
        open_units(whole, units - whole)
    half = kept.shape[0]

    @pl.loop(0, D // 1024)
    def _(index):
        span = pl.ds(pl.multiple_of(index * 1024, 1024), 1024)
        result = jnp.dot(hidden[...], down[:, span], preferred_element_type=F32)
        kept[:, span] = result[:half].astype(BF16)
        passed[:, span] = result[half:count].astype(BF16)
        tail[:, span] = result[count:]

    fold(tail[...], folded)
    kept[:, D:] = folded[:half, :].astype(BF16)
    passed[:, D:] = folded[half:, :].astype(BF16)


def expert_call(parts, gate, up, down):
    counts = tuple(part.shape[0] for part in parts)
    count = sum(counts)
    rows = count + count // FOLD
    units = down.shape[0]
    anywhere = pl.BlockSpec(memory_space=pl.ANY)
    near = pl.BlockSpec(memory_space=pltpu.VMEM)
    return pl.pallas_call(
        functools.partial(expert_kernel, counts),
        in_specs=[anywhere] * len(parts) + [near] * 3,
        out_specs=[near, near],
        out_shape=[jax.ShapeDtypeStruct((count // 2, D + 128), BF16)] * 2,
        scratch_shapes=[
            pltpu.VMEM((rows, D), BF16),
            pltpu.VMEM((count, 128), BF16),
            pltpu.VMEM((count, 128), F32),
            pltpu.VMEM((rows, units), BF16),
            pltpu.VMEM((count // FOLD, D), F32),
            pltpu.SemaphoreType.DMA((len(parts),)),
            pltpu.SemaphoreType.DMA((len(parts),)),
        ],
        compiler_params=pltpu.CompilerParams(vmem_limit_bytes=24 * 2**20),
        cost_estimate=pl.CostEstimate(
            flops=6 * rows * D * units,
            bytes_accessed=4 * rows * D + 6 * D * units,
            transcendentals=rows * units,
        ),
        name="expert",
    )(*parts, gate, up, down)


def settle_kernel(kept, got, top_after, top_before, bottom_before, bottom_after, out):
    half = top_after.shape[0]
    for index, others in enumerate(((top_after, top_before), (bottom_before, bottom_after))):
        span = pl.ds(index * half, half)
        total = kept[span, :].astype(F32) + got[span, :].astype(F32)
        for other in others:
            total = total + other[...].astype(F32)
        out[span, :] = total.astype(BF16)


def settle_call(*arrays):
    return pl.pallas_call(
        settle_kernel,
        out_shape=jax.ShapeDtypeStruct(arrays[0].shape, BF16),
        compiler_params=pltpu.CompilerParams(vmem_limit_bytes=16 * 2**20),
        cost_estimate=pl.CostEstimate(flops=2 * 10**6, bytes_accessed=5 * 2**20, transcendentals=0),
        name="settle",
    )(*arrays)


def from_before(values):
    size = lax.axis_size("exp")
    return lax.ppermute(values, "exp", [(i, (i + 2) % size) for i in range(size)])


def from_after(values):
    size = lax.axis_size("exp")
    return lax.ppermute(values, "exp", [(i, (i - 2) % size) for i in range(size)])


def from_sibling(values):
    size = lax.axis_size("exp")
    return lax.ppermute(values, "exp", [(i, i ^ 1) for i in range(size)])


def add_up(*terms):
    total = terms[0].astype(F32)
    for term in terms[1:]:
        total = total + term.astype(F32)
    return total.astype(BF16)


def after(values, *earlier):
    return lax.optimization_barrier((tuple(values), earlier))[0]


def expert_layer(own, gate, up, down):
    half = own.shape[0] // 2
    top, bottom = own[:half], own[half:]
    own_other = from_sibling(own)
    before_top = from_before(top)
    after_bottom = from_after(bottom)
    call = functools.partial(expert_call, gate=gate, up=up, down=down)
    kept_own, passed = call((own, own_other))
    before_top, after_bottom, kept_own, passed, top, bottom = after(
        (before_top, after_bottom, kept_own, passed, top, bottom)
    )
    got_own = from_sibling(passed)
    others = from_sibling(before_top), from_sibling(after_bottom)
    far_top = from_before(before_top)
    far_bottom = from_after(after_bottom)
    before_bottom = from_before(bottom)
    after_top = from_after(top)
    kept, passed = call((before_top, after_bottom, *others))
    far_top, far_bottom, got_own, kept, passed = after(
        (far_top, far_bottom, got_own, kept, passed)
    )
    got = from_sibling(passed)
    others = from_sibling(far_top), from_sibling(far_bottom)
    near_top, near_bottom = add_up(kept[:half], got[:half]), add_up(kept[half:], got[half:])
    near_top, near_bottom, far_top, far_bottom = after(
        (near_top, near_bottom, far_top, far_bottom)
    )
    top_after = from_after(near_top)
    bottom_before = from_before(near_bottom)
    kept, passed = call((far_top, far_bottom, *others))
    after_top, before_bottom, kept, passed = after((after_top, before_bottom, kept, passed))
    late = from_sibling(after_top), from_sibling(before_bottom)
    got = from_sibling(passed)
    far_top, far_bottom = add_up(kept[:half], got[:half]), add_up(kept[half:], got[half:])
    far_top, far_bottom, after_top, before_bottom = after(
        (far_top, far_bottom, after_top, before_bottom)
    )
    relay_top = from_before(far_top)
    relay_bottom = from_after(far_bottom)
    kept, passed = call((after_top, before_bottom, *late))
    relay_top, relay_bottom, top_after, bottom_before, kept, passed = after(
        (relay_top, relay_bottom, top_after, bottom_before, kept, passed)
    )
    got = from_sibling(passed)
    top_before = from_before(add_up(kept[:half], got[:half], relay_top))
    bottom_after = from_after(add_up(kept[half:], got[half:], relay_bottom))
    return settle_call(
        kept_own, got_own, top_after, top_before, bottom_before, bottom_after
    )


def on_device(
    ssd_input,
    ssd_gate,
    state_write,
    state_read,
    step_size,
    decay_log,
    skip_gain,
    norm_gain,
    w_out,
    resid,
    moe_gain,
    w_gate,
    w_up,
    w_down,
    routes,
    gates,
    directions,
):
    length_dev, seqs, width_dev = ssd_input.shape
    heads_dev = decay_log.shape[0]
    experts = lax.axis_size("seq")
    columns = lax.axis_size("exp")
    rows_keep = length_dev * seqs // columns

    def swap(values):
        return jnp.transpose(values, (1, 0, 2))

    decays, steps = swap(decay_log), swap(step_size)
    inputs, writes, reads = swap(ssd_input), swap(state_write), swap(state_read)
    parcel, first = contrib_call(decays, steps, inputs, writes)
    parcels = lax.all_to_all(parcel, "seq", split_axis=0, concat_axis=0, tiled=True)
    skip = jnp.repeat(skip_gain, HEAD_DIM)[None, :]
    within_early, factor_early = within_call(
        0, decays, steps, inputs, writes, reads, skip, first
    )
    (parcels,) = after((parcels,), within_early)
    entering = lax.all_to_all(
        scan_call(parcels), "seq", split_axis=0, concat_axis=0, tiled=True
    )
    within_late, factor_late = within_call(
        1, decays, steps, inputs, writes, reads, skip, first
    )
    gating = swap(ssd_gate)
    (entering,) = after((entering,), within_late, gating)
    place = lax.axis_index("exp").astype(jnp.int32)[None]
    kept, passed = mixer_call(
        0, place, factor_early, reads, entering, within_early, gating, norm_gain[None, :], w_out, columns
    )
    got = from_sibling(passed)
    (place,) = after((place,), kept)
    kept_late, passed = mixer_call(
        1, place, factor_late, reads, entering, within_late, gating, norm_gain[None, :], w_out, columns
    )
    got_late = from_sibling(passed)
    relay_top = from_before(add_up(kept[2], got[2]))
    top_after = from_after(add_up(kept[3], got[3]))
    relay_bottom = from_after(add_up(kept_late[2], got_late[2]))
    bottom_before = from_before(add_up(kept_late[1], got_late[1]))
    top_before = from_before(add_up(kept[1], got[1], relay_top))
    bottom_after = from_after(add_up(kept_late[3], got_late[3], relay_bottom))
    capacity = max(2, 2 * rows_keep * 17 // (16 * experts))
    assert capacity == FOLD + 1
    picks = swap(routes).reshape(-1)
    onehot = (picks[:, None] == jnp.arange(experts, dtype=jnp.int32)[None, :]).astype(jnp.int32)
    before = jnp.cumsum(onehot, axis=0) - onehot
    ranked = jnp.sum(before * onehot, axis=1)
    places = jnp.where(
        ranked < FOLD, picks * FOLD + ranked, experts * FOLD + picks
    ).reshape(rows_keep, 2)
    hidden_state, packed = dispatch_call(
        resid,
        moe_gain[None, :],
        places.T,
        (kept, got, kept_late, got_late),
        (top_after, top_before, bottom_before, bottom_after),
        experts,
    )
    arrived = lax.all_to_all(
        packed.reshape(experts, FOLD, D + 128), "seq", split_axis=0, concat_axis=0, tiled=True
    )
    summed = expert_layer(arrived.reshape(packed.shape), w_gate[0], w_up[0], w_down[0])
    returned = lax.all_to_all(
        summed.reshape(experts, FOLD, D + 128), "seq", split_axis=0, concat_axis=0, tiled=True
    )
    combined = combine_call(
        returned.reshape(packed.shape),
        places,
        swap(gates).reshape(rows_keep, 2),
        hidden_state,
        directions,
    )
    return combined


def solution(mesh):
    in_specs = (
        P("seq", None, "exp"),
        P("seq", None, "exp"),
        P("seq", None, "exp"),
        P("seq", None, "exp"),
        P("exp", None, "seq"),
        P("exp", None, "seq"),
        P("exp"),
        P("exp"),
        P("exp", None),
        P(("seq", "exp"), None, None),
        P(),
        P("seq", None, "exp"),
        P("seq", None, "exp"),
        P("seq", "exp", None),
        P(("seq", "exp"), None, None),
        P(("seq", "exp"), None, None),
        P(),
    )
    out_specs = P(("seq", "exp"), None, None)
    return jax.shard_map(
        on_device, mesh=mesh, in_specs=in_specs, out_specs=out_specs, check_vma=False
    )
```
